128 devices in a mesh: gx: 16 (over z, y), gy: 8 (over x, core).
Axes of the slice: x: 4, y: 4, z: 4, core: 2. Of those that a mesh axis runs over, the one named last changes fastest.
Arguments:
- tracers: float32 [8, 16, 4, 36, 64, 128], P('gy', 'gx'), may hold values from -6 to 6
- velocity: float32 [8, 16, 2, 36, 64, 128], P('gy', 'gx'), may hold values from -0.8 to 0.8
- mixing_rate: float32 [8, 16, 35, 64, 128], P('gy', 'gx'), may hold values from 0.05 to 5
- column_depth: float32 [8, 16, 64, 128], P('gy', 'gx'), may hold values from 0.25 to 2.5
- ocean_mask: int32 [8, 28], replicated, may hold values from 0 to 1, as said below
- clinic_list: int32 [8, 16], replicated, may hold values from 0 to 27, as said below
- tropic_list: int32 [8, 32], replicated, may hold values from -1 to 27, as said below
Outputs:
- new_tracers: float32 [8, 16, 4, 36, 64, 128], P('gy', 'gx')
- surface_height: float32 [8, 32, 64, 128], P('gy', 'gx')
The draws below stay inside these ranges and needn't reach their ends.
Inputs may be any that keep to these rules, and one draw needn't show every extreme that they name: `ocean_mask`: every block row holds exactly 16 ocean blocks. `clinic_list`: row r lists every ocean block column of block row r exactly once. `tropic_list`: row r lists every ocean block column of block row r exactly once and holds -1 elsewhere; the 2 entries of one device are either all -1 or all blocks.
All inputs are finite; a program needn't handle non-finite values.
Results may differ from the reference program's by a relative error of at most 0.0003.
Values sent between devices are 32-bit elements; how exact they have to be, the bound alone decides.
No kernel may reach another device: no remote copies, remote signals or barrier semaphores. Data moves between devices by JAX's collectives and lax.ppermute only.
A program may use at most 128 MiB of HBM per device.

```python
import math
import jax
import jax.numpy as jnp
from jax import lax

LEV = 36
NTR = 4
BN = 64
BE = 128
SLOTS = 1
ITERS = 3
SLOTS2 = 2
NOCEAN = 16
NBX = 28
N_GX = 16
N_GY = 8


def block_layout(key):
    base_key = jax.random.fold_in(key, 4242)
    row_keys = jax.random.split(base_key, N_GY)

    def one_row(row_key):
        first_key, second_key, third_key = jax.random.split(row_key, 3)
        order = jax.random.permutation(first_key, NBX).astype(jnp.int32)
        ocean = order[:NOCEAN]
        land_row = jnp.zeros((NBX,), jnp.int32).at[ocean].set(1)
        shuffled = jax.random.permutation(second_key, ocean).astype(jnp.int32)
        ranking = jax.random.permutation(third_key, N_GX).astype(jnp.int32)
        busy = jnp.zeros((N_GX,), jnp.int32).at[ranking].set(jnp.arange(N_GX, dtype=jnp.int32)) < N_GX // 2
        position = jnp.cumsum(busy.astype(jnp.int32)) - 1
        groups = shuffled.reshape(N_GX // 2, SLOTS2)
        chosen = groups[jnp.clip(position, 0, N_GX // 2 - 1)]
        tropic_row = jnp.where(busy[:, None], chosen, -1).reshape(N_GX * SLOTS2).astype(jnp.int32)
        return (land_row, ocean, tropic_row)
    return jax.vmap(one_row)(row_keys)


def draw_tracers(key, part):
    base_key = jax.random.fold_in(key, 7171)
    rough_key, offset_key = jax.random.split(base_key)
    full_shape = (N_GY, N_GX * SLOTS, NTR, LEV, BN, BE)
    rough = jax.random.normal(rough_key, full_shape, jnp.float32)
    offsets = jax.random.uniform(offset_key, (N_GY, N_GX * SLOTS, 2), jnp.float32, -2.0, 2.0)
    shifts = jnp.concatenate([offsets, jnp.zeros((N_GY, N_GX * SLOTS, NTR - 2), jnp.float32)], axis=2)
    return jnp.clip(rough + shifts[:, :, :, None, None, None], -6.0, 6.0)


def draw_ocean_mask(key, part):
    return block_layout(key)[0]


def draw_clinic_list(key, part):
    return block_layout(key)[1]


def draw_tropic_list(key, part):
    return block_layout(key)[2]


def block_levels(stream_key, extent, cuts, low, high):
    loudness, own = 1.0, jax.random.fold_in(stream_key, 6)
    for axis_at, shards_of in cuts:
        heights = jnp.exp(jax.random.uniform(jax.random.fold_in(own, axis_at), (shards_of,), jnp.float32, low / len(cuts), high / len(cuts)))
        loudness = loudness * jnp.repeat(heights, extent[axis_at] // shards_of).reshape([-1 if axis == axis_at else 1 for axis in range(len(extent))])
    return loudness


def bell_draw(stream_key, extent, scale, reach, cuts=(), kind=jnp.bfloat16):
    values = scale * jax.random.normal(stream_key, extent, jnp.float32)
    if cuts:
        values = values * block_levels(stream_key, extent, cuts, -0.22, 0.18)
    return jnp.clip(values, -reach, reach).astype(kind)


def setup_inputs(seed: int = 0) -> dict:
    keys = jax.random.split(jax.random.key(seed), 8)
    return {
        "tracers": draw_tracers(jax.random.fold_in(keys[7], 71), 0),
        "velocity": bell_draw(keys[1], (N_GY, N_GX * SLOTS, 2, LEV, BN, BE), 0.2, 0.8, ((0, 8), (1, 16)), jnp.float32),
        "mixing_rate": jnp.clip(jnp.exp(math.log(5.0) - 4.6051702 * jax.random.uniform(keys[2], (N_GY, N_GX * SLOTS, LEV - 1, BN, BE), jnp.float32) ** block_levels(keys[2], (N_GY, N_GX * SLOTS, LEV - 1, BN, BE), ((0, 8), (1, 16)), -0.2, 0.2)), 0.05, 5.0),
        "column_depth": jnp.clip(jnp.exp(math.log(2.5) - 2.3025851 * jax.random.uniform(keys[3], (N_GY, N_GX * SLOTS, BN, BE), jnp.float32) ** block_levels(keys[3], (N_GY, N_GX * SLOTS, BN, BE), ((0, 8), (1, 16)), -0.2, 0.2)), 0.25, 2.5),
        "ocean_mask": draw_ocean_mask(jax.random.fold_in(keys[7], 71), 0),
        "clinic_list": draw_clinic_list(jax.random.fold_in(keys[7], 71), 0),
        "tropic_list": draw_tropic_list(jax.random.fold_in(keys[7], 71), 0),
    }


diffusion = 0.12
area_term = 0.1
thermal = 0.2
haline = 0.25
cabbeling = 0.05
forcing = 4.0


def inverse_map(column_list, row_width):
    row_count, slot_count = column_list.shape
    target = jnp.where(column_list < 0, row_width, column_list).astype(jnp.int32)
    row_ids = jnp.broadcast_to(jnp.arange(row_count, dtype=jnp.int32)[:, None], (row_count, slot_count))
    slot_ids = jnp.broadcast_to(jnp.arange(slot_count, dtype=jnp.int32)[None, :], (row_count, slot_count))
    lookup = jnp.zeros((row_count, row_width + 1), jnp.int32).at[row_ids, target].set(slot_ids)
    return lookup[:, :row_width]


def links(columns, row_ids, ocean_mask, inverse):
    row_count, row_width = ocean_mask.shape
    in_use = (columns >= 0).astype(jnp.float32)
    column = jnp.maximum(columns, 0).astype(jnp.int32)
    east_col = (column + 1) % row_width
    west_col = (column + row_width - 1) % row_width
    north_row = jnp.minimum(row_ids + 1, row_count - 1)
    south_row = jnp.maximum(row_ids - 1, 0)
    has_north = (row_ids + 1 < row_count).astype(jnp.float32)
    has_south = (row_ids > 0).astype(jnp.float32)
    mask_float = ocean_mask.astype(jnp.float32)
    face_open = (in_use * mask_float[row_ids, east_col], in_use * mask_float[row_ids, west_col],
                 in_use * has_north * mask_float[north_row, column], in_use * has_south * mask_float[south_row, column])
    slot_ids = (inverse[row_ids, east_col], inverse[row_ids, west_col], inverse[north_row, column], inverse[south_row, column])
    return face_open, slot_ids


def divergence(values, speeds, low_side, high_side, low_speed, open_low, open_high, along_axis):
    length = values.shape[along_axis]
    extended = jnp.concatenate([jnp.expand_dims(low_side, along_axis), values, jnp.expand_dims(high_side, along_axis)], axis=along_axis)
    face_speed = jnp.concatenate([jnp.expand_dims(low_speed, along_axis), speeds], axis=along_axis)
    behind = lax.slice_in_dim(extended, 0, length + 1, axis=along_axis)
    forward = lax.slice_in_dim(extended, 1, length + 2, axis=along_axis)
    fluxes = face_speed * (0.5 * (behind + forward)) - diffusion * (forward - behind)
    fluxes = jnp.concatenate([lax.slice_in_dim(fluxes, 0, 1, axis=along_axis) * open_low,
                              lax.slice_in_dim(fluxes, 1, length, axis=along_axis),
                              lax.slice_in_dim(fluxes, length, length + 1, axis=along_axis) * open_high], axis=along_axis)
    return lax.slice_in_dim(fluxes, 1, length + 1, axis=along_axis) - lax.slice_in_dim(fluxes, 0, length, axis=along_axis)


def vertical_mix(stirred, mixing_rate):
    levels = stirred.shape[3]
    coupling = mixing_rate[:, :, None]
    nothing = jnp.zeros_like(coupling[:, :, :, 0])
    interfaces = [coupling[:, :, :, level_index] for level_index in range(levels - 1)]
    above = [nothing] + interfaces
    beneath = interfaces + [nothing]
    factors = []
    partial_sol = []
    for level_index in range(levels):
        diagonal = 1.0 + above[level_index] + beneath[level_index]
        source = stirred[:, :, :, level_index]
        if level_index > 0:
            diagonal = diagonal - above[level_index] * factors[level_index - 1]
            source = source + above[level_index] * partial_sol[level_index - 1]
        factors.append(beneath[level_index] / diagonal)
        partial_sol.append(source / diagonal)
    result_levels = [partial_sol[levels - 1]]
    for level_index in range(levels - 2, -1, -1):
        result_levels.insert(0, partial_sol[level_index] + factors[level_index] * result_levels[0])
    return jnp.stack(result_levels, axis=3)


def tracer_core(tracers, velocity, mixing_rate, halo_values, face_open):
    west_tracer, west_speed, east_tracer, south_tracer, south_speed, north_tracer = halo_values
    open_east, open_west, open_north, open_south = [opening[:, :, None, None, None, None] for opening in face_open]
    east_speed = velocity[:, :, 0:1]
    north_speed = velocity[:, :, 1:2]
    stirred = (tracers
               - divergence(tracers, east_speed, west_tracer, east_tracer, west_speed[:, :, None], open_west, open_east, 5)
               - divergence(tracers, north_speed, south_tracer, north_tracer, south_speed[:, :, None], open_south, open_north, 4))
    mixed = vertical_mix(stirred, mixing_rate)
    levels = mixed.shape[3]
    spacing = 2.0 * (jnp.arange(levels, dtype=jnp.float32) + 1.0) / (levels * (levels + 1))
    heat = mixed[:, :, 0]
    salinity = mixed[:, :, 1]
    density = haline * salinity - thermal * heat - cabbeling * heat * heat
    column_forcing = forcing * jnp.sum(density * spacing[None, None, :, None, None], axis=2)
    return mixed, column_forcing


def face_weights(column_depth, depth_halos, face_open):
    west_depth, east_depth, south_depth, north_depth = depth_halos
    open_east, open_west, open_north, open_south = [opening[:, :, None, None] for opening in face_open]
    cells_east = column_depth.shape[3]
    cells_north = column_depth.shape[2]
    edge_east = (jnp.arange(cells_east) == cells_east - 1)[None, None, None, :]
    edge_west = (jnp.arange(cells_east) == 0)[None, None, None, :]
    edge_north = (jnp.arange(cells_north) == cells_north - 1)[None, None, :, None]
    edge_south = (jnp.arange(cells_north) == 0)[None, None, :, None]
    to_east = jnp.concatenate([column_depth[..., 1:], east_depth[..., None]], axis=3)
    to_west = jnp.concatenate([west_depth[..., None], column_depth[..., :-1]], axis=3)
    to_north = jnp.concatenate([column_depth[:, :, 1:], north_depth[:, :, None]], axis=2)
    to_south = jnp.concatenate([south_depth[:, :, None], column_depth[:, :, :-1]], axis=2)
    weight_east = 0.5 * (column_depth + to_east) * jnp.where(edge_east, open_east, 1.0)
    weight_west = 0.5 * (column_depth + to_west) * jnp.where(edge_west, open_west, 1.0)
    weight_north = 0.5 * (column_depth + to_north) * jnp.where(edge_north, open_north, 1.0)
    weight_south = 0.5 * (column_depth + to_south) * jnp.where(edge_south, open_south, 1.0)
    return jnp.stack([weight_east, weight_west, weight_north, weight_south], axis=2)


def apply_operator(values, weights, halo_values):
    east_side, west_side, north_side, south_side = halo_values
    weight_east = weights[:, :, 0]
    weight_west = weights[:, :, 1]
    weight_north = weights[:, :, 2]
    weight_south = weights[:, :, 3]
    to_east = jnp.concatenate([values[..., 1:], east_side[..., None]], axis=3)
    to_west = jnp.concatenate([west_side[..., None], values[..., :-1]], axis=3)
    to_north = jnp.concatenate([values[:, :, 1:], north_side[:, :, None]], axis=2)
    to_south = jnp.concatenate([south_side[:, :, None], values[:, :, :-1]], axis=2)
    return ((area_term + weight_east + weight_west + weight_north + weight_south) * values
            - weight_east * to_east - weight_west * to_west - weight_north * to_north - weight_south * to_south)


def reference(tracers, velocity, mixing_rate, column_depth, ocean_mask, clinic_list, tropic_list):
    row_count, slot_count = clinic_list.shape
    row_width = ocean_mask.shape[1]
    row_ids = jnp.broadcast_to(jnp.arange(row_count, dtype=jnp.int32)[:, None], (row_count, slot_count))
    inverse = inverse_map(clinic_list, row_width)
    face_open, slot_ids = links(clinic_list, row_ids, ocean_mask, inverse)
    slot_east, slot_west, slot_north, slot_south = slot_ids
    north_ids = jnp.minimum(row_ids + 1, row_count - 1)
    south_ids = jnp.maximum(row_ids - 1, 0)
    halo_values = (tracers[..., -1][row_ids, slot_west], velocity[:, :, 0, :, :, -1][row_ids, slot_west],
                   tracers[..., 0][row_ids, slot_east], tracers[..., -1, :][south_ids, slot_south],
                   velocity[:, :, 1, :, -1, :][south_ids, slot_south], tracers[..., 0, :][north_ids, slot_north])

    def one_row(pieces):
        row_tracers, row_velocity, row_mixing, row_halos, row_open = pieces
        mixed, row_forcing = tracer_core(row_tracers[None], row_velocity[None], row_mixing[None],
                                         tuple(member[None] for member in row_halos),
                                         tuple(opening[None] for opening in row_open))
        return mixed[0], row_forcing[0]

    new_tracers, column_forcing = lax.map(one_row, (tracers, velocity, mixing_rate, halo_values, face_open))
    depth_halos = (column_depth[..., -1][row_ids, slot_west], column_depth[..., 0][row_ids, slot_east],
                   column_depth[..., -1, :][south_ids, slot_south], column_depth[..., 0, :][north_ids, slot_north])
    weights = face_weights(column_depth, depth_halos, face_open)

    def operate(values):
        neighbour_sides = (values[..., 0][row_ids, slot_east], values[..., -1][row_ids, slot_west],
                           values[..., 0, :][north_ids, slot_north], values[..., -1, :][south_ids, slot_south])
        return apply_operator(values, weights, neighbour_sides)

    solution = jnp.zeros_like(column_forcing)
    residual = column_forcing
    direction = column_forcing
    norm_now = jnp.sum(residual * residual)
    for iteration in range(ITERS):
        image_field = operate(direction)
        step_size = norm_now / jnp.sum(direction * image_field)
        solution = solution + step_size * direction
        residual = residual - step_size * image_field
        norm_next = jnp.sum(residual * residual)
        direction = residual + (norm_next / norm_now) * direction
        norm_now = norm_next
    tropic_count = tropic_list.shape[1]
    tropic_rows = jnp.broadcast_to(jnp.arange(row_count, dtype=jnp.int32)[:, None], (row_count, tropic_count))
    in_use = tropic_list >= 0
    source_slot = inverse[tropic_rows, jnp.maximum(tropic_list, 0).astype(jnp.int32)]
    surface_height = jnp.where(in_use[:, :, None, None], solution[tropic_rows, source_slot], 0.0)
    return new_tracers, surface_height
```

```python
import functools
import jax
import jax.numpy as jnp
from jax import lax
from jax.experimental import pallas as pl
from jax.experimental.pallas import tpu as pltpu
from jax.sharding import PartitionSpec as P

F32 = jnp.float32
LEV, BN, BE = 36, 64, 128
NBX = 28
PIECE = 40

DEPTH_ROW = 36

diffusion = 0.12
area_term = 0.1
thermal = 0.2
haline = 0.25
cabbeling = 0.05
forcing = 4.0

NBR = 0
FROM = 8
SEND = 12
TFROM = 28
TSEND = 30
PLAN = 40

DIRS = ((0, 1), (0, -1), (1, 0), (-1, 0), (1, 1), (1, -1), (-1, 1), (-1, -1))


def north_rows(group):
    return 3 * PIECE if group == 0 else 2 * PIECE


def item_rows(group):
    return north_rows(group) + 2 * PIECE + 2 * BN


def params(**more):
    return pltpu.CompilerParams(vmem_limit_bytes=48 * 1024 * 1024, **more)


VM = pl.BlockSpec(memory_space=pltpu.VMEM)
SM = pl.BlockSpec(memory_space=pltpu.SMEM)
ANY = pl.BlockSpec(memory_space=pl.ANY)


def plan_kernel(side, n_gy, slots, clinic, tropic, out):
    gx = lax.axis_index("gx")
    gy = lax.axis_index("gy")
    z = gx // side
    y = lax.rem(gx, side)

    def find(row, column, ok):
        row = jnp.clip(row, 0, n_gy - 1)
        slot = jnp.int32(-1)
        for s in range(slots):
            slot = jnp.where(clinic[row, s] == column, jnp.int32(s), slot)
        return jnp.where(ok, slot, jnp.int32(-1))

    def neighbour(column, dr, dc):
        row = gy + dr
        ok = jnp.logical_and(row >= 0, row < n_gy)
        target = column + dc
        target = jnp.where(target < 0, target + NBX, target)
        target = jnp.where(target >= NBX, target - NBX, target)
        return find(row, target, ok)

    column = clinic[gy, gx]
    for d, (dr, dc) in enumerate(DIRS):
        slot = neighbour(column, dr, dc)
        out[NBR + d] = jnp.where(slot < 0, jnp.int32(-1), slot * n_gy + gy + dr)
        if d < 4:
            shift = lax.rem(z - slot // side + side, side)
            out[FROM + d] = jnp.where(slot < 0, jnp.int32(-1), shift)
    for k in range(side):
        there = lax.rem(z + k, side) * side + y
        column = clinic[gy, there]
        for d, (dr, dc) in enumerate(DIRS[:4]):
            slot = neighbour(column, dr, dc)
            shift = lax.rem(y - lax.rem(slot, side) + side, side)
            out[SEND + 4 * k + d] = jnp.where(slot < 0, jnp.int32(0), shift)
        for b in range(2):
            column_b = tropic[gy, 2 * there + b]
            slot = find(gy, column_b, column_b >= 0)
            shift = lax.rem(y - lax.rem(slot, side) + side, side)
            out[TSEND + 2 * k + b] = jnp.where(slot < 0, jnp.int32(0), shift)
    for b in range(2):
        column_b = tropic[gy, 2 * gx + b]
        slot = find(gy, column_b, column_b >= 0)
        shift = lax.rem(z - slot // side + side, side)
        out[TFROM + b] = jnp.where(slot < 0, jnp.int32(-1), shift)
    for i in range(TSEND + 8, PLAN):
        out[i] = jnp.int32(0)


def pack_kernel(group, tracers, velocity, depth, north, south, east, west, q, vel, sems):
    first = 2 * group * LEV
    copies = [
        pltpu.make_async_copy(tracers.at[pl.ds(first + f * LEV, LEV)], q.at[f], sems.at[f])
        for f in range(2)
    ]
    if group == 0:
        copies += [
            pltpu.make_async_copy(velocity.at[pl.ds(f * LEV, LEV)], vel.at[f], sems.at[2 + f])
            for f in range(2)
        ]
    for copy in copies:
        copy.start()
    lane = lax.broadcasted_iota(jnp.int32, (BN, BE), 1)
    east[...] = jnp.zeros((BN, BE), F32)
    west[...] = jnp.zeros((BN, BE), F32)
    fields = 3 if group == 0 else 2
    for f in range(fields):
        north[pl.ds(f * PIECE + 32, 8), :] = jnp.zeros((8, BE), F32)
        if f < 2:
            south[pl.ds(f * PIECE + 32, 8), :] = jnp.zeros((8, BE), F32)
    for f in range(fields):
        copies[f].wait()
        source = q.at[f] if f < 2 else vel.at[0]

        def level(k, carry, f=f, source=source):
            tile = source[k]
            spot = f * LEV + k
            carry_e = jnp.where(lane == spot, pltpu.roll(tile, spot + 1, 1), carry[0])
            if f < 2:
                carry_w = jnp.where(lane == spot, pltpu.roll(tile, spot, 1), carry[1])
                return carry_e, carry_w
            return carry_e, carry[1]

        e, w = lax.fori_loop(0, LEV, level, (east[...], west[...]), unroll=2)
        east[...] = e
        west[...] = w
        if f == 2:
            copies[3].wait()
        rows = q.at[f] if f < 2 else vel.at[1]
        for k in range(LEV):
            north[pl.ds(f * PIECE + k, 1), :] = rows[k, pl.ds(BN - 1, 1), :]
            if f < 2:
                south[pl.ds(f * PIECE + k, 1), :] = rows[k, pl.ds(0, 1), :]
    if group == 0:
        north[pl.ds(DEPTH_ROW, 3), :] = depth[pl.ds(BN - 3, 3), :]
        south[pl.ds(DEPTH_ROW, 3), :] = depth[pl.ds(0, 3), :]


def pack(group, tracers, velocity, depth):
    shape = lambda *s: jax.ShapeDtypeStruct(s, F32)
    return pl.pallas_call(
        functools.partial(pack_kernel, group),
        out_shape=(
            shape(north_rows(group), BE),
            shape(2 * PIECE, BE),
            shape(BN, BE),
            shape(BN, BE),
        ),
        in_specs=[ANY, ANY, VM],
        out_specs=(VM, VM, VM, VM),
        scratch_shapes=[
            pltpu.VMEM((2, LEV, BN, BE), F32),
            pltpu.VMEM((2, LEV if group == 0 else 1, BN, BE), F32),
            pltpu.SemaphoreType.DMA((4,)),
        ],
        compiler_params=params(),
        name=f"pack{group}",
    )(tracers, velocity, depth)


def chosen(shift, arrays, start, rows):
    value = arrays[-1][pl.ds(start, rows), :]
    for k in range(len(arrays) - 1):
        value = jnp.where(shift == k, arrays[k][pl.ds(start, rows), :], value)
    return value


def select_kernel(group, plan, x0, x1, x2, x3, o0, o1, o2, o3):
    n = north_rows(group)
    spans = {3: (0, n), 2: (n, 2 * PIECE), 1: (n + 2 * PIECE, BN), 0: (n + 2 * PIECE + BN, BN)}
    for k, out in enumerate((o0, o1, o2, o3)):
        for d, (start, rows) in spans.items():
            out[pl.ds(start, rows), :] = chosen(
                plan[SEND + 4 * k + d], (x0, x1, x2, x3), start, rows
            )


def select(group, plan, arrays):
    rows = item_rows(group)
    return pl.pallas_call(
        functools.partial(select_kernel, group),
        out_shape=(jax.ShapeDtypeStruct((rows, BE), F32),) * 4,
        in_specs=[SM] + [VM] * 4,
        out_specs=(VM,) * 4,
        compiler_params=params(),
        name=f"select{group}",
    )(plan, *arrays)


def main_kernel(group, chunk, *refs):
    if group == 0:
        (plan, tracers, velocity, mixing, north, south, east, west, h0, h1, h2, h3, depth,
         new, force, items, q, vel, mix, fac, fe_s, fw_s, fn_s, fs_s, sems, out_sems) = refs
        vel_north, vel_east, vel_halo = north, east, (h0, h1, h2, h3)
    else:
        (plan, tracers, velocity, mixing, north, south, east, west, h0, h1, h2, h3,
         vel_north, vel_east, g0, g1, g2, g3, _aliased,
         new, q, vel, mix, fac, fe_s, fw_s, fn_s, fs_s, sems, out_sems) = refs
        vel_halo = (g0, g1, g2, g3)
    first = 2 * group * LEV
    parts = LEV // chunk
    copies = []
    for c in range(parts):
        levels = pl.ds(c * chunk, chunk)
        row = []
        for f in range(2):
            row.append(pltpu.make_async_copy(
                tracers.at[pl.ds(first + f * LEV + c * chunk, chunk)], q.at[f, levels], sems.at[c, f]))
            row.append(pltpu.make_async_copy(
                velocity.at[pl.ds(f * LEV + c * chunk, chunk)], vel.at[f, levels], sems.at[c, 2 + f]))
        size = chunk if c + 1 < parts else chunk - 1
        row.append(pltpu.make_async_copy(
            mixing.at[pl.ds(c * chunk, size)], mix.at[pl.ds(c * chunk, size)], sems.at[c, 4]))
        copies.append(row)
        for copy in row:
            copy.start()
    mix[LEV - 1] = jnp.zeros((BN, BE), F32)

    halo = (h0, h1, h2, h3)
    lane = lax.broadcasted_iota(jnp.int32, (BN, BE), 1)
    row_id = lax.broadcasted_iota(jnp.int32, (BN, BE), 0)
    n0, n = north_rows(0), north_rows(group)
    from_e, from_w, from_n, from_s = (plan[FROM + d] for d in range(4))

    def flux(speed, low, high):
        return speed * (0.5 * (low + high)) - diffusion * (high - low)

    def aligned(column_item):
        return jnp.where(lane < LEV, pltpu.roll(column_item, BE - 2 * LEV, 1),
                         pltpu.roll(column_item, BE - LEV, 1))

    col = n + 2 * PIECE
    col0 = n0 + 2 * PIECE
    from_east = chosen(from_e, halo, col + BN, BN)
    from_west = chosen(from_w, halo, col, BN)
    u_west = chosen(from_w, vel_halo, col0, BN)
    fe_s[...] = jnp.where(from_e >= 0, flux(aligned(vel_east[...]), east[...], from_east), 0.0)
    fw_s[...] = jnp.where(from_w >= 0, flux(aligned(u_west), from_west, west[...]), 0.0)
    v_own = vel_north[pl.ds(2 * PIECE, PIECE), :]
    v_south = chosen(from_s, vel_halo, 2 * PIECE, PIECE)
    for f in range(2):
        span = pl.ds(f * PIECE, PIECE)
        there = chosen(from_n, halo, n + f * PIECE, PIECE)
        fn_s[span, :] = jnp.where(from_n >= 0, flux(v_own, north[span, :], there), 0.0)
        there = chosen(from_s, halo, f * PIECE, PIECE)
        fs_s[span, :] = jnp.where(from_s >= 0, flux(v_south, there, south[span, :]), 0.0)

    def forward(k, carry):
        m_up, fac_up, sol_up = carry
        m = mix[k]
        half_u = 0.5 * vel[0, k]
        half_v = 0.5 * vel[1, k]
        ua, ub = half_u + diffusion, half_u - diffusion
        va, vb = half_v + diffusion, half_v - diffusion
        inverse = 1.0 / (1.0 + m_up + m - m_up * fac_up)
        fac_k = m * inverse
        fac[k] = fac_k
        sols = []
        for f in range(2):
            tile = q[f, k]
            spot = f * LEV + k
            fe = ua * tile + ub * pltpu.roll(tile, BE - 1, 1)
            fe = jnp.where(lane == BE - 1, pltpu.roll(fe_s[...], BE - 1 - spot, 1), fe)
            fw = jnp.where(lane == 0, pltpu.roll(fw_s[...], BE - spot, 1), pltpu.roll(fe, 1, 1))
            fn = va * tile + vb * pltpu.roll(tile, BN - 1, 0)
            fn = jnp.where(row_id == BN - 1, fn_s[pl.ds(f * PIECE + k, 1), :], fn)
            fs = jnp.where(row_id == 0, fs_s[pl.ds(f * PIECE + k, 1), :], pltpu.roll(fn, 1, 0))
            stirred = tile - (fe - fw) - (fn - fs)
            sol = (stirred + m_up * sol_up[f]) * inverse
            q[f, k] = sol
            sols.append(sol)
        return m, fac_k, tuple(sols)

    zero = jnp.zeros((BN, BE), F32)
    carry = (zero, zero, (zero, zero))
    for c in range(parts):
        for copy in copies[c]:
            copy.wait()
        carry = lax.fori_loop(c * chunk, (c + 1) * chunk, forward, carry)

    def backward(i, carry, top):
        k = top - i
        factor = fac[k]
        heat = q[0, k] + factor * carry[0]
        salt = q[1, k] + factor * carry[1]
        q[0, k] = heat
        q[1, k] = salt
        if group == 0:
            weight = (forcing * 2.0 / (LEV * (LEV + 1))) * (k + 1).astype(F32)
            density = haline * salt - thermal * heat - cabbeling * heat * heat
            return heat, salt, carry[2] + density * weight
        return heat, salt

    carry = (zero, zero, zero) if group == 0 else (zero, zero)
    outs = []
    for c in range(parts - 1, -1, -1):
        carry = lax.fori_loop(
            0, chunk, functools.partial(backward, top=(c + 1) * chunk - 1), carry)
        for f in range(2):
            copy = pltpu.make_async_copy(
                q.at[f, pl.ds(c * chunk, chunk)],
                new.at[pl.ds(first + f * LEV + c * chunk, chunk)], out_sems.at[c, f])
            copy.start()
            outs.append(copy)
    if group == 0:
        field = carry[2]
        force[...] = field
        turned = jnp.concatenate([field, depth[...]], axis=0).T
        east_item, west_item = turned[BE - 3:, :], turned[:3, :]
        sends = (east_item, west_item, field[BN - 3:, :], field[:3, :],
                 east_item, west_item, east_item, west_item)
        for d, item in enumerate(sends):
            to = plan[NBR + d]

            @pl.when(to >= 0)
            def _(to=to, item=item):
                items[to, pl.ds(0, 3), :] = item
    for copy in outs:
        copy.wait()


def main(group, args, chunk=6):
    shape = lambda *s: jax.ShapeDtypeStruct(s, F32)
    outs = [shape(4 * LEV, BN, BE)]
    out_specs = [ANY]
    in_specs = [SM, ANY, ANY, ANY] + [VM] * (len(args) - 4)
    aliases = {}
    if group == 0:
        outs += [shape(BN, BE), shape(128, 4, BE)]
        out_specs += [VM, VM]
    else:
        in_specs[-1] = ANY
        aliases = {len(args) - 1: 0}
    parts = LEV // chunk
    return pl.pallas_call(
        functools.partial(main_kernel, group, chunk),
        out_shape=tuple(outs),
        in_specs=in_specs,
        out_specs=tuple(out_specs),
        input_output_aliases=aliases,
        scratch_shapes=[
            pltpu.VMEM((2, LEV, BN, BE), F32),
            pltpu.VMEM((2, LEV, BN, BE), F32),
            pltpu.VMEM((LEV, BN, BE), F32),
            pltpu.VMEM((LEV, BN, BE), F32),
            pltpu.VMEM((BN, BE), F32),
            pltpu.VMEM((BN, BE), F32),
            pltpu.VMEM((2 * PIECE, BE), F32),
            pltpu.VMEM((2 * PIECE, BE), F32),
            pltpu.SemaphoreType.DMA((parts, 5)),
            pltpu.SemaphoreType.DMA((parts, 2)),
        ],
        compiler_params=params(),
        name=f"mix{group}",
    )(*args)


TALL, WIDE = BN + 8, 2 * BE


def krylov_kernel(plan, field, depth, h0, h1, h2, h3, got, vectors, sums, b_s, d_s):
    halo = (h0, h1, h2, h3)
    n = north_rows(0)
    lane = lax.broadcasted_iota(jnp.int32, (BE, BE), 1)
    nothing = jnp.zeros((3, BE), F32)

    def item(d):
        to = plan[NBR + d]
        return jnp.where(to >= 0, got[jnp.maximum(to, 0), pl.ds(0, 3), :], nothing)

    b_s[...] = jnp.zeros((TALL, WIDE), F32)
    d_s[...] = jnp.zeros((TALL, WIDE), F32)
    b_s[pl.ds(0, BN), pl.ds(0, BE)] = field[...]
    d_s[pl.ds(0, BN), pl.ds(0, BE)] = depth[...]
    b_s[pl.ds(BN, 3), pl.ds(0, BE)] = item(2)
    b_s[pl.ds(TALL - 3, 3), pl.ds(0, BE)] = item(3)
    from_n, from_s = plan[FROM + 2], plan[FROM + 3]
    d_s[pl.ds(BN, 3), pl.ds(0, BE)] = jnp.where(
        from_n >= 0, chosen(from_n, halo, n + DEPTH_ROW, 3), 0.0)
    d_s[pl.ds(TALL - 3, 3), pl.ds(0, BE)] = jnp.where(
        from_s >= 0, chosen(from_s, halo, DEPTH_ROW, 3), 0.0)
    middle = jnp.zeros((BE - 6, BE), F32)
    sides = jnp.concatenate([item(0), middle, item(1)], axis=0).T
    b_s[pl.ds(0, BN), pl.ds(BE, BE)] = sides[:BN]
    d_s[pl.ds(0, BN), pl.ds(BE, BE)] = sides[BN:]
    place = lax.broadcasted_iota(jnp.int32, (3, BE), 1)
    place = jnp.where(place >= BN, place - BN, place)

    def corner(north, south):
        return jnp.where(place < 3, north, jnp.where(
            jnp.logical_and(place >= 5, place < 8), pltpu.roll(south, BE - BN + 8, 1), 0.0))

    corners = jnp.concatenate([corner(item(4), item(6)), middle, corner(item(5), item(7))], axis=0).T
    b_s[pl.ds(BN, 8), pl.ds(BE, BE)] = corners[:8]
    d_s[pl.ds(BN, 8), pl.ds(BE, BE)] = corners[BN:BN + 8]

    d = d_s[...]
    east = lambda a: pltpu.roll(a, WIDE - 1, 1)
    west = lambda a: pltpu.roll(a, 1, 1)
    north = lambda a: pltpu.roll(a, TALL - 1, 0)
    south = lambda a: pltpu.roll(a, 1, 0)
    d_e, d_n = east(d), north(d)
    w_e = jnp.where(jnp.logical_and(d > 0, d_e > 0), 0.5 * (d + d_e), 0.0)
    w_n = jnp.where(jnp.logical_and(d > 0, d_n > 0), 0.5 * (d + d_n), 0.0)
    w_w, w_s = west(w_e), south(w_n)
    diagonal = area_term + w_e + w_w + w_n + w_s

    def operate(h):
        return diagonal * h - w_e * east(h) - w_w * west(h) - w_n * north(h) - w_s * south(h)

    v0 = b_s[...]
    v1 = operate(v0)
    v2 = operate(v1)
    v3 = operate(v2)
    v = [a[:BN, :BE] for a in (v0, v1, v2, v3)]
    for i in range(3):
        vectors[pl.ds(i * BN, BN), :] = v[i]
    pairs = ((0, 0), (0, 1), (1, 1), (1, 2), (2, 2), (2, 3))
    at = lax.broadcasted_iota(jnp.int32, (1, BE), 1)
    total = jnp.zeros((1, BE), F32)
    for i, (a, b) in enumerate(pairs):
        value = jnp.sum(jnp.sum(v[a] * v[b], axis=0, keepdims=True), axis=1, keepdims=True)
        total = jnp.where(at == i, value, total)
    for i in range(128):
        sums[i] = total


def krylov(plan, field, depth, halo, got):
    return pl.pallas_call(
        krylov_kernel,
        out_shape=(
            jax.ShapeDtypeStruct((3 * BN, BE), F32),
            jax.ShapeDtypeStruct((128, 1, BE), F32),
        ),
        in_specs=[SM] + [VM] * 7,
        out_specs=(VM, VM),
        scratch_shapes=[pltpu.VMEM((TALL, WIDE), F32)] * 2,
        compiler_params=params(),
        name="krylov",
    )(plan, field, depth, *halo, got)


def combine_kernel(plan, sums, a0, a1, a2, a3, o0, o1, o2, o3):
    total = jnp.sum(sums[...], axis=0, keepdims=True)
    moment = [total[:, i:i + 1] for i in range(6)]

    def inner(a, b, lift):
        value = None
        for i in range(len(a)):
            for j in range(len(b)):
                term = a[i] * b[j] * moment[i + j + lift]
                value = term if value is None else value + term
        return value

    one = jnp.ones((1, 1), F32)
    zero = jnp.zeros((1, 1), F32)
    residual, direction = [one], [one]
    solution = [zero, zero, zero]
    rr = moment[0]
    for step in range(3):
        alpha = rr / inner(direction, direction, 1)
        for i, c in enumerate(direction):
            solution[i] = solution[i] + alpha * c
        if step < 2:
            image = [zero] + direction
            padded = residual + [zero]
            residual = [r - alpha * c for r, c in zip(padded, image)]
            following = inner(residual, residual, 0)
            beta = following / rr
            direction = [r + beta * c for r, c in zip(residual, direction + [zero])]
            rr = following
    solved = []
    for a in (a0, a1, a2, a3):
        v = [a[pl.ds(i * BN, BN), :] for i in range(3)]
        solved.append(solution[0] * v[0] + solution[1] * v[1] + solution[2] * v[2])
    for k, out in enumerate((o0, o1, o2, o3)):
        for b in range(2):
            shift = plan[TSEND + 2 * k + b]
            value = solved[3]
            for j in range(3):
                value = jnp.where(shift == j, solved[j], value)
            out[pl.ds(b * BN, BN), :] = value


def combine(plan, sums, arrays):
    return pl.pallas_call(
        combine_kernel,
        out_shape=(jax.ShapeDtypeStruct((2 * BN, BE), F32),) * 4,
        in_specs=[SM] + [VM] * 5,
        out_specs=(VM,) * 4,
        compiler_params=params(),
        name="combine",
    )(plan, sums, *arrays)


def place_kernel(plan, a0, a1, a2, a3, out):
    for b in range(2):
        shift = plan[TFROM + b]
        value = chosen(shift, (a0, a1, a2, a3), b * BN, BN)
        out[b] = jnp.where(shift >= 0, value, 0.0)


def place(plan, arrays):
    return pl.pallas_call(
        place_kernel,
        out_shape=jax.ShapeDtypeStruct((2, BN, BE), F32),
        in_specs=[SM] + [VM] * 4,
        out_specs=VM,
        compiler_params=params(),
        name="place",
    )(plan, *arrays)


def body(tracers, velocity, mixing_rate, column_depth, ocean_mask, clinic_list, tropic_list):
    n_gx, n_gy = lax.axis_size("gx"), lax.axis_size("gy")
    side = 4
    tracers = tracers.reshape(4 * LEV, BN, BE)
    velocity = velocity.reshape(2 * LEV, BN, BE)
    mixing = mixing_rate.reshape(LEV - 1, BN, BE)
    depth = column_depth.reshape(BN, BE)

    def along_y(value, k):
        return lax.ppermute(value, "gx", [
            (z * side + y, z * side + (y + k) % side) for z in range(side) for y in range(side)])

    def along_z(value, k):
        return lax.ppermute(value, "gx", [
            (z * side + y, (z + k) % side * side + y) for z in range(side) for y in range(side)])

    plan = pl.pallas_call(
        functools.partial(plan_kernel, side, n_gy, n_gx),
        out_shape=jax.ShapeDtypeStruct((PLAN,), jnp.int32),
        in_specs=[SM, SM],
        out_specs=SM,
        name="plan",
    )(clinic_list, tropic_list)

    def route(group):
        north, south, east, west = pack(group, tracers, velocity, depth)
        below = lax.ppermute(north, "gy", [(i, i + 1) for i in range(n_gy - 1)])
        above = lax.ppermute(south, "gy", [(i, i - 1) for i in range(1, n_gy)])
        own = jnp.concatenate([below, above, east, west], axis=0)
        line = [own] + [along_y(own, k) for k in range(1, side)]
        sends = select(group, plan, line)
        halo = [sends[0]] + [along_z(sends[k], k) for k in range(1, side)]
        return (north, south, east, west), halo

    edges0, halo0 = route(0)
    new, field, items = main(0, (plan, tracers, velocity, mixing, *edges0, *halo0, depth))
    edges1, halo1 = route(1)
    (new,) = main(1, (plan, tracers, velocity, mixing, *edges1, *halo1,
                      edges0[0], edges0[2], *halo0, new))
    got = lax.all_to_all(items, ("gx", "gy"), 0, 0)
    vectors, sums = krylov(plan, field, depth, halo0, got)
    line = [vectors] + [along_y(vectors, k) for k in range(1, side)]
    totals = lax.all_to_all(sums, ("gx", "gy"), 0, 0)
    sends = combine(plan, totals.reshape(128, BE), line)
    arrived = [sends[0]] + [along_z(sends[k], k) for k in range(1, side)]
    height = place(plan, arrived)
    return new.reshape(1, 1, 4, LEV, BN, BE), height[None]


def solution(mesh):
    return jax.shard_map(
        body,
        mesh=mesh,
        in_specs=(
            P("gy", "gx", None, None, None, None),
            P("gy", "gx", None, None, None, None),
            P("gy", "gx", None, None, None),
            P("gy", "gx", None, None),
            P(),
            P(),
            P(),
        ),
        out_specs=(P("gy", "gx", None, None, None, None), P("gy", "gx", None, None)),
        check_vma=False,
    )
```

```python
import functools
import jax
import jax.numpy as jnp
from jax import lax
from jax.experimental import pallas as pl
from jax.experimental.pallas import tpu as pltpu
from jax.sharding import PartitionSpec as P

F32 = jnp.float32
LEV, BN, BE = 36, 64, 128
NBX = 28
CELLS = LEV * BN
HALF = BE // 2

NORTH = 0
NORTH_Q = (0, LEV, 3 * LEV, 4 * LEV)
NORTH_V = 2 * LEV
NORTH_D = 5 * LEV
SOUTH = 184
SOUTH_Q = tuple(SOUTH + f * LEV for f in range(4))
SOUTH_D = SOUTH + 4 * LEV
EAST = 332
WEST = 440
ITEM = 512
PART = 4

diffusion = 0.12
area_term = 0.1
thermal = 0.2
haline = 0.25
cabbeling = 0.05
forcing = 4.0

NBR = 0
TFROM = 8
TSEND = 10
RELAY = 18
PLAN = RELAY + 128
WRAP = NBX + 4

DIRS = ((0, 1), (0, -1), (1, 0), (-1, 0), (1, 1), (1, -1), (-1, 1), (-1, -1))


def params(mib, **more):
    return pltpu.CompilerParams(vmem_limit_bytes=mib * 1024 * 1024, **more)


VM = pl.BlockSpec(memory_space=pltpu.VMEM)
SM = pl.BlockSpec(memory_space=pltpu.SMEM)
ANY = pl.BlockSpec(memory_space=pl.ANY)
HBM = pl.BlockSpec(memory_space=pltpu.HBM)


def shaped(*shape):
    return jax.ShapeDtypeStruct(shape, F32)


def plan_kernel(side, n_gy, slots, clinic, tropic, out, pos):
    gx = lax.axis_index("gx")
    gy = lax.axis_index("gy")
    z = gx // side
    y = lax.rem(gx, side)

    def clear(i, carry):
        pos[i] = jnp.int32(-1)
        return carry

    lax.fori_loop(0, (n_gy + 2) * WRAP, clear, 0, unroll=16)
    for row in range(n_gy):
        for slot in range(slots):
            pos[(row + 1) * WRAP + 1 + clinic[row, slot]] = jnp.int32(slot * n_gy + row)
    for row in range(1, n_gy + 1):
        pos[row * WRAP] = pos[row * WRAP + NBX]
        pos[row * WRAP + NBX + 1] = pos[row * WRAP + 1]
    centre = (gy + 1) * WRAP + 1 + clinic[gy, gx]
    for d, (dr, dc) in enumerate(DIRS):
        out[NBR + d] = pos[centre + (dr * WRAP + dc)]
    me = gx * n_gy + gy
    kind_s, kind_n, kind_w = me < SOUTH // PART, me < EAST // PART, me < WEST // PART
    move = jnp.where(kind_s, jnp.int32(-WRAP), jnp.where(kind_n, jnp.int32(WRAP), jnp.where(
        kind_w, jnp.int32(-1), jnp.int32(1))))
    for row in range(n_gy):
        for there in range(slots):
            source = pos[(row + 1) * WRAP + 1 + clinic[row, there] + move]
            out[RELAY + there * n_gy + row] = jnp.maximum(source, 0)

    def owner(there, b):
        column_b = tropic[gy, 2 * there + b]
        device = pos[(gy + 1) * WRAP + 1 + jnp.maximum(column_b, 0)]
        return jnp.where(column_b < 0, jnp.int32(-1), device // n_gy)

    for k in range(side):
        there = lax.rem(z + k, side) * side + y
        for b in range(2):
            slot = owner(there, b)
            shift = lax.rem(y - lax.rem(slot, side) + side, side)
            out[TSEND + 2 * k + b] = jnp.where(slot < 0, jnp.int32(0), shift)
    for b in range(2):
        slot = owner(gx, b)
        shift = lax.rem(z - slot // side + side, side)
        out[TFROM + b] = jnp.where(slot < 0, jnp.int32(-1), shift)


def pack_kernel(tracers, velocity, depth_in, item, q, vel, turn, own, depth, sems):
    order = (0, 2, 4, 1, 3, 5)
    copies = {}
    fetch_depth = pltpu.make_async_copy(depth_in, depth, sems.at[6])
    fetch_depth.start()
    for f in order:
        source, at = (tracers, f) if f < 4 else (velocity, f - 4)
        target = q if f < 4 else vel
        span = pl.ds(at * CELLS, CELLS)
        copies[f] = pltpu.make_async_copy(source.at[span], target.at[span], sems.at[f])
        copies[f].start()
    fetch_depth.wait()
    lane = lax.broadcasted_iota(jnp.int32, (BN, BE), 1)
    level = lane // 2
    own[pl.ds(NORTH_D, 3), :] = depth[pl.ds(BN - 3, 3), :]
    own[pl.ds(NORTH_D + 3, 1), :] = jnp.zeros((1, BE), F32)
    own[pl.ds(SOUTH_D, 3), :] = depth[pl.ds(0, 3), :]
    own[pl.ds(SOUTH_D + 3, 1), :] = jnp.zeros((1, BE), F32)

    def columns(f):
        copies[f].wait()
        sides = jnp.zeros((BN, BE), F32)
        for k in range(LEV):
            tile = q[pl.ds(f * CELLS + k * BN, BN), :]
            sides = jnp.where(level == k, pltpu.roll(tile, 2 * k + 1, 1), sides)
        own[pl.ds(NORTH_Q[f], LEV), :] = q[pl.ds(f * CELLS + BN - 1, LEV, stride=BN), :]
        own[pl.ds(SOUTH_Q[f], LEV), :] = q[pl.ds(f * CELLS, LEV, stride=BN), :]
        return sides

    for j in range(2):
        first, second = columns(j), columns(2 + j)
        if j == 0:
            copies[4].wait()
            for k in range(LEV):
                tile = vel[pl.ds(k * BN, BN), :]
                first = jnp.where(lane == 2 * LEV + k, pltpu.roll(tile, 2 * LEV + 1 + k, 1), first)
        turn[...] = jnp.concatenate([first, second], axis=0).T
        own[pl.ds(EAST + j * LEV, LEV), :] = turn[pl.ds(0, LEV, stride=2), :]
        own[pl.ds(WEST + j * LEV, LEV), :] = turn[pl.ds(1, LEV, stride=2), :]
        if j == 0:
            own[pl.ds(EAST + 2 * LEV, LEV), :] = turn[pl.ds(2 * LEV, LEV), :]
    copies[5].wait()
    own[pl.ds(NORTH_V, LEV), :] = vel[pl.ds(CELLS + BN - 1, LEV, stride=BN), :]
    pltpu.sync_copy(own, item)


def pack(tracers, velocity, depth):
    return pl.pallas_call(
        pack_kernel,
        out_shape=pltpu.HBM((ITEM, BE), F32),
        in_specs=[HBM, HBM, HBM],
        out_specs=HBM,
        scratch_shapes=[
            pltpu.VMEM((4 * CELLS, BE), F32),
            pltpu.VMEM((2 * CELLS, BE), F32),
            pltpu.VMEM((BE, BE), F32),
            pltpu.VMEM((ITEM, BE), F32),
            pltpu.VMEM((BN, BE), F32),
            pltpu.SemaphoreType.DMA((7,)),
        ],
        compiler_params=params(12),
        name="pack",
    )(tracers, velocity, depth)


def select_kernel(plan, got, out, chosen_parts):
    def one(d, carry):
        chosen_parts[d] = got[plan[RELAY + d]]
        return carry

    lax.fori_loop(0, 128, one, 0, unroll=8)
    pltpu.sync_copy(chosen_parts, out)


def select(plan, got):
    return pl.pallas_call(
        select_kernel,
        out_shape=pltpu.HBM((128, PART, BE), F32),
        in_specs=[SM, VM],
        out_specs=HBM,
        scratch_shapes=[pltpu.VMEM((128, PART, BE), F32)],
        compiler_params=params(2),
        name="select",
    )(plan, got)


def stencil_loads(fields, chunk, tracers, velocity, mixing, q, u, v, mix, sems):
    parts = LEV // chunk
    rows = chunk * BN
    copies = []
    for c in range(parts):
        row = []
        for i, f in enumerate(fields):
            row.append(pltpu.make_async_copy(
                tracers.at[pl.ds(f * CELLS + c * rows, rows)], q[i].at[pl.ds(8 + c * rows, rows)],
                sems.at[c, i]))
        row.append(pltpu.make_async_copy(
            velocity.at[pl.ds(CELLS + c * rows, rows)], v.at[pl.ds(8 + c * rows, rows)], sems.at[c, 2]))
        row.append(pltpu.make_async_copy(
            velocity.at[pl.ds(c * rows, rows)], u.at[pl.ds(c * rows, rows)], sems.at[c, 3]))
        if mixing is not None:
            size = rows if c + 1 < parts else rows - BN
            row.append(pltpu.make_async_copy(
                mixing.at[pl.ds(c * rows, size)], mix.at[pl.ds(c * rows, size)], sems.at[c, 4]))
        copies.append(row)
    pad = jnp.zeros((8, BE), F32)
    for ref in (*q, v):
        ref[pl.ds(0, 8), :] = pad
        ref[pl.ds(8 + CELLS, 8), :] = pad
    return copies


def stencil_level(k, q, u, v, s):
    lane = lax.broadcasted_iota(jnp.int32, (BN, BE), 1)
    row_id = lax.broadcasted_iota(jnp.int32, (BN, BE), 0)
    at = pl.multiple_of(k * BN, BN)
    here, north, south = pl.ds(at + 8, BN), pl.ds(at + 9, BN), pl.ds(at + 7, BN)
    half_u = 0.5 * u[pl.ds(at, BN), :]
    half_w = pltpu.roll(half_u, 1, 1)
    ua = jnp.where(lane == BE - 1, 0.0, half_u + diffusion)
    ub = jnp.where(lane == BE - 1, 0.0, half_u - diffusion)
    uaw = jnp.where(lane == 0, 0.0, half_w + diffusion)
    ubw = jnp.where(lane == 0, 0.0, half_w - diffusion)
    half_v, half_s = 0.5 * v[here, :], 0.5 * v[south, :]
    va = jnp.where(row_id == BN - 1, 0.0, half_v + diffusion)
    vb = jnp.where(row_id == BN - 1, 0.0, half_v - diffusion)
    vas = jnp.where(row_id == 0, 0.0, half_s + diffusion)
    vbs = jnp.where(row_id == 0, 0.0, half_s - diffusion)
    centre = 1.0 - (ua - ubw) - (va - vbs)
    for f in range(2):
        tile = q[f][here, :]
        s[pl.ds(pl.multiple_of(f * CELLS + at, BN), BN), :] = (
            centre * tile - ub * pltpu.roll(tile, BE - 1, 1) + uaw * pltpu.roll(tile, 1, 1)
            - vb * q[f][north, :] + vas * q[f][south, :])


AHEAD = 6


def begin(copies, c):
    for copy in copies[c] if c < len(copies) else ():
        copy.start()


def arrived(copies, c, beyond=0):
    for d in range(1 + beyond) if c == 0 else (c + beyond,):
        for copy in copies[d] if d < len(copies) else ():
            copy.wait()
    begin(copies, c + AHEAD)


def stencil_kernel(group, chunk, *refs):
    parts = LEV // chunk
    rows = chunk * BN
    if group == 0:
        tracers, velocity, mixing, s, inv_out, q0, q1, u, v, inv, mix, sems, out_sems = refs
    else:
        tracers, velocity, stirred, q0, q1, u, v, s, sems, out_sems = refs
        mixing = mix = None
    q = (q0, q1)
    copies = stencil_loads((2 * group, 2 * group + 1), chunk, tracers, velocity, mixing, q, u, v, mix, sems)
    for c in range(AHEAD):
        begin(copies, c)
    zero = jnp.zeros((BN, BE), F32)
    if group == 0:
        mix[pl.ds(CELLS - BN, BN), :] = zero

    def level(k, carry):
        stencil_level(k, q, u, v, s)
        if group == 1:
            return carry
        m_up, fac_up = carry
        span = pl.ds(pl.multiple_of(k * BN, BN), BN)
        m = mix[span, :]
        inverse = 1.0 / (1.0 + m_up + m - m_up * fac_up)
        inv[span, :] = inverse
        return m, m * inverse

    carry = (zero, zero) if group == 0 else 0
    outs = []
    for c in range(parts):
        arrived(copies, c, 1)
        carry = lax.fori_loop(c * chunk, (c + 1) * chunk, level, carry, unroll=2)
        if group == 0:
            span = pl.ds(c * rows, rows)
            outs.append(pltpu.make_async_copy(inv.at[span], inv_out.at[span], out_sems.at[c, 0]))
            outs[-1].start()
        else:
            for f in range(2):
                span = pl.ds(f * CELLS + c * rows, rows)
                outs.append(pltpu.make_async_copy(s.at[span], stirred.at[span], out_sems.at[c, f]))
                outs[-1].start()
    for copy in outs:
        copy.wait()


def cells(extra=0, fields=1):
    return pltpu.VMEM((fields * CELLS + extra, BE), F32)


def stencil(group, args, chunk=6):
    parts = LEV // chunk
    if group == 0:
        outs, out_specs = (cells(0, 2), pltpu.HBM((CELLS, BE), F32)), (VM, HBM)
        more = [cells(), cells()]
    else:
        outs, out_specs = (pltpu.HBM((2 * CELLS, BE), F32),), (HBM,)
        more = [cells(0, 2)]
    return pl.pallas_call(
        functools.partial(stencil_kernel, group, chunk),
        out_shape=outs,
        in_specs=[HBM] * len(args),
        out_specs=out_specs,
        scratch_shapes=[
            cells(16), cells(16), cells(), cells(16), *more,
            pltpu.SemaphoreType.DMA((parts, 5)),
            pltpu.SemaphoreType.DMA((parts, 2)),
        ],
        compiler_params=params(10),
        name=f"stencil{group}",
    )(*args)


EDGE_N, EDGE_S, EDGE = BN, BN + 40, BN + 80
EDGE_D = 4 * EDGE


def flux(speed, low, high):
    return speed * (0.5 * (low + high)) - diffusion * (high - low)


def edges(plan, own, halo, out, turn):
    lane = lax.broadcasted_iota(jnp.int32, (LEV, BE), 1)
    open_e, open_w, open_n, open_s = (plan[NBR + d] >= 0 for d in range(4))
    row = lambda ref, at: ref[pl.ds(at, LEV), :]
    v_own, v_south = row(own, NORTH_V), row(halo, NORTH_V)
    for f in range(4):
        fn = flux(v_own, row(own, NORTH_Q[f]), row(halo, SOUTH_Q[f]))
        fs = flux(v_south, row(halo, NORTH_Q[f]), row(own, SOUTH_Q[f]))
        out[pl.ds(f * EDGE + EDGE_N, LEV), :] = jnp.where(open_n, -fn, 0.0)
        out[pl.ds(f * EDGE + EDGE_S, LEV), :] = jnp.where(open_s, fs, 0.0)

    def both(speed):
        return jnp.where(lane < HALF, speed, pltpu.roll(speed, HALF, 1))

    u_own, u_west = both(row(own, EAST + 2 * LEV)), both(row(halo, EAST + 2 * LEV))
    for j in range(2):
        fe = flux(u_own, row(own, EAST + j * LEV), row(halo, WEST + j * LEV))
        fw = flux(u_west, row(halo, EAST + j * LEV), row(own, WEST + j * LEV))
        turn[...] = jnp.zeros((BE, BE), F32)
        turn[pl.ds(0, LEV, stride=2), :] = jnp.where(open_e, -fe, 0.0)
        turn[pl.ds(1, LEV, stride=2), :] = jnp.where(open_w, fw, 0.0)
        turned = turn[...].T
        out[pl.ds(j * EDGE, BN), :] = turned[:BN]
        out[pl.ds((2 + j) * EDGE, BN), :] = turned[BN:]


def solve_kernel(group, chunk, out_chunk, *refs):
    parts = LEV // chunk
    rows = chunk * BN
    outs = []
    if group == 0:
        (plan, source, inv_in, mixing, own_in, halo, depth_in,
         new, edge_out, force_out, items, s, inv, mix, edge, turn, parts_out, own, depth, force,
         sems, out_sems, side_sems) = refs
        sides = [pltpu.make_async_copy(a, b, side_sems.at[i]) for i, (a, b) in enumerate(
            ((own_in, own), (depth_in, depth)))]
    else:
        (stirred, inv_in, mixing, edge_in, _aliased,
         new, s, inv, mix, edge, sems, out_sems, side_sems) = refs
        source = s
        sides = [pltpu.make_async_copy(edge_in, edge, side_sems.at[0])]
    for copy in sides:
        copy.start()
    first = 2 * group
    copies = []
    for c in range(parts):
        row = []
        if group == 1:
            for f in range(2):
                span = pl.ds(f * CELLS + c * rows, rows)
                row.append(pltpu.make_async_copy(stirred.at[span], s.at[span], sems.at[c, f]))
        span = pl.ds(c * rows, rows)
        row.append(pltpu.make_async_copy(inv_in.at[span], inv.at[span], sems.at[c, 2]))
        span = pl.ds(c * rows, rows if c + 1 < parts else rows - BN)
        row.append(pltpu.make_async_copy(mixing.at[span], mix.at[span], sems.at[c, 3]))
        copies.append(row)
        begin(copies, c)
    for copy in sides:
        copy.wait()
    if group == 0:
        edges(plan, own, halo, edge, turn)
        edge[pl.ds(EDGE_D, 8), :] = halo[pl.ds(NORTH_D - 4, 8), :]
        edge[pl.ds(EDGE_D + 8, 8), :] = halo[pl.ds(SOUTH_D, 8), :]
        outs.append(pltpu.make_async_copy(edge, edge_out, side_sems.at[3]))
        outs[-1].start()
    lane = lax.broadcasted_iota(jnp.int32, (BN, BE), 1)
    rim = jnp.logical_or(lane == 0, lane == BE - 1)
    sub = lax.broadcasted_iota(jnp.int32, (8, BE), 0)
    tile = lambda f, k: pl.ds(f * CELLS + k * BN, BN)
    m_up, sol_up = None, [None, None]
    columns = [edge[pl.ds((first + f) * EDGE, BN), :] for f in range(2)]

    for c in range(parts):
        for copy in copies[c]:
            copy.wait()
        for k in range(c * chunk, (c + 1) * chunk):
            inverse = inv[tile(0, k), :]
            for f in range(2):
                value = source[tile(f, k), :] + jnp.where(
                    rim, pltpu.roll(columns[f], BE - 1 - 2 * k, 1), 0.0)
                row = (first + f) * EDGE + k
                value = jnp.concatenate([
                    value[:8] + jnp.where(sub == 0, edge[pl.ds(row + EDGE_S, 1), :], 0.0),
                    value[8:BN - 8],
                    value[BN - 8:] + jnp.where(sub == 7, edge[pl.ds(row + EDGE_N, 1), :], 0.0),
                ], axis=0)
                if k:
                    value = value + m_up * sol_up[f]
                sol_up[f] = value * inverse
                s[tile(f, k), :] = sol_up[f]
            m_up = mix[tile(0, k), :] if k + 1 < LEV else None
    heat, salt = sol_up
    total = None
    for k in range(LEV - 1, -1, -1):
        if k + 1 < LEV:
            factor = mix[tile(0, k), :] * inv[tile(0, k), :]
            heat = s[tile(0, k), :] + factor * heat
            salt = s[tile(1, k), :] + factor * salt
            s[tile(0, k), :] = heat
            s[tile(1, k), :] = salt
        if group == 0:
            weight = forcing * 2.0 * (k + 1) / (LEV * (LEV + 1))
            density = (haline * weight) * salt - heat * (thermal * weight + (cabbeling * weight) * heat)
            total = density if total is None else total + density
        if k % out_chunk == 0:
            for f in range(2):
                outs.append(pltpu.make_async_copy(
                    s.at[pl.ds(f * CELLS + k * BN, out_chunk * BN)],
                    new.at[pl.ds((first + f) * CELLS + k * BN, out_chunk * BN)],
                    out_sems.at[k // out_chunk, f]))
                outs[-1].start()
    if group == 0:
        field = total
        force[...] = field
        outs.append(pltpu.make_async_copy(force, force_out, side_sems.at[4]))
        outs[-1].start()
        turned = jnp.concatenate([field, depth[...]], axis=0).T
        east_item, west_item = turned[BE - 3:, :], turned[:3, :]
        sends = (east_item, west_item, field[BN - 3:, :], field[:3, :],
                 east_item, west_item, east_item, west_item)
        for d, item in enumerate(sends):
            to = plan[NBR + d]

            @pl.when(to >= 0)
            def _(to=to, item=item):
                parts_out[to, pl.ds(0, 3), :] = item

        outs.append(pltpu.make_async_copy(parts_out, items, side_sems.at[5]))
        outs[-1].start()
    for copy in outs:
        copy.wait()


def solve(group, args, chunk=12, out_chunk=6):
    outs, out_specs = [pltpu.HBM((4 * CELLS, BE), F32)], [HBM]
    edge_rows = EDGE_D + 16
    block = lambda rows: pltpu.VMEM((rows, BE), F32)
    aliases = {}
    scratch = [cells(0, 2), cells(), cells(), block(edge_rows)]
    if group == 0:
        in_specs = [SM, VM, HBM, HBM, HBM, VM, HBM]
        outs += [pltpu.HBM((edge_rows, BE), F32), pltpu.HBM((BN, BE), F32),
                 pltpu.HBM((128, PART, BE), F32)]
        out_specs += [HBM] * 3
        scratch += [block(BE), pltpu.VMEM((128, PART, BE), F32), block(ITEM), block(BN), block(BN)]
    else:
        in_specs = [HBM] * 5
        aliases = {4: 0}
    scratch += [pltpu.SemaphoreType.DMA((LEV // chunk, 4)),
                pltpu.SemaphoreType.DMA((LEV // out_chunk, 2)), pltpu.SemaphoreType.DMA((6,))]
    return pl.pallas_call(
        functools.partial(solve_kernel, group, chunk, out_chunk),
        out_shape=tuple(outs),
        in_specs=in_specs,
        out_specs=tuple(out_specs),
        input_output_aliases=aliases,
        scratch_shapes=scratch,
        compiler_params=params(8),
        name=f"solve{group}",
    )(*args)


def chosen(shift, arrays, start, rows):
    value = arrays[-1][pl.ds(start, rows), :]
    for k in range(len(arrays) - 1):
        value = jnp.where(shift == k, arrays[k][pl.ds(start, rows), :], value)
    return value


TALL, WIDE = BN + 8, 2 * BE


def krylov_kernel(plan, field, depth, edge, got, vectors, sums, b_s, d_s, edge_d, sems):
    copies = [
        pltpu.make_async_copy(field, b_s.at[pl.ds(0, BN), pl.ds(0, BE)], sems.at[0]),
        pltpu.make_async_copy(depth, d_s.at[pl.ds(0, BN), pl.ds(0, BE)], sems.at[1]),
        pltpu.make_async_copy(edge.at[pl.ds(EDGE_D, 16)], edge_d, sems.at[2]),
    ]
    for copy in copies:
        copy.start()
    nothing = jnp.zeros((3, BE), F32)

    def item(d):
        to = plan[NBR + d]
        return jnp.where(to >= 0, got[jnp.maximum(to, 0), pl.ds(0, 3), :], nothing)

    for ref in (b_s, d_s):
        ref[pl.ds(BN, 8), :] = jnp.zeros((8, WIDE), F32)
    b_s[pl.ds(BN, 3), pl.ds(0, BE)] = item(2)
    b_s[pl.ds(TALL - 3, 3), pl.ds(0, BE)] = item(3)
    middle = jnp.zeros((BE - 6, BE), F32)
    sides = jnp.concatenate([item(0), middle, item(1)], axis=0).T
    b_s[pl.ds(0, BN), pl.ds(BE, BE)] = sides[:BN]
    d_s[pl.ds(0, BN), pl.ds(BE, BE)] = sides[BN:]
    place = lax.broadcasted_iota(jnp.int32, (3, BE), 1)
    place = jnp.where(place >= BN, place - BN, place)

    def corner(north, south):
        return jnp.where(place < 3, north, jnp.where(
            jnp.logical_and(place >= 5, place < 8), pltpu.roll(south, BE - BN + 8, 1), 0.0))

    corners = jnp.concatenate([corner(item(4), item(6)), middle, corner(item(5), item(7))], axis=0).T
    b_s[pl.ds(BN, 8), pl.ds(BE, BE)] = corners[:8]
    d_s[pl.ds(BN, 8), pl.ds(BE, BE)] = corners[BN:BN + 8]

    for copy in copies:
        copy.wait()
    d_s[pl.ds(BN, 3), pl.ds(0, BE)] = jnp.where(
        plan[NBR + 2] >= 0, edge_d[pl.ds(8, 3), :], 0.0)
    d_s[pl.ds(TALL - 3, 3), pl.ds(0, BE)] = jnp.where(
        plan[NBR + 3] >= 0, edge_d[pl.ds(4, 3), :], 0.0)
    d = d_s[...]
    east = lambda a: pltpu.roll(a, WIDE - 1, 1)
    west = lambda a: pltpu.roll(a, 1, 1)
    north = lambda a: pltpu.roll(a, TALL - 1, 0)
    south = lambda a: pltpu.roll(a, 1, 0)
    d_e, d_n = east(d), north(d)
    w_e = jnp.where(jnp.logical_and(d > 0, d_e > 0), 0.5 * (d + d_e), 0.0)
    w_n = jnp.where(jnp.logical_and(d > 0, d_n > 0), 0.5 * (d + d_n), 0.0)
    w_w, w_s = west(w_e), south(w_n)
    diagonal = area_term + w_e + w_w + w_n + w_s

    def operate(h):
        return diagonal * h - w_e * east(h) - w_w * west(h) - w_n * north(h) - w_s * south(h)

    v0 = b_s[...]
    v1 = operate(v0)
    v2 = operate(v1)
    v3 = operate(v2)
    v = [a[:BN, :BE] for a in (v0, v1, v2, v3)]
    for i in range(3):
        vectors[pl.ds(i * BN, BN), :] = v[i]
    pairs = ((0, 0), (0, 1), (1, 1), (1, 2), (2, 2), (2, 3))
    at = lax.broadcasted_iota(jnp.int32, (1, BE), 1)
    total = jnp.zeros((1, BE), F32)
    for i, (a, b) in enumerate(pairs):
        value = jnp.sum(jnp.sum(v[a] * v[b], axis=0, keepdims=True), axis=1, keepdims=True)
        total = jnp.where(at == i, value, total)
    for i in range(128):
        sums[i] = total


def krylov(plan, field, depth, edge, got):
    return pl.pallas_call(
        krylov_kernel,
        out_shape=(
            jax.ShapeDtypeStruct((3 * BN, BE), F32),
            jax.ShapeDtypeStruct((128, 1, BE), F32),
        ),
        in_specs=[SM] + [HBM] * 3 + [VM],
        out_specs=(VM, VM),
        scratch_shapes=[pltpu.VMEM((TALL, WIDE), F32)] * 2 + [
            pltpu.VMEM((16, BE), F32), pltpu.SemaphoreType.DMA((3,))],
        compiler_params=params(4),
        name="krylov",
    )(plan, field, depth, edge, got)


def combine_kernel(plan, sums, a0, a1, a2, a3, o0, o1, o2, o3):
    total = jnp.sum(sums[...], axis=0, keepdims=True)
    moment = [total[:, i:i + 1] for i in range(6)]

    def inner(a, b, lift):
        value = None
        for i in range(len(a)):
            for j in range(len(b)):
                term = a[i] * b[j] * moment[i + j + lift]
                value = term if value is None else value + term
        return value

    one = jnp.ones((1, 1), F32)
    zero = jnp.zeros((1, 1), F32)
    residual, direction = [one], [one]
    solution = [zero, zero, zero]
    rr = moment[0]
    for step in range(3):
        alpha = rr / inner(direction, direction, 1)
        for i, c in enumerate(direction):
            solution[i] = solution[i] + alpha * c
        if step < 2:
            image = [zero] + direction
            padded = residual + [zero]
            residual = [r - alpha * c for r, c in zip(padded, image)]
            following = inner(residual, residual, 0)
            beta = following / rr
            direction = [r + beta * c for r, c in zip(residual, direction + [zero])]
            rr = following
    solved = []
    for a in (a0, a1, a2, a3):
        v = [a[pl.ds(i * BN, BN), :] for i in range(3)]
        solved.append(solution[0] * v[0] + solution[1] * v[1] + solution[2] * v[2])
    for k, out in enumerate((o0, o1, o2, o3)):
        for b in range(2):
            shift = plan[TSEND + 2 * k + b]
            value = solved[3]
            for j in range(3):
                value = jnp.where(shift == j, solved[j], value)
            out[pl.ds(b * BN, BN), :] = value


def combine(plan, sums, arrays):
    return pl.pallas_call(
        combine_kernel,
        out_shape=(jax.ShapeDtypeStruct((2 * BN, BE), F32),) * 4,
        in_specs=[SM] + [VM] * 5,
        out_specs=(VM,) * 4,
        compiler_params=params(4),
        name="combine",
    )(plan, sums, *arrays)


def place_kernel(plan, a0, a1, a2, a3, out):
    for b in range(2):
        shift = plan[TFROM + b]
        value = chosen(shift, (a0, a1, a2, a3), b * BN, BN)
        out[b] = jnp.where(shift >= 0, value, 0.0)


def place(plan, arrays):
    return pl.pallas_call(
        place_kernel,
        out_shape=jax.ShapeDtypeStruct((2, BN, BE), F32),
        in_specs=[SM] + [VM] * 4,
        out_specs=VM,
        compiler_params=params(4),
        name="place",
    )(plan, *arrays)


def body(tracers, velocity, mixing_rate, column_depth, ocean_mask, clinic_list, tropic_list):
    n_gx, n_gy = lax.axis_size("gx"), lax.axis_size("gy")
    side = 4
    depth = column_depth.reshape(BN, BE)
    every = lambda value: lax.all_to_all(value, ("gx", "gy"), 0, 0)

    def along_y(value, k):
        return lax.ppermute(value, "gx", [
            (z * side + y, z * side + (y + k) % side) for z in range(side) for y in range(side)])

    def along_z(value, k):
        return lax.ppermute(value, "gx", [
            (z * side + y, (z + k) % side * side + y) for z in range(side) for y in range(side)])

    in_hbm = lambda value: pltpu.with_memory_space_constraint(value, pltpu.HBM)
    tracers = in_hbm(tracers.reshape(4 * CELLS, BE))
    velocity = in_hbm(velocity.reshape(2 * CELLS, BE))
    mixing = in_hbm(mixing_rate.reshape((LEV - 1) * BN, BE))
    depth = in_hbm(depth)
    own = pack(tracers, velocity, depth)
    plan = pl.pallas_call(
        functools.partial(plan_kernel, side, n_gy, n_gx),
        out_shape=jax.ShapeDtypeStruct((PLAN,), jnp.int32),
        in_specs=[SM, SM],
        out_specs=SM,
        scratch_shapes=[pltpu.SMEM(((n_gy + 2) * WRAP,), jnp.int32)],
        compiler_params=params(1),
        name="plan",
    )(clinic_list, tropic_list)
    in_vmem = lambda value: pltpu.with_memory_space_constraint(value, pltpu.VMEM)
    (last_two,) = stencil(1, (tracers, velocity))
    first_two, inv = stencil(0, (tracers, velocity, mixing))
    first_two, inv = in_vmem(first_two), in_hbm(inv)
    scattered = every(own.reshape(128, PART, BE))
    scattered, last_two = lax.optimization_barrier((scattered, last_two))
    halo = every(select(plan, scattered)).reshape(ITEM, BE)
    new, edge, field, items = solve(0, (plan, first_two, inv, mixing, in_hbm(own), halo, depth))
    got = every(items)
    edge, field = in_hbm(edge), in_hbm(field)
    (new,) = solve(1, (in_hbm(last_two), inv, mixing, edge, new))
    got, new = lax.optimization_barrier((got, new))
    vectors, sums = krylov(plan, field, depth, edge, got)
    totals = every(sums)
    line = [vectors] + [along_y(vectors, k) for k in range(1, side)]
    sends = combine(plan, totals.reshape(128, BE), line)
    arrived = [sends[0]] + [along_z(sends[k], k) for k in range(1, side)]
    height = place(plan, arrived)
    return new.reshape(1, 1, 4, LEV, BN, BE), height[None]


def solution(mesh):
    return jax.shard_map(
        body,
        mesh=mesh,
        in_specs=(
            P("gy", "gx", None, None, None, None),
            P("gy", "gx", None, None, None, None),
            P("gy", "gx", None, None, None),
            P("gy", "gx", None, None),
            P(),
            P(),
            P(),
        ),
        out_specs=(P("gy", "gx", None, None, None, None), P("gy", "gx", None, None)),
        check_vma=False,
    )
```

```python
import functools
import jax
import jax.numpy as jnp
from jax import lax
from jax.experimental import pallas as pl
from jax.experimental.pallas import tpu as pltpu
from jax.sharding import PartitionSpec as P

F32 = jnp.float32
LEV, BN, BE = 36, 64, 128
NBX = 28
N_GX, N_GY, SIDE = 16, 8, 4
CELLS = LEV * BN
HALF = BE // 2

NORTH = 0
NORTH_Q = (0, LEV, 3 * LEV, 4 * LEV)
NORTH_V = 2 * LEV
NORTH_D = 5 * LEV
SOUTH = 184
SOUTH_Q = tuple(SOUTH + f * LEV for f in range(4))
SOUTH_D = SOUTH + 4 * LEV
EAST = 332
WEST = 440
ITEM = 512
PART = 4

diffusion = 0.12
area_term = 0.1
thermal = 0.2
haline = 0.25
cabbeling = 0.05
forcing = 4.0

NBR = 0
TFROM = 8
TSEND = 10
RELAY = 18
PLAN = RELAY + 128
WRAP = NBX + 4

DIRS = ((0, 1), (0, -1), (1, 0), (-1, 0), (1, 1), (1, -1), (-1, 1), (-1, -1))


def params(mib, **more):
    return pltpu.CompilerParams(vmem_limit_bytes=mib * 1024 * 1024, **more)


VM = pl.BlockSpec(memory_space=pltpu.VMEM)
SM = pl.BlockSpec(memory_space=pltpu.SMEM)
ANY = pl.BlockSpec(memory_space=pl.ANY)
HBM = pl.BlockSpec(memory_space=pltpu.HBM)


def shaped(*shape):
    return jax.ShapeDtypeStruct(shape, F32)


def make_plan(side, n_gy, slots, clinic, tropic, out, pos):
    gx = lax.axis_index("gx")
    gy = lax.axis_index("gy")
    z = gx // side
    y = lax.rem(gx, side)

    def clear(i, carry):
        pos[i] = jnp.int32(-1)
        return carry

    lax.fori_loop(0, (n_gy + 2) * WRAP, clear, 0, unroll=16)
    for row in range(n_gy):
        for slot in range(slots):
            pos[(row + 1) * WRAP + 1 + clinic[row, slot]] = jnp.int32(slot * n_gy + row)
    for row in range(1, n_gy + 1):
        pos[row * WRAP] = pos[row * WRAP + NBX]
        pos[row * WRAP + NBX + 1] = pos[row * WRAP + 1]
    centre = (gy + 1) * WRAP + 1 + clinic[gy, gx]
    for d, (dr, dc) in enumerate(DIRS):
        out[NBR + d] = pos[centre + (dr * WRAP + dc)]
    me = gx * n_gy + gy
    kind_s, kind_n, kind_w = me < SOUTH // PART, me < EAST // PART, me < WEST // PART
    move = jnp.where(kind_s, jnp.int32(-WRAP), jnp.where(kind_n, jnp.int32(WRAP), jnp.where(
        kind_w, jnp.int32(-1), jnp.int32(1))))
    for row in range(n_gy):
        for there in range(slots):
            source = pos[(row + 1) * WRAP + 1 + clinic[row, there] + move]
            out[RELAY + there * n_gy + row] = jnp.maximum(source, 0)

    def owner(there, b):
        column_b = tropic[gy, 2 * there + b]
        device = pos[(gy + 1) * WRAP + 1 + jnp.maximum(column_b, 0)]
        return jnp.where(column_b < 0, jnp.int32(-1), device // n_gy)

    for k in range(side):
        there = lax.rem(z + k, side) * side + y
        for b in range(2):
            slot = owner(there, b)
            shift = lax.rem(y - lax.rem(slot, side) + side, side)
            out[TSEND + 2 * k + b] = jnp.where(slot < 0, jnp.int32(0), shift)
    for b in range(2):
        slot = owner(gx, b)
        shift = lax.rem(z - slot // side + side, side)
        out[TFROM + b] = jnp.where(slot < 0, jnp.int32(-1), shift)


def pack_kernel(tracers, velocity, depth_in, item, q, vel, turn, own, depth, sems):
    order = (0, 2, 4, 1, 3, 5)
    copies = {}
    fetch_depth = pltpu.make_async_copy(depth_in, depth, sems.at[6])
    fetch_depth.start()
    for f in order:
        source, at = (tracers, f) if f < 4 else (velocity, f - 4)
        target = q if f < 4 else vel
        span = pl.ds(at * CELLS, CELLS)
        copies[f] = pltpu.make_async_copy(source.at[span], target.at[span], sems.at[f])
        copies[f].start()
    fetch_depth.wait()
    lane = lax.broadcasted_iota(jnp.int32, (BN, BE), 1)
    level = lane // 2
    own[pl.ds(NORTH_D, 3), :] = depth[pl.ds(BN - 3, 3), :]
    own[pl.ds(NORTH_D + 3, 1), :] = jnp.zeros((1, BE), F32)
    own[pl.ds(SOUTH_D, 3), :] = depth[pl.ds(0, 3), :]
    own[pl.ds(SOUTH_D + 3, 1), :] = jnp.zeros((1, BE), F32)

    def columns(f):
        copies[f].wait()
        sides = jnp.zeros((BN, BE), F32)
        for k in range(LEV):
            tile = q[pl.ds(f * CELLS + k * BN, BN), :]
            sides = jnp.where(level == k, pltpu.roll(tile, 2 * k + 1, 1), sides)
        own[pl.ds(NORTH_Q[f], LEV), :] = q[pl.ds(f * CELLS + BN - 1, LEV, stride=BN), :]
        own[pl.ds(SOUTH_Q[f], LEV), :] = q[pl.ds(f * CELLS, LEV, stride=BN), :]
        return sides

    for j in range(2):
        first, second = columns(j), columns(2 + j)
        if j == 0:
            copies[4].wait()
            for k in range(LEV):
                tile = vel[pl.ds(k * BN, BN), :]
                first = jnp.where(lane == 2 * LEV + k, pltpu.roll(tile, 2 * LEV + 1 + k, 1), first)
        turn[...] = jnp.concatenate([first, second], axis=0).T
        own[pl.ds(EAST + j * LEV, LEV), :] = turn[pl.ds(0, LEV, stride=2), :]
        own[pl.ds(WEST + j * LEV, LEV), :] = turn[pl.ds(1, LEV, stride=2), :]
        if j == 0:
            own[pl.ds(EAST + 2 * LEV, LEV), :] = turn[pl.ds(2 * LEV, LEV), :]
    copies[5].wait()
    own[pl.ds(NORTH_V, LEV), :] = vel[pl.ds(CELLS + BN - 1, LEV, stride=BN), :]
    pltpu.sync_copy(own, item)


def pack(tracers, velocity, depth):
    return pl.pallas_call(
        pack_kernel,
        out_shape=pltpu.HBM((ITEM, BE), F32),
        in_specs=[HBM, HBM, HBM],
        out_specs=HBM,
        scratch_shapes=[
            pltpu.VMEM((4 * CELLS, BE), F32),
            pltpu.VMEM((2 * CELLS, BE), F32),
            pltpu.VMEM((BE, BE), F32),
            pltpu.VMEM((ITEM, BE), F32),
            pltpu.VMEM((BN, BE), F32),
            pltpu.SemaphoreType.DMA((7,)),
        ],
        compiler_params=params(12),
        name="pack",
    )(tracers, velocity, depth)


def select_kernel(plan, got, out, chosen_parts):
    def one(d, carry):
        chosen_parts[d] = got[plan[RELAY + d]]
        return carry

    lax.fori_loop(0, 128, one, 0, unroll=8)
    pltpu.sync_copy(chosen_parts, out)


def select(plan, got):
    return pl.pallas_call(
        select_kernel,
        out_shape=pltpu.HBM((128, PART, BE), F32),
        in_specs=[SM, VM],
        out_specs=HBM,
        scratch_shapes=[pltpu.VMEM((128, PART, BE), F32)],
        compiler_params=params(2),
        name="select",
    )(plan, got)


def stencil_loads(fields, chunk, tracers, velocity, mixing, q, u, v, mix, sems):
    parts = LEV // chunk
    rows = chunk * BN
    copies = []
    for c in range(parts):
        row = []
        for i, f in enumerate(fields):
            row.append(pltpu.make_async_copy(
                tracers.at[pl.ds(f * CELLS + c * rows, rows)], q[i].at[pl.ds(8 + c * rows, rows)],
                sems.at[c, i]))
        row.append(pltpu.make_async_copy(
            velocity.at[pl.ds(CELLS + c * rows, rows)], v.at[pl.ds(8 + c * rows, rows)], sems.at[c, 2]))
        row.append(pltpu.make_async_copy(
            velocity.at[pl.ds(c * rows, rows)], u.at[pl.ds(c * rows, rows)], sems.at[c, 3]))
        if mixing is not None:
            size = rows if c + 1 < parts else rows - BN
            row.append(pltpu.make_async_copy(
                mixing.at[pl.ds(c * rows, size)], mix.at[pl.ds(c * rows, size)], sems.at[c, 4]))
        copies.append(row)
    pad = jnp.zeros((8, BE), F32)
    for ref in (*q, v):
        ref[pl.ds(0, 8), :] = pad
        ref[pl.ds(8 + CELLS, 8), :] = pad
    return copies


def stencil_level(k, q, u, v, s):
    lane = lax.broadcasted_iota(jnp.int32, (BN, BE), 1)
    row_id = lax.broadcasted_iota(jnp.int32, (BN, BE), 0)
    at = pl.multiple_of(k * BN, BN)
    here, north, south = pl.ds(at + 8, BN), pl.ds(at + 9, BN), pl.ds(at + 7, BN)
    half_u = 0.5 * u[pl.ds(at, BN), :]
    ua = jnp.where(lane == BE - 1, 0.0, half_u + diffusion)
    ub = jnp.where(lane == BE - 1, 0.0, half_u - diffusion)
    half_v, half_s = 0.5 * v[here, :], 0.5 * v[south, :]
    va = jnp.where(row_id == BN - 1, 0.0, half_v + diffusion)
    vb = jnp.where(row_id == BN - 1, 0.0, half_v - diffusion)
    vas = jnp.where(row_id == 0, 0.0, half_s + diffusion)
    vbs = jnp.where(row_id == 0, 0.0, half_s - diffusion)
    centre = 1.0 - (va - vbs)
    for f in range(2):
        tile = q[f][here, :]
        fe = ua * tile + ub * pltpu.roll(tile, BE - 1, 1)
        s[pl.ds(pl.multiple_of(f * CELLS + at, BN), BN), :] = (
            centre * tile - (fe - pltpu.roll(fe, 1, 1))
            - vb * q[f][north, :] + vas * q[f][south, :])


AHEAD = 6


def begin(copies, c):
    for copy in copies[c] if c < len(copies) else ():
        copy.start()


def arrived(copies, c, beyond=0):
    for d in range(1 + beyond) if c == 0 else (c + beyond,):
        for copy in copies[d] if d < len(copies) else ():
            copy.wait()
    begin(copies, c + AHEAD)


def stencil_kernel(group, chunk, *refs):
    parts = LEV // chunk
    rows = chunk * BN
    if group == 0:
        tracers, velocity, mixing, s, inv_out, q0, q1, u, v, inv, mix, sems, out_sems = refs
    else:
        tracers, velocity, _aliased, s, new, q0, q1, u, v, sems, out_sems = refs
        mixing = mix = None
        leave = pltpu.make_async_copy(s, new.at[pl.ds(0, 2 * CELLS)], out_sems.at[0, 0])
        leave.start()
    q = (q0, q1)
    copies = stencil_loads((2 * group, 2 * group + 1), chunk, tracers, velocity, mixing, q, u, v, mix, sems)
    for c in range(AHEAD):
        begin(copies, c)
    zero = jnp.zeros((BN, BE), F32)
    if group == 0:
        mix[pl.ds(CELLS - BN, BN), :] = zero
    else:
        leave.wait()

    def level(k, carry):
        stencil_level(k, q, u, v, s)
        if group == 1:
            return carry
        m_up, fac_up = carry
        span = pl.ds(pl.multiple_of(k * BN, BN), BN)
        m = mix[span, :]
        inverse = 1.0 / (1.0 + m_up + m - m_up * fac_up)
        inv[span, :] = inverse
        return m, m * inverse

    carry = (zero, zero) if group == 0 else 0
    outs = []
    for c in range(parts):
        arrived(copies, c, 1)
        carry = lax.fori_loop(c * chunk, (c + 1) * chunk, level, carry, unroll=2)
        if group == 0:
            span = pl.ds(c * rows, rows)
            outs.append(pltpu.make_async_copy(inv.at[span], inv_out.at[span], out_sems.at[c, 0]))
            outs[-1].start()
    for copy in outs:
        copy.wait()


def cells(extra=0, fields=1):
    return pltpu.VMEM((fields * CELLS + extra, BE), F32)


def stencil(group, args, chunk=6):
    parts = LEV // chunk
    if group == 0:
        outs, out_specs = (cells(0, 2), pltpu.HBM((CELLS, BE), F32)), (VM, HBM)
        more = [cells(), cells()]
    else:
        outs, out_specs = (cells(0, 2), pltpu.HBM((4 * CELLS, BE), F32)), (VM, HBM)
        more = []
    return pl.pallas_call(
        functools.partial(stencil_kernel, group, chunk),
        out_shape=outs,
        in_specs=[HBM] * 3 if group == 0 else [HBM, HBM, VM],
        out_specs=out_specs,
        input_output_aliases={} if group == 0 else {2: 0},
        scratch_shapes=[
            cells(16), cells(16), cells(), cells(16), *more,
            pltpu.SemaphoreType.DMA((parts, 5)),
            pltpu.SemaphoreType.DMA((parts, 2)),
        ],
        compiler_params=params(10),
        name=f"stencil{group}",
    )(*args)


EDGE_N, EDGE_S, EDGE = BN, BN + 40, BN + 80
EDGE_D = 4 * EDGE


def flux(speed, low, high):
    return speed * (0.5 * (low + high)) - diffusion * (high - low)


def edges(plan, own, halo, out, turn):
    lane = lax.broadcasted_iota(jnp.int32, (LEV, BE), 1)
    open_e, open_w, open_n, open_s = (plan[NBR + d] >= 0 for d in range(4))
    row = lambda ref, at: ref[pl.ds(at, LEV), :]
    v_own, v_south = row(own, NORTH_V), row(halo, NORTH_V)
    for f in range(4):
        fn = flux(v_own, row(own, NORTH_Q[f]), row(halo, SOUTH_Q[f]))
        fs = flux(v_south, row(halo, NORTH_Q[f]), row(own, SOUTH_Q[f]))
        out[pl.ds(f * EDGE + EDGE_N, LEV), :] = jnp.where(open_n, -fn, 0.0)
        out[pl.ds(f * EDGE + EDGE_S, LEV), :] = jnp.where(open_s, fs, 0.0)

    def both(speed):
        return jnp.where(lane < HALF, speed, pltpu.roll(speed, HALF, 1))

    u_own, u_west = both(row(own, EAST + 2 * LEV)), both(row(halo, EAST + 2 * LEV))
    for j in range(2):
        fe = flux(u_own, row(own, EAST + j * LEV), row(halo, WEST + j * LEV))
        fw = flux(u_west, row(halo, EAST + j * LEV), row(own, WEST + j * LEV))
        turn[...] = jnp.zeros((BE, BE), F32)
        turn[pl.ds(0, LEV, stride=2), :] = jnp.where(open_e, -fe, 0.0)
        turn[pl.ds(1, LEV, stride=2), :] = jnp.where(open_w, fw, 0.0)
        turned = turn[...].T
        out[pl.ds(j * EDGE, BN), :] = turned[:BN]
        out[pl.ds((2 + j) * EDGE, BN), :] = turned[BN:]


def solve_kernel(group, chunk, out_chunk, *refs):
    parts = LEV // chunk
    rows = chunk * BN
    outs = []
    if group == 0:
        (plan, _aliased, inv_in, mixing, own_in, halo, depth_in,
         s, edge_out, force_out, items, inv, mix, edge, turn, parts_out, own, depth, force,
         sems, side_sems) = refs
        sides = [pltpu.make_async_copy(a, b, side_sems.at[i]) for i, (a, b) in enumerate(
            ((own_in, own), (depth_in, depth)))]
    else:
        (_stirred, inv_in, mixing, edge_in, _new,
         s, new, inv, mix, edge, sems, out_sems, side_sems) = refs
        sides = [pltpu.make_async_copy(edge_in, edge, side_sems.at[0])]
    for copy in sides:
        copy.start()
    first = 2 * group
    copies = []
    for c in range(parts):
        row = []
        span = pl.ds(c * rows, rows)
        row.append(pltpu.make_async_copy(inv_in.at[span], inv.at[span], sems.at[c, 2]))
        span = pl.ds(c * rows, rows if c + 1 < parts else rows - BN)
        row.append(pltpu.make_async_copy(mixing.at[span], mix.at[span], sems.at[c, 3]))
        copies.append(row)
        begin(copies, c)
    for copy in sides:
        copy.wait()
    if group == 0:
        edges(plan, own, halo, edge, turn)
        edge[pl.ds(EDGE_D, 8), :] = halo[pl.ds(NORTH_D - 4, 8), :]
        edge[pl.ds(EDGE_D + 8, 8), :] = halo[pl.ds(SOUTH_D, 8), :]
        outs.append(pltpu.make_async_copy(edge, edge_out, side_sems.at[3]))
        outs[-1].start()
    lane = lax.broadcasted_iota(jnp.int32, (BN, BE), 1)
    rim = jnp.logical_or(lane == 0, lane == BE - 1)
    sub = lax.broadcasted_iota(jnp.int32, (8, BE), 0)
    tile = lambda f, k: pl.ds(f * CELLS + k * BN, BN)
    m_up, sol_up = None, [None, None]
    columns = [edge[pl.ds((first + f) * EDGE, BN), :] for f in range(2)]

    for c in range(parts):
        for copy in copies[c]:
            copy.wait()
        for k in range(c * chunk, (c + 1) * chunk):
            inverse = inv[tile(0, k), :]
            for f in range(2):
                value = s[tile(f, k), :] + jnp.where(
                    rim, pltpu.roll(columns[f], BE - 1 - 2 * k, 1), 0.0)
                row = (first + f) * EDGE + k
                value = jnp.concatenate([
                    value[:8] + jnp.where(sub == 0, edge[pl.ds(row + EDGE_S, 1), :], 0.0),
                    value[8:BN - 8],
                    value[BN - 8:] + jnp.where(sub == 7, edge[pl.ds(row + EDGE_N, 1), :], 0.0),
                ], axis=0)
                if k:
                    value = value + m_up * sol_up[f]
                sol_up[f] = value * inverse
                s[tile(f, k), :] = sol_up[f]
            m_up = mix[tile(0, k), :] if k + 1 < LEV else None
    heat, salt = sol_up
    total = None
    for k in range(LEV - 1, -1, -1):
        if k + 1 < LEV:
            factor = mix[tile(0, k), :] * inv[tile(0, k), :]
            heat = s[tile(0, k), :] + factor * heat
            salt = s[tile(1, k), :] + factor * salt
            s[tile(0, k), :] = heat
            s[tile(1, k), :] = salt
        if group == 0:
            weight = forcing * 2.0 * (k + 1) / (LEV * (LEV + 1))
            density = (haline * weight) * salt - heat * (thermal * weight + (cabbeling * weight) * heat)
            total = density if total is None else total + density
        if group == 1 and k % out_chunk == 0:
            for f in range(2):
                outs.append(pltpu.make_async_copy(
                    s.at[pl.ds(f * CELLS + k * BN, out_chunk * BN)],
                    new.at[pl.ds((first + f) * CELLS + k * BN, out_chunk * BN)],
                    out_sems.at[k // out_chunk, f]))
                outs[-1].start()
    if group == 0:
        field = total
        force[...] = field
        outs.append(pltpu.make_async_copy(force, force_out, side_sems.at[4]))
        outs[-1].start()
        turned = jnp.concatenate([field, depth[...]], axis=0).T
        east_item, west_item = turned[BE - 3:, :], turned[:3, :]
        sends = (east_item, west_item, field[BN - 3:, :], field[:3, :],
                 east_item, west_item, east_item, west_item)
        for d, item in enumerate(sends):
            to = plan[NBR + d]

            @pl.when(to >= 0)
            def _(to=to, item=item):
                parts_out[to, pl.ds(0, 3), :] = item

        outs.append(pltpu.make_async_copy(parts_out, items, side_sems.at[5]))
        outs[-1].start()
    for copy in outs:
        copy.wait()


def solve(group, args, chunk=12, out_chunk=6):
    edge_rows = EDGE_D + 16
    block = lambda rows: pltpu.VMEM((rows, BE), F32)
    if group == 0:
        in_specs = [SM, VM, HBM, HBM, HBM, VM, HBM]
        outs = [cells(0, 2), pltpu.HBM((edge_rows, BE), F32), pltpu.HBM((BN, BE), F32),
                pltpu.HBM((128, PART, BE), F32)]
        out_specs = [VM] + [HBM] * 3
        scratch = [cells(), cells(), block(edge_rows), block(BE), pltpu.VMEM((128, PART, BE), F32),
                   block(ITEM), block(BN), block(BN)]
    else:
        in_specs = [VM] + [HBM] * 4
        outs, out_specs = [cells(0, 2), pltpu.HBM((4 * CELLS, BE), F32)], [VM, HBM]
        scratch = [cells(), cells(), block(edge_rows)]
    scratch += [pltpu.SemaphoreType.DMA((LEV // chunk, 4))]
    if group == 1:
        scratch += [pltpu.SemaphoreType.DMA((LEV // out_chunk, 2))]
    scratch += [pltpu.SemaphoreType.DMA((6,))]
    return pl.pallas_call(
        functools.partial(solve_kernel, group, chunk, out_chunk),
        out_shape=tuple(outs),
        in_specs=in_specs,
        out_specs=tuple(out_specs),
        scratch_shapes=scratch,
        input_output_aliases={1: 0} if group == 0 else {0: 0, 4: 1},
        compiler_params=params(8),
        name=f"solve{group}",
    )(*args)


def chosen(shift, arrays, start, rows):
    value = arrays[-1][pl.ds(start, rows), :]
    for k in range(len(arrays) - 1):
        value = jnp.where(shift == k, arrays[k][pl.ds(start, rows), :], value)
    return value


TALL, WIDE = BN + 8, 2 * BE


def krylov_kernel(plan, field, depth, edge, got, vectors, sums, b_s, d_s, edge_d, sems):
    copies = [
        pltpu.make_async_copy(field, b_s.at[pl.ds(0, BN), pl.ds(0, BE)], sems.at[0]),
        pltpu.make_async_copy(depth, d_s.at[pl.ds(0, BN), pl.ds(0, BE)], sems.at[1]),
        pltpu.make_async_copy(edge.at[pl.ds(EDGE_D, 16)], edge_d, sems.at[2]),
    ]
    for copy in copies:
        copy.start()
    nothing = jnp.zeros((3, BE), F32)

    def item(d):
        to = plan[NBR + d]
        return jnp.where(to >= 0, got[jnp.maximum(to, 0), pl.ds(0, 3), :], nothing)

    for ref in (b_s, d_s):
        ref[pl.ds(BN, 8), :] = jnp.zeros((8, WIDE), F32)
    b_s[pl.ds(BN, 3), pl.ds(0, BE)] = item(2)
    b_s[pl.ds(TALL - 3, 3), pl.ds(0, BE)] = item(3)
    middle = jnp.zeros((BE - 6, BE), F32)
    sides = jnp.concatenate([item(0), middle, item(1)], axis=0).T
    b_s[pl.ds(0, BN), pl.ds(BE, BE)] = sides[:BN]
    d_s[pl.ds(0, BN), pl.ds(BE, BE)] = sides[BN:]
    place = lax.broadcasted_iota(jnp.int32, (3, BE), 1)
    place = jnp.where(place >= BN, place - BN, place)

    def corner(north, south):
        return jnp.where(place < 3, north, jnp.where(
            jnp.logical_and(place >= 5, place < 8), pltpu.roll(south, BE - BN + 8, 1), 0.0))

    corners = jnp.concatenate([corner(item(4), item(6)), middle, corner(item(5), item(7))], axis=0).T
    b_s[pl.ds(BN, 8), pl.ds(BE, BE)] = corners[:8]
    d_s[pl.ds(BN, 8), pl.ds(BE, BE)] = corners[BN:BN + 8]

    for copy in copies:
        copy.wait()
    d_s[pl.ds(BN, 3), pl.ds(0, BE)] = jnp.where(
        plan[NBR + 2] >= 0, edge_d[pl.ds(8, 3), :], 0.0)
    d_s[pl.ds(TALL - 3, 3), pl.ds(0, BE)] = jnp.where(
        plan[NBR + 3] >= 0, edge_d[pl.ds(4, 3), :], 0.0)
    d = d_s[...]
    east = lambda a: pltpu.roll(a, WIDE - 1, 1)
    west = lambda a: pltpu.roll(a, 1, 1)
    north = lambda a: pltpu.roll(a, TALL - 1, 0)
    south = lambda a: pltpu.roll(a, 1, 0)
    d_e, d_n = east(d), north(d)
    w_e = jnp.where(jnp.logical_and(d > 0, d_e > 0), 0.5 * (d + d_e), 0.0)
    w_n = jnp.where(jnp.logical_and(d > 0, d_n > 0), 0.5 * (d + d_n), 0.0)
    w_w, w_s = west(w_e), south(w_n)
    diagonal = area_term + w_e + w_w + w_n + w_s

    def operate(h):
        return diagonal * h - w_e * east(h) - w_w * west(h) - w_n * north(h) - w_s * south(h)

    v0 = b_s[...]
    v1 = operate(v0)
    v2 = operate(v1)
    v3 = operate(v2)
    v = [a[:BN, :BE] for a in (v0, v1, v2, v3)]
    for i in range(3):
        vectors[pl.ds(i * BN, BN), :] = v[i]
    pairs = ((0, 0), (0, 1), (1, 1), (1, 2), (2, 2), (2, 3))
    at = lax.broadcasted_iota(jnp.int32, (1, BE), 1)
    total = jnp.zeros((1, BE), F32)
    for i, (a, b) in enumerate(pairs):
        value = jnp.sum(jnp.sum(v[a] * v[b], axis=0, keepdims=True), axis=1, keepdims=True)
        total = jnp.where(at == i, value, total)
    for i in range(128):
        sums[i] = total


def krylov(plan, field, depth, edge, got):
    return pl.pallas_call(
        krylov_kernel,
        out_shape=(
            jax.ShapeDtypeStruct((3 * BN, BE), F32),
            jax.ShapeDtypeStruct((128, 1, BE), F32),
        ),
        in_specs=[SM] + [HBM] * 3 + [VM],
        out_specs=(VM, VM),
        scratch_shapes=[pltpu.VMEM((TALL, WIDE), F32)] * 2 + [
            pltpu.VMEM((16, BE), F32), pltpu.SemaphoreType.DMA((3,))],
        compiler_params=params(4),
        name="krylov",
    )(plan, field, depth, edge, got)


def combine_kernel(plan, sums, a0, a1, a2, a3, o0, o1, o2, o3):
    total = jnp.sum(sums[...], axis=0, keepdims=True)
    moment = [total[:, i:i + 1] for i in range(6)]

    def inner(a, b, lift):
        value = None
        for i in range(len(a)):
            for j in range(len(b)):
                term = a[i] * b[j] * moment[i + j + lift]
                value = term if value is None else value + term
        return value

    one = jnp.ones((1, 1), F32)
    zero = jnp.zeros((1, 1), F32)
    residual, direction = [one], [one]
    solution = [zero, zero, zero]
    rr = moment[0]
    for step in range(3):
        alpha = rr / inner(direction, direction, 1)
        for i, c in enumerate(direction):
            solution[i] = solution[i] + alpha * c
        if step < 2:
            image = [zero] + direction
            padded = residual + [zero]
            residual = [r - alpha * c for r, c in zip(padded, image)]
            following = inner(residual, residual, 0)
            beta = following / rr
            direction = [r + beta * c for r, c in zip(residual, direction + [zero])]
            rr = following
    solved = []
    for a in (a0, a1, a2, a3):
        v = [a[pl.ds(i * BN, BN), :] for i in range(3)]
        solved.append(solution[0] * v[0] + solution[1] * v[1] + solution[2] * v[2])
    for k, out in enumerate((o0, o1, o2, o3)):
        for b in range(2):
            shift = plan[TSEND + 2 * k + b]
            value = solved[3]
            for j in range(3):
                value = jnp.where(shift == j, solved[j], value)
            out[pl.ds(b * BN, BN), :] = value


def combine(plan, sums, arrays):
    return pl.pallas_call(
        combine_kernel,
        out_shape=(jax.ShapeDtypeStruct((2 * BN, BE), F32),) * 4,
        in_specs=[SM] + [VM] * 5,
        out_specs=(VM,) * 4,
        compiler_params=params(4),
        name="combine",
    )(plan, sums, *arrays)


def place_kernel(plan, a0, a1, a2, a3, out):
    for b in range(2):
        shift = plan[TFROM + b]
        value = chosen(shift, (a0, a1, a2, a3), b * BN, BN)
        out[b] = jnp.where(shift >= 0, value, 0.0)


def place(plan, arrays):
    return pl.pallas_call(
        place_kernel,
        out_shape=jax.ShapeDtypeStruct((2, BN, BE), F32),
        in_specs=[SM] + [VM] * 4,
        out_specs=VM,
        compiler_params=params(4),
        name="place",
    )(plan, *arrays)


def body(tracers, velocity, mixing_rate, column_depth, ocean_mask, clinic_list, tropic_list):
    side = SIDE
    depth = column_depth.reshape(BN, BE)
    every = lambda value: lax.all_to_all(value, ("gx", "gy"), 0, 0)

    def along_y(value, k):
        return lax.ppermute(value, "gx", [
            (z * side + y, z * side + (y + k) % side) for z in range(side) for y in range(side)])

    def along_z(value, k):
        return lax.ppermute(value, "gx", [
            (z * side + y, (z + k) % side * side + y) for z in range(side) for y in range(side)])

    in_hbm = lambda value: pltpu.with_memory_space_constraint(value, pltpu.HBM)
    tracers = in_hbm(tracers.reshape(4 * CELLS, BE))
    velocity = in_hbm(velocity.reshape(2 * CELLS, BE))
    mixing = in_hbm(mixing_rate.reshape((LEV - 1) * BN, BE))
    depth = in_hbm(depth)
    own = pack(tracers, velocity, depth)
    in_vmem = lambda value: pltpu.with_memory_space_constraint(value, pltpu.VMEM)
    plan = pl.pallas_call(
        functools.partial(make_plan, SIDE, N_GY, N_GX),
        out_shape=jax.ShapeDtypeStruct((PLAN,), jnp.int32),
        in_specs=[SM, SM],
        out_specs=SM,
        scratch_shapes=[pltpu.SMEM(((N_GY + 2) * WRAP,), jnp.int32)],
        compiler_params=params(1),
        name="plan",
    )(clinic_list, tropic_list)
    first_two, inv = stencil(0, (tracers, velocity, mixing))
    first_two, inv = in_vmem(first_two), in_hbm(inv)
    scattered = every(own.reshape(128, PART, BE))
    halo = every(select(plan, scattered)).reshape(ITEM, BE)
    mixed, edge, field, items = solve(0, (plan, first_two, inv, mixing, in_hbm(own), halo, depth))
    got = every(items)
    edge, field = in_hbm(edge), in_hbm(field)
    last_two, new = stencil(1, (tracers, velocity, in_vmem(mixed)))
    got, last_two = lax.optimization_barrier((got, last_two))
    vectors, sums = krylov(plan, field, depth, edge, got)
    totals = every(sums)
    _, new = solve(1, (in_vmem(last_two), inv, mixing, edge, in_hbm(new)))
    totals, new = lax.optimization_barrier((totals, new))
    line = [vectors] + [along_y(vectors, k) for k in range(1, side)]
    sends = combine(plan, totals.reshape(128, BE), line)
    arrived = [sends[0]] + [along_z(sends[k], k) for k in range(1, side)]
    height = place(plan, arrived)
    return new.reshape(1, 1, 4, LEV, BN, BE), height[None]


def solution(mesh):
    return jax.shard_map(
        body,
        mesh=mesh,
        in_specs=(
            P("gy", "gx", None, None, None, None),
            P("gy", "gx", None, None, None, None),
            P("gy", "gx", None, None, None),
            P("gy", "gx", None, None),
            P(),
            P(),
            P(),
        ),
        out_specs=(P("gy", "gx", None, None, None, None), P("gy", "gx", None, None)),
        check_vma=False,
    )
```

```python
import functools
import jax
import jax.numpy as jnp
from jax import lax
from jax.experimental import pallas as pl
from jax.experimental.pallas import tpu as pltpu
from jax.sharding import Mesh, PartitionSpec as P

F32 = jnp.float32
LEV, BN, BE = 36, 64, 128
NBX = 28
N_GX, N_GY, SIDE = 16, 8, 4
SIZES = {"z": 4, "y": 4, "x": 4, "c": 2}
EVERY = ('c', 'z', 'x', 'y')
CELLS = LEV * BN
HALF = BE // 2

NORTH = 0
NORTH_Q = (0, LEV, 3 * LEV, 4 * LEV)
NORTH_V = 2 * LEV
NORTH_D = 5 * LEV
SOUTH = 184
SOUTH_Q = tuple(SOUTH + f * LEV for f in range(4))
SOUTH_D = SOUTH + 4 * LEV
EAST = 332
WEST = 440
ITEM = 512
PART = 4

diffusion = 0.12
area_term = 0.1
thermal = 0.2
haline = 0.25
cabbeling = 0.05
forcing = 4.0

NBR = 0
TFROM = 8
TSEND = 10
RELAY = 18
PLAN = RELAY + 128
WRAP = NBX + 4

DIRS = ((0, 1), (0, -1), (1, 0), (-1, 0), (1, 1), (1, -1), (-1, 1), (-1, -1))


def params(mib, **more):
    return pltpu.CompilerParams(vmem_limit_bytes=mib * 1024 * 1024, **more)


VM = pl.BlockSpec(memory_space=pltpu.VMEM)
SM = pl.BlockSpec(memory_space=pltpu.SMEM)
ANY = pl.BlockSpec(memory_space=pl.ANY)
HBM = pl.BlockSpec(memory_space=pltpu.HBM)


def shaped(*shape):
    return jax.ShapeDtypeStruct(shape, F32)


def place_of(axis, slot, row):
    return {"z": slot // SIDE, "y": slot % SIDE, "x": row // 2, "c": row % 2}[axis]


def device_of(slot, row):
    index = 0
    for axis in EVERY:
        index = index * SIZES[axis] + place_of(axis, slot, row)
    return index


def slot_of(device):
    stride, at = 1, {}
    for axis in reversed(EVERY):
        at[axis] = lax.rem(device // stride, SIZES[axis])
        stride *= SIZES[axis]
    return at["z"] * SIDE + at["y"]


def make_plan(side, n_gy, slots, clinic, tropic, out, pos):
    z, y = lax.axis_index("z"), lax.axis_index("y")
    gx = z * side + y
    gy = lax.axis_index("x") * 2 + lax.axis_index("c")

    def clear(i, carry):
        pos[i] = jnp.int32(-1)
        return carry

    lax.fori_loop(0, (n_gy + 2) * WRAP, clear, 0, unroll=16)
    for row in range(n_gy):
        for slot in range(slots):
            pos[(row + 1) * WRAP + 1 + clinic[row, slot]] = jnp.int32(device_of(slot, row))
    for row in range(1, n_gy + 1):
        pos[row * WRAP] = pos[row * WRAP + NBX]
        pos[row * WRAP + NBX + 1] = pos[row * WRAP + 1]
    centre = (gy + 1) * WRAP + 1 + clinic[gy, gx]
    for d, (dr, dc) in enumerate(DIRS):
        out[NBR + d] = pos[centre + (dr * WRAP + dc)]
    me = jnp.int32(0)
    for axis in EVERY:
        me = me * SIZES[axis] + lax.axis_index(axis)
    kind_s, kind_n, kind_w = me < SOUTH // PART, me < EAST // PART, me < WEST // PART
    move = jnp.where(kind_s, jnp.int32(-WRAP), jnp.where(kind_n, jnp.int32(WRAP), jnp.where(
        kind_w, jnp.int32(-1), jnp.int32(1))))
    for row in range(n_gy):
        for there in range(slots):
            source = pos[(row + 1) * WRAP + 1 + clinic[row, there] + move]
            out[RELAY + device_of(there, row)] = jnp.maximum(source, 0)

    def owner(there, b):
        column_b = tropic[gy, 2 * there + b]
        device = pos[(gy + 1) * WRAP + 1 + jnp.maximum(column_b, 0)]
        return jnp.where(column_b < 0, jnp.int32(-1), slot_of(device))

    for k in range(side):
        there = lax.rem(z + k, side) * side + y
        for b in range(2):
            slot = owner(there, b)
            shift = lax.rem(y - lax.rem(slot, side) + side, side)
            out[TSEND + 2 * k + b] = jnp.where(slot < 0, jnp.int32(0), shift)
    for b in range(2):
        slot = owner(gx, b)
        shift = lax.rem(z - slot // side + side, side)
        out[TFROM + b] = jnp.where(slot < 0, jnp.int32(-1), shift)


def pack_kernel(tracers, velocity, depth_in, item, q, vel, turn, own, depth, sems):
    order = (0, 2, 4, 1, 3, 5)
    copies = {}
    fetch_depth = pltpu.make_async_copy(depth_in, depth, sems.at[6])
    fetch_depth.start()
    for f in order:
        source, at = (tracers, f) if f < 4 else (velocity, f - 4)
        target = q if f < 4 else vel
        span = pl.ds(at * CELLS, CELLS)
        copies[f] = pltpu.make_async_copy(source.at[span], target.at[span], sems.at[f])
        copies[f].start()
    fetch_depth.wait()
    lane = lax.broadcasted_iota(jnp.int32, (BN, BE), 1)
    level = lane // 2
    own[pl.ds(NORTH_D, 3), :] = depth[pl.ds(BN - 3, 3), :]
    own[pl.ds(NORTH_D + 3, 1), :] = jnp.zeros((1, BE), F32)
    own[pl.ds(SOUTH_D, 3), :] = depth[pl.ds(0, 3), :]
    own[pl.ds(SOUTH_D + 3, 1), :] = jnp.zeros((1, BE), F32)

    def columns(f):
        copies[f].wait()
        sides = jnp.zeros((BN, BE), F32)
        for k in range(LEV):
            tile = q[pl.ds(f * CELLS + k * BN, BN), :]
            sides = jnp.where(level == k, pltpu.roll(tile, 2 * k + 1, 1), sides)
        own[pl.ds(NORTH_Q[f], LEV), :] = q[pl.ds(f * CELLS + BN - 1, LEV, stride=BN), :]
        own[pl.ds(SOUTH_Q[f], LEV), :] = q[pl.ds(f * CELLS, LEV, stride=BN), :]
        return sides

    for j in range(2):
        first, second = columns(j), columns(2 + j)
        if j == 0:
            copies[4].wait()
            for k in range(LEV):
                tile = vel[pl.ds(k * BN, BN), :]
                first = jnp.where(lane == 2 * LEV + k, pltpu.roll(tile, 2 * LEV + 1 + k, 1), first)
        if j == 1:
            copies[5].wait()
            own[pl.ds(NORTH_V, LEV), :] = vel[pl.ds(CELLS + BN - 1, LEV, stride=BN), :]
            rows_out = pltpu.make_async_copy(own.at[pl.ds(0, 328)], item.at[pl.ds(0, 328)], sems.at[7])
            rows_out.start()
        turn[...] = jnp.concatenate([first, second], axis=0).T
        own[pl.ds(EAST + j * LEV, LEV), :] = turn[pl.ds(0, LEV, stride=2), :]
        own[pl.ds(WEST + j * LEV, LEV), :] = turn[pl.ds(1, LEV, stride=2), :]
        if j == 0:
            own[pl.ds(EAST + 2 * LEV, LEV), :] = turn[pl.ds(2 * LEV, LEV), :]
    rest = pl.ds(328, ITEM - 328)
    rest_out = pltpu.make_async_copy(own.at[rest], item.at[rest], sems.at[8])
    rest_out.start()
    rows_out.wait()
    rest_out.wait()


def pack(tracers, velocity, depth):
    return pl.pallas_call(
        pack_kernel,
        out_shape=pltpu.HBM((ITEM, BE), F32),
        in_specs=[HBM, HBM, HBM],
        out_specs=HBM,
        scratch_shapes=[
            pltpu.VMEM((4 * CELLS, BE), F32),
            pltpu.VMEM((2 * CELLS, BE), F32),
            pltpu.VMEM((BE, BE), F32),
            pltpu.VMEM((ITEM, BE), F32),
            pltpu.VMEM((BN, BE), F32),
            pltpu.SemaphoreType.DMA((9,)),
        ],
        compiler_params=params(12),
        name="pack",
    )(tracers, velocity, depth)


def select_kernel(plan, got, out, chosen_parts, sems):
    def one(d, carry):
        chosen_parts[d] = got[plan[RELAY + d]]
        return carry

    copies = []
    for half in range(2):
        lax.fori_loop(64 * half, 64 * half + 64, one, 0, unroll=16)
        span = pl.ds(64 * half, 64)
        copies.append(pltpu.make_async_copy(chosen_parts.at[span], out.at[span], sems.at[half]))
        copies[-1].start()
    for copy in copies:
        copy.wait()


def select(plan, got):
    return pl.pallas_call(
        select_kernel,
        out_shape=pltpu.HBM((128, PART, BE), F32),
        in_specs=[SM, VM],
        out_specs=HBM,
        scratch_shapes=[pltpu.VMEM((128, PART, BE), F32), pltpu.SemaphoreType.DMA((2,))],
        compiler_params=params(2),
        name="select",
    )(plan, got)


def stencil_loads(fields, chunk, tracers, velocity, mixing, q, u, v, mix, sems):
    parts = LEV // chunk
    rows = chunk * BN
    copies = []
    for c in range(parts):
        row = []
        for i, f in enumerate(fields):
            row.append(pltpu.make_async_copy(
                tracers.at[pl.ds(f * CELLS + c * rows, rows)], q[i].at[pl.ds(8 + c * rows, rows)],
                sems.at[c, i]))
        row.append(pltpu.make_async_copy(
            velocity.at[pl.ds(CELLS + c * rows, rows)], v.at[pl.ds(8 + c * rows, rows)], sems.at[c, 2]))
        row.append(pltpu.make_async_copy(
            velocity.at[pl.ds(c * rows, rows)], u.at[pl.ds(c * rows, rows)], sems.at[c, 3]))
        if mixing is not None:
            size = rows if c + 1 < parts else rows - BN
            row.append(pltpu.make_async_copy(
                mixing.at[pl.ds(c * rows, size)], mix.at[pl.ds(c * rows, size)], sems.at[c, 4]))
        copies.append(row)
    pad = jnp.zeros((8, BE), F32)
    for ref in (*q, v):
        ref[pl.ds(0, 8), :] = pad
        ref[pl.ds(8 + CELLS, 8), :] = pad
    return copies


def stencil_level(k, q, u, v, s):
    lane = lax.broadcasted_iota(jnp.int32, (BN, BE), 1)
    row_id = lax.broadcasted_iota(jnp.int32, (BN, BE), 0)
    at = pl.multiple_of(k * BN, BN)
    here, north, south = pl.ds(at + 8, BN), pl.ds(at + 9, BN), pl.ds(at + 7, BN)
    half_u = 0.5 * u[pl.ds(at, BN), :]
    ua = jnp.where(lane == BE - 1, 0.0, half_u + diffusion)
    ub = jnp.where(lane == BE - 1, 0.0, half_u - diffusion)
    half_v, half_s = 0.5 * v[here, :], 0.5 * v[south, :]
    va = jnp.where(row_id == BN - 1, 0.0, half_v + diffusion)
    vb = jnp.where(row_id == BN - 1, 0.0, half_v - diffusion)
    vas = jnp.where(row_id == 0, 0.0, half_s + diffusion)
    vbs = jnp.where(row_id == 0, 0.0, half_s - diffusion)
    centre = 1.0 - (va - vbs)
    for f in range(2):
        tile = q[f][here, :]
        fe = ua * tile + ub * pltpu.roll(tile, BE - 1, 1)
        s[pl.ds(pl.multiple_of(f * CELLS + at, BN), BN), :] = (
            centre * tile - (fe - pltpu.roll(fe, 1, 1))
            - vb * q[f][north, :] + vas * q[f][south, :])


AHEAD = 6


def begin(copies, c):
    for copy in copies[c] if c < len(copies) else ():
        copy.start()


def arrived(copies, c, beyond=0):
    for d in range(1 + beyond) if c == 0 else (c + beyond,):
        for copy in copies[d] if d < len(copies) else ():
            copy.wait()
    begin(copies, c + AHEAD)


def stencil_kernel(group, chunk, *refs):
    parts = LEV // chunk
    rows = chunk * BN
    if group == 0:
        tracers, velocity, mixing, s, inv_out, q0, q1, u, v, inv, mix, sems, out_sems = refs
    else:
        tracers, velocity, _aliased, s, new, q0, q1, u, v, sems, out_sems = refs
        mixing = mix = None
        leave = pltpu.make_async_copy(s, new.at[pl.ds(0, 2 * CELLS)], out_sems.at[0, 0])
        leave.start()
    q = (q0, q1)
    copies = stencil_loads((2 * group, 2 * group + 1), chunk, tracers, velocity, mixing, q, u, v, mix, sems)
    for c in range(AHEAD):
        begin(copies, c)
    zero = jnp.zeros((BN, BE), F32)
    if group == 0:
        mix[pl.ds(CELLS - BN, BN), :] = zero
    else:
        leave.wait()

    def level(k, carry):
        stencil_level(k, q, u, v, s)
        if group == 1:
            return carry
        m_up, fac_up = carry
        span = pl.ds(pl.multiple_of(k * BN, BN), BN)
        m = mix[span, :]
        inverse = 1.0 / (1.0 + m_up + m - m_up * fac_up)
        inv[span, :] = inverse
        return m, m * inverse

    carry = (zero, zero) if group == 0 else 0
    outs = []
    for c in range(parts):
        arrived(copies, c, 1)
        carry = lax.fori_loop(c * chunk, (c + 1) * chunk, level, carry, unroll=2)
        if group == 0:
            span = pl.ds(c * rows, rows)
            outs.append(pltpu.make_async_copy(inv.at[span], inv_out.at[span], out_sems.at[c, 0]))
            outs[-1].start()
    for copy in outs:
        copy.wait()


def cells(extra=0, fields=1):
    return pltpu.VMEM((fields * CELLS + extra, BE), F32)


def stencil(group, args, chunk=6):
    parts = LEV // chunk
    if group == 0:
        outs, out_specs = (cells(0, 2), pltpu.HBM((CELLS, BE), F32)), (VM, HBM)
        more = [cells(), cells()]
    else:
        outs, out_specs = (cells(0, 2), pltpu.HBM((4 * CELLS, BE), F32)), (VM, HBM)
        more = []
    return pl.pallas_call(
        functools.partial(stencil_kernel, group, chunk),
        out_shape=outs,
        in_specs=[HBM] * 3 if group == 0 else [HBM, HBM, VM],
        out_specs=out_specs,
        input_output_aliases={} if group == 0 else {2: 0},
        scratch_shapes=[
            cells(16), cells(16), cells(), cells(16), *more,
            pltpu.SemaphoreType.DMA((parts, 5)),
            pltpu.SemaphoreType.DMA((parts, 2)),
        ],
        compiler_params=params(10),
        name=f"stencil{group}",
    )(*args)


EDGE_N, EDGE_S, EDGE = BN, BN + 40, BN + 80
BASE_D, BASE_S, BASE_N, BASE = BN, 2 * BN, 2 * BN + 8, 2 * BN + 16


def flux(speed, low, high):
    return speed * (0.5 * (low + high)) - diffusion * (high - low)


def edges(plan, own, halo, out, turn):
    lane = lax.broadcasted_iota(jnp.int32, (LEV, BE), 1)
    open_e, open_w, open_n, open_s = (plan[NBR + d] >= 0 for d in range(4))
    row = lambda ref, at: ref[pl.ds(at, LEV), :]
    v_own, v_south = row(own, NORTH_V), row(halo, NORTH_V)
    for f in range(4):
        fn = flux(v_own, row(own, NORTH_Q[f]), row(halo, SOUTH_Q[f]))
        fs = flux(v_south, row(halo, NORTH_Q[f]), row(own, SOUTH_Q[f]))
        out[pl.ds(f * EDGE + EDGE_N, LEV), :] = jnp.where(open_n, -fn, 0.0)
        out[pl.ds(f * EDGE + EDGE_S, LEV), :] = jnp.where(open_s, fs, 0.0)

    def both(speed):
        return jnp.where(lane < HALF, speed, pltpu.roll(speed, HALF, 1))

    u_own, u_west = both(row(own, EAST + 2 * LEV)), both(row(halo, EAST + 2 * LEV))
    for j in range(2):
        fe = flux(u_own, row(own, EAST + j * LEV), row(halo, WEST + j * LEV))
        fw = flux(u_west, row(halo, EAST + j * LEV), row(own, WEST + j * LEV))
        turn[...] = jnp.zeros((BE, BE), F32)
        turn[pl.ds(0, LEV, stride=2), :] = jnp.where(open_e, -fe, 0.0)
        turn[pl.ds(1, LEV, stride=2), :] = jnp.where(open_w, fw, 0.0)
        turned = turn[...].T
        out[pl.ds(j * EDGE, BN), :] = turned[:BN]
        out[pl.ds((2 + j) * EDGE, BN), :] = turned[BN:]


def solve_kernel(group, chunk, out_chunk, *refs):
    parts = LEV // chunk
    rows = chunk * BN
    outs = []
    if group == 0:
        (plan, _aliased, inv_in, mixing, own_in, halo, depth_in,
         s, edge_out, base, items, inv, mix, edge, turn, parts_out, own, depth,
         sems, side_sems) = refs
        sides = [pltpu.make_async_copy(a, b, side_sems.at[i]) for i, (a, b) in enumerate(
            ((own_in, own), (depth_in, depth)))]
    else:
        (_stirred, inv_in, mixing, edge_in, _new,
         s, new, inv, mix, edge, sems, out_sems, side_sems) = refs
        sides = [pltpu.make_async_copy(edge_in, edge, side_sems.at[0])]
    for copy in sides:
        copy.start()
    first = 2 * group
    copies = []
    for c in range(parts):
        row = []
        span = pl.ds(c * rows, rows)
        row.append(pltpu.make_async_copy(inv_in.at[span], inv.at[span], sems.at[c, 2]))
        span = pl.ds(c * rows, rows if c + 1 < parts else rows - BN)
        row.append(pltpu.make_async_copy(mixing.at[span], mix.at[span], sems.at[c, 3]))
        copies.append(row)
        begin(copies, c)
    for copy in sides:
        copy.wait()
    if group == 0:
        edges(plan, own, halo, edge, turn)
        base[pl.ds(BASE_D, BN), :] = depth[...]
        base[pl.ds(BASE_S, 8), :] = halo[pl.ds(NORTH_D - 4, 8), :]
        base[pl.ds(BASE_N, 8), :] = halo[pl.ds(SOUTH_D, 8), :]
        outs.append(pltpu.make_async_copy(edge, edge_out, side_sems.at[3]))
        outs[-1].start()
    lane = lax.broadcasted_iota(jnp.int32, (BN, BE), 1)
    rim = jnp.logical_or(lane == 0, lane == BE - 1)
    sub = lax.broadcasted_iota(jnp.int32, (8, BE), 0)
    tile = lambda f, k: pl.ds(f * CELLS + k * BN, BN)
    m_up, sol_up = None, [None, None]
    columns = [edge[pl.ds((first + f) * EDGE, BN), :] for f in range(2)]

    for c in range(parts):
        for copy in copies[c]:
            copy.wait()
        for k in range(c * chunk, (c + 1) * chunk):
            inverse = inv[tile(0, k), :]
            for f in range(2):
                value = s[tile(f, k), :] + jnp.where(
                    rim, pltpu.roll(columns[f], BE - 1 - 2 * k, 1), 0.0)
                row = (first + f) * EDGE + k
                value = jnp.concatenate([
                    value[:8] + jnp.where(sub == 0, edge[pl.ds(row + EDGE_S, 1), :], 0.0),
                    value[8:BN - 8],
                    value[BN - 8:] + jnp.where(sub == 7, edge[pl.ds(row + EDGE_N, 1), :], 0.0),
                ], axis=0)
                if k:
                    value = value + m_up * sol_up[f]
                sol_up[f] = value * inverse
                s[tile(f, k), :] = sol_up[f]
            m_up = mix[tile(0, k), :] if k + 1 < LEV else None
    heat, salt = sol_up
    total = None
    for k in range(LEV - 1, -1, -1):
        if k + 1 < LEV:
            factor = mix[tile(0, k), :] * inv[tile(0, k), :]
            heat = s[tile(0, k), :] + factor * heat
            salt = s[tile(1, k), :] + factor * salt
            s[tile(0, k), :] = heat
            s[tile(1, k), :] = salt
        if group == 0:
            weight = forcing * 2.0 * (k + 1) / (LEV * (LEV + 1))
            density = (haline * weight) * salt - heat * (thermal * weight + (cabbeling * weight) * heat)
            total = density if total is None else total + density
        if group == 1 and k % out_chunk == 0:
            for f in range(2):
                outs.append(pltpu.make_async_copy(
                    s.at[pl.ds(f * CELLS + k * BN, out_chunk * BN)],
                    new.at[pl.ds((first + f) * CELLS + k * BN, out_chunk * BN)],
                    out_sems.at[k // out_chunk, f]))
                outs[-1].start()
    if group == 0:
        field = total
        base[pl.ds(0, BN), :] = field
        turned = jnp.concatenate([field, depth[...]], axis=0).T
        east_item, west_item = turned[BE - 3:, :], turned[:3, :]
        sends = (east_item, west_item, field[BN - 3:, :], field[:3, :],
                 east_item, west_item, east_item, west_item)
        for d, item in enumerate(sends):
            to = plan[NBR + d]

            @pl.when(to >= 0)
            def _(to=to, item=item):
                parts_out[to, pl.ds(0, 3), :] = item

        outs.append(pltpu.make_async_copy(parts_out, items, side_sems.at[5]))
        outs[-1].start()
    for copy in outs:
        copy.wait()


def solve(group, args, chunk=12, out_chunk=6):
    edge_rows = 4 * EDGE
    block = lambda rows: pltpu.VMEM((rows, BE), F32)
    if group == 0:
        in_specs = [SM, VM, HBM, HBM, HBM, VM, HBM]
        outs = [cells(0, 2), pltpu.HBM((edge_rows, BE), F32), block(BASE),
                pltpu.HBM((128, PART, BE), F32)]
        out_specs = [VM, HBM, VM, HBM]
        scratch = [cells(), cells(), block(edge_rows), block(BE), pltpu.VMEM((128, PART, BE), F32),
                   block(ITEM), block(BN)]
    else:
        in_specs = [VM] + [HBM] * 4
        outs, out_specs = [cells(0, 2), pltpu.HBM((4 * CELLS, BE), F32)], [VM, HBM]
        scratch = [cells(), cells(), block(edge_rows)]
    scratch += [pltpu.SemaphoreType.DMA((LEV // chunk, 4))]
    if group == 1:
        scratch += [pltpu.SemaphoreType.DMA((LEV // out_chunk, 2))]
    scratch += [pltpu.SemaphoreType.DMA((6,))]
    return pl.pallas_call(
        functools.partial(solve_kernel, group, chunk, out_chunk),
        out_shape=tuple(outs),
        in_specs=in_specs,
        out_specs=tuple(out_specs),
        scratch_shapes=scratch,
        input_output_aliases={1: 0} if group == 0 else {0: 0, 4: 1},
        compiler_params=params(8),
        name=f"solve{group}",
    )(*args)


def chosen(shift, arrays, start, rows):
    value = arrays[-1][pl.ds(start, rows), :]
    for k in range(len(arrays) - 1):
        value = jnp.where(shift == k, arrays[k][pl.ds(start, rows), :], value)
    return value


TALL, WIDE = BN + 8, 2 * BE


def krylov_kernel(plan, base, got, vectors, sums, b_s, d_s):
    nothing = jnp.zeros((3, BE), F32)

    def item(d):
        to = plan[NBR + d]
        return jnp.where(to >= 0, got[jnp.maximum(to, 0), pl.ds(0, 3), :], nothing)

    for ref in (b_s, d_s):
        ref[pl.ds(BN, 8), :] = jnp.zeros((8, WIDE), F32)
    b_s[pl.ds(0, BN), pl.ds(0, BE)] = base[pl.ds(0, BN), :]
    d_s[pl.ds(0, BN), pl.ds(0, BE)] = base[pl.ds(BASE_D, BN), :]
    b_s[pl.ds(BN, 3), pl.ds(0, BE)] = item(2)
    b_s[pl.ds(TALL - 3, 3), pl.ds(0, BE)] = item(3)
    middle = jnp.zeros((BE - 6, BE), F32)
    sides = jnp.concatenate([item(0), middle, item(1)], axis=0).T
    b_s[pl.ds(0, BN), pl.ds(BE, BE)] = sides[:BN]
    d_s[pl.ds(0, BN), pl.ds(BE, BE)] = sides[BN:]
    place = lax.broadcasted_iota(jnp.int32, (3, BE), 1)
    place = jnp.where(place >= BN, place - BN, place)

    def corner(north, south):
        return jnp.where(place < 3, north, jnp.where(
            jnp.logical_and(place >= 5, place < 8), pltpu.roll(south, BE - BN + 8, 1), 0.0))

    corners = jnp.concatenate([corner(item(4), item(6)), middle, corner(item(5), item(7))], axis=0).T
    b_s[pl.ds(BN, 8), pl.ds(BE, BE)] = corners[:8]
    d_s[pl.ds(BN, 8), pl.ds(BE, BE)] = corners[BN:BN + 8]

    d_s[pl.ds(BN, 3), pl.ds(0, BE)] = jnp.where(
        plan[NBR + 2] >= 0, base[pl.ds(BASE_N, 3), :], 0.0)
    d_s[pl.ds(TALL - 3, 3), pl.ds(0, BE)] = jnp.where(
        plan[NBR + 3] >= 0, base[pl.ds(BASE_S + 4, 3), :], 0.0)
    d = d_s[...]
    east = lambda a: pltpu.roll(a, WIDE - 1, 1)
    west = lambda a: pltpu.roll(a, 1, 1)
    north = lambda a: pltpu.roll(a, TALL - 1, 0)
    south = lambda a: pltpu.roll(a, 1, 0)
    d_e, d_n = east(d), north(d)
    w_e = jnp.where(jnp.logical_and(d > 0, d_e > 0), 0.5 * (d + d_e), 0.0)
    w_n = jnp.where(jnp.logical_and(d > 0, d_n > 0), 0.5 * (d + d_n), 0.0)
    w_w, w_s = west(w_e), south(w_n)
    diagonal = area_term + w_e + w_w + w_n + w_s

    def operate(h):
        return diagonal * h - w_e * east(h) - w_w * west(h) - w_n * north(h) - w_s * south(h)

    v0 = b_s[...]
    v1 = operate(v0)
    v2 = operate(v1)
    v3 = operate(v2)
    v = [a[:BN, :BE] for a in (v0, v1, v2, v3)]
    for i in range(3):
        vectors[pl.ds(i * BN, BN), :] = v[i]
    pairs = ((0, 0), (0, 1), (1, 1), (1, 2), (2, 2), (2, 3))
    at = lax.broadcasted_iota(jnp.int32, (1, BE), 1)
    total = jnp.zeros((1, BE), F32)
    for i, (a, b) in enumerate(pairs):
        value = jnp.sum(jnp.sum(v[a] * v[b], axis=0, keepdims=True), axis=1, keepdims=True)
        total = jnp.where(at == i, value, total)
    for i in range(128):
        sums[i] = total


def krylov(plan, base, got):
    return pl.pallas_call(
        krylov_kernel,
        out_shape=(
            jax.ShapeDtypeStruct((3 * BN, BE), F32),
            jax.ShapeDtypeStruct((128, 1, BE), F32),
        ),
        in_specs=[SM, VM, VM],
        out_specs=(VM, VM),
        scratch_shapes=[pltpu.VMEM((TALL, WIDE), F32)] * 2,
        compiler_params=params(4),
        name="krylov",
    )(plan, base, got)


def combine_kernel(plan, sums, a0, a1, a2, a3, o0, o1, o2, o3):
    total = jnp.sum(sums[...], axis=0, keepdims=True)
    moment = [total[:, i:i + 1] for i in range(6)]

    def inner(a, b, lift):
        value = None
        for i in range(len(a)):
            for j in range(len(b)):
                term = a[i] * b[j] * moment[i + j + lift]
                value = term if value is None else value + term
        return value

    one = jnp.ones((1, 1), F32)
    zero = jnp.zeros((1, 1), F32)
    residual, direction = [one], [one]
    solution = [zero, zero, zero]
    rr = moment[0]
    for step in range(3):
        alpha = rr / inner(direction, direction, 1)
        for i, c in enumerate(direction):
            solution[i] = solution[i] + alpha * c
        if step < 2:
            image = [zero] + direction
            padded = residual + [zero]
            residual = [r - alpha * c for r, c in zip(padded, image)]
            following = inner(residual, residual, 0)
            beta = following / rr
            direction = [r + beta * c for r, c in zip(residual, direction + [zero])]
            rr = following
    solved = []
    for a in (a0, a1, a2, a3):
        v = [a[pl.ds(i * BN, BN), :] for i in range(3)]
        solved.append(solution[0] * v[0] + solution[1] * v[1] + solution[2] * v[2])
    for k, out in enumerate((o0, o1, o2, o3)):
        for b in range(2):
            shift = plan[TSEND + 2 * k + b]
            value = solved[3]
            for j in range(3):
                value = jnp.where(shift == j, solved[j], value)
            out[pl.ds(b * BN, BN), :] = value


def combine(plan, sums, arrays):
    return pl.pallas_call(
        combine_kernel,
        out_shape=(jax.ShapeDtypeStruct((2 * BN, BE), F32),) * 4,
        in_specs=[SM] + [VM] * 5,
        out_specs=(VM,) * 4,
        compiler_params=params(4),
        name="combine",
    )(plan, sums, *arrays)


def place_kernel(plan, a0, a1, a2, a3, out):
    for b in range(2):
        shift = plan[TFROM + b]
        value = chosen(shift, (a0, a1, a2, a3), b * BN, BN)
        out[b] = jnp.where(shift >= 0, value, 0.0)


def place(plan, arrays):
    return pl.pallas_call(
        place_kernel,
        out_shape=jax.ShapeDtypeStruct((2, BN, BE), F32),
        in_specs=[SM] + [VM] * 4,
        out_specs=VM,
        compiler_params=params(4),
        name="place",
    )(plan, *arrays)


def body(tracers, velocity, mixing_rate, column_depth, ocean_mask, clinic_list, tropic_list):
    side = SIDE
    depth = column_depth.reshape(BN, BE)
    every = lambda value: lax.all_to_all(value, EVERY, 0, 0)

    def along_y(value, k):
        return lax.ppermute(value, "y", [(y, (y + k) % side) for y in range(side)])

    def along_z(value, k):
        return lax.ppermute(value, "z", [(z, (z + k) % side) for z in range(side)])

    in_hbm = lambda value: pltpu.with_memory_space_constraint(value, pltpu.HBM)
    tracers = in_hbm(tracers.reshape(4 * CELLS, BE))
    velocity = in_hbm(velocity.reshape(2 * CELLS, BE))
    mixing = in_hbm(mixing_rate.reshape((LEV - 1) * BN, BE))
    depth = in_hbm(depth)
    own = pack(tracers, velocity, depth)
    in_vmem = lambda value: pltpu.with_memory_space_constraint(value, pltpu.VMEM)
    plan = pl.pallas_call(
        functools.partial(make_plan, SIDE, N_GY, N_GX),
        out_shape=jax.ShapeDtypeStruct((PLAN,), jnp.int32),
        in_specs=[SM, SM],
        out_specs=SM,
        scratch_shapes=[pltpu.SMEM(((N_GY + 2) * WRAP,), jnp.int32)],
        compiler_params=params(1),
        name="plan",
    )(clinic_list, tropic_list)
    first_two, inv = stencil(0, (tracers, velocity, mixing))
    first_two, inv = in_vmem(first_two), in_hbm(inv)
    scattered = every(own.reshape(128, PART, BE))
    halo = every(select(plan, scattered)).reshape(ITEM, BE)
    mixed, edge, base, items = solve(0, (plan, first_two, inv, mixing, in_hbm(own), halo, depth))
    got = every(items)
    edge = in_hbm(edge)
    last_two, new = stencil(1, (tracers, velocity, in_vmem(mixed)))
    got, last_two = lax.optimization_barrier((got, last_two))
    vectors, sums = krylov(plan, in_vmem(base), got)
    totals = every(sums)
    _, new = solve(1, (in_vmem(last_two), inv, mixing, edge, in_hbm(new)))
    totals, new = lax.optimization_barrier((totals, new))
    line = [vectors] + [along_y(vectors, k) for k in range(1, side)]
    sends = combine(plan, totals.reshape(128, BE), line)
    arrived = [sends[0]] + [along_z(sends[k], k) for k in range(1, side)]
    height = place(plan, arrived)
    return new.reshape(1, 1, 4, LEV, BN, BE), height[None]


def solution(mesh):
    mesh = Mesh(mesh.devices.reshape(*(SIZES[axis] for axis in "zyxc")), tuple("zyxc"))
    gx, gy = ("z", "y"), ("x", "c")
    return jax.shard_map(
        body,
        mesh=mesh,
        in_specs=(P(gy, gx), P(gy, gx), P(gy, gx), P(gy, gx), P(), P(), P()),
        out_specs=(P(gy, gx), P(gy, gx)),
        check_vma=False,
    )
```

```python
import functools
import jax
import jax.numpy as jnp
from jax import lax
from jax.experimental import pallas as pl
from jax.experimental.pallas import tpu as pltpu
from jax.sharding import Mesh, PartitionSpec as P

F32 = jnp.float32
LEV, BN, BE = 36, 64, 128
NBX = 28
N_GX, N_GY, SIDE = 16, 8, 4
SIZES = {"z": 4, "y": 4, "x": 4, "c": 2}
EVERY = ('c', 'z', 'x', 'y')
CELLS = LEV * BN
HALF = BE // 2

NORTH = 0
NORTH_Q = (0, LEV, 3 * LEV, 4 * LEV)
NORTH_V = 2 * LEV
NORTH_D = 5 * LEV
SOUTH = 184
SOUTH_Q = tuple(SOUTH + f * LEV for f in range(4))
SOUTH_D = SOUTH + 4 * LEV
EAST = 332
WEST = 440
ITEM = 512
PART = 4

diffusion = 0.12
area_term = 0.1
thermal = 0.2
haline = 0.25
cabbeling = 0.05
forcing = 4.0

NBR = 0
TFROM = 8
TSEND = 10
RELAY = 18
PLAN = RELAY + 128
WRAP = NBX + 4

DIRS = ((0, 1), (0, -1), (1, 0), (-1, 0), (1, 1), (1, -1), (-1, 1), (-1, -1))


def params(mib, **more):
    return pltpu.CompilerParams(vmem_limit_bytes=mib * 1024 * 1024, **more)


VM = pl.BlockSpec(memory_space=pltpu.VMEM)
SM = pl.BlockSpec(memory_space=pltpu.SMEM)
ANY = pl.BlockSpec(memory_space=pl.ANY)
HBM = pl.BlockSpec(memory_space=pltpu.HBM)


def shaped(*shape):
    return jax.ShapeDtypeStruct(shape, F32)


def place_of(axis, slot, row):
    return {"z": slot // SIDE, "y": slot % SIDE, "x": row // 2, "c": row % 2}[axis]


def device_of(slot, row):
    index = 0
    for axis in EVERY:
        index = index * SIZES[axis] + place_of(axis, slot, row)
    return index


def slot_of(device):
    stride, at = 1, {}
    for axis in reversed(EVERY):
        at[axis] = lax.rem(device // stride, SIZES[axis])
        stride *= SIZES[axis]
    return at["z"] * SIDE + at["y"]


def make_plan(side, n_gy, slots, clinic, tropic, out, pos):
    z, y = lax.axis_index("z"), lax.axis_index("y")
    gx = z * side + y
    gy = lax.axis_index("x") * 2 + lax.axis_index("c")

    def clear(i, carry):
        pos[i] = jnp.int32(-1)
        return carry

    lax.fori_loop(0, (n_gy + 2) * WRAP, clear, 0, unroll=16)
    for row in range(n_gy):
        for slot in range(slots):
            pos[(row + 1) * WRAP + 1 + clinic[row, slot]] = jnp.int32(device_of(slot, row))
    for row in range(1, n_gy + 1):
        pos[row * WRAP] = pos[row * WRAP + NBX]
        pos[row * WRAP + NBX + 1] = pos[row * WRAP + 1]
    centre = (gy + 1) * WRAP + 1 + clinic[gy, gx]
    for d, (dr, dc) in enumerate(DIRS):
        out[NBR + d] = pos[centre + (dr * WRAP + dc)]
    me = jnp.int32(0)
    for axis in EVERY:
        me = me * SIZES[axis] + lax.axis_index(axis)
    kind_s, kind_n, kind_w = me < SOUTH // PART, me < EAST // PART, me < WEST // PART
    move = jnp.where(kind_s, jnp.int32(-WRAP), jnp.where(kind_n, jnp.int32(WRAP), jnp.where(
        kind_w, jnp.int32(-1), jnp.int32(1))))
    for row in range(n_gy):
        for there in range(slots):
            source = pos[(row + 1) * WRAP + 1 + clinic[row, there] + move]
            out[RELAY + device_of(there, row)] = jnp.maximum(source, 0)

    def owner(there, b):
        column_b = tropic[gy, 2 * there + b]
        device = pos[(gy + 1) * WRAP + 1 + jnp.maximum(column_b, 0)]
        return jnp.where(column_b < 0, jnp.int32(-1), slot_of(device))

    for k in range(side):
        there = lax.rem(z + k, side) * side + y
        for b in range(2):
            slot = owner(there, b)
            shift = lax.rem(y - lax.rem(slot, side) + side, side)
            out[TSEND + 2 * k + b] = jnp.where(slot < 0, jnp.int32(0), shift)
    for b in range(2):
        slot = owner(gx, b)
        shift = lax.rem(z - slot // side + side, side)
        out[TFROM + b] = jnp.where(slot < 0, jnp.int32(-1), shift)


def pack_kernel(tracers, velocity, depth_in, item, q, vel, turn, own, depth, sems):
    order = (0, 2, 4, 1, 3, 5)
    copies = {}
    fetch_depth = pltpu.make_async_copy(depth_in, depth, sems.at[6])
    fetch_depth.start()
    for f in order:
        source, at = (tracers, f) if f < 4 else (velocity, f - 4)
        target = q if f < 4 else vel
        span = pl.ds(at * CELLS, CELLS)
        copies[f] = pltpu.make_async_copy(source.at[span], target.at[span], sems.at[f])
        copies[f].start()
    fetch_depth.wait()
    lane = lax.broadcasted_iota(jnp.int32, (BN, BE), 1)
    level = lane // 2
    own[pl.ds(NORTH_D, 3), :] = depth[pl.ds(BN - 3, 3), :]
    own[pl.ds(NORTH_D + 3, 1), :] = jnp.zeros((1, BE), F32)
    own[pl.ds(SOUTH_D, 3), :] = depth[pl.ds(0, 3), :]
    own[pl.ds(SOUTH_D + 3, 1), :] = jnp.zeros((1, BE), F32)

    def columns(f):
        copies[f].wait()
        sides = jnp.zeros((BN, BE), F32)
        for k in range(LEV):
            tile = q[pl.ds(f * CELLS + k * BN, BN), :]
            sides = jnp.where(level == k, pltpu.roll(tile, 2 * k + 1, 1), sides)
        own[pl.ds(NORTH_Q[f], LEV), :] = q[pl.ds(f * CELLS + BN - 1, LEV, stride=BN), :]
        own[pl.ds(SOUTH_Q[f], LEV), :] = q[pl.ds(f * CELLS, LEV, stride=BN), :]
        return sides

    for j in range(2):
        first, second = columns(j), columns(2 + j)
        if j == 0:
            copies[4].wait()
            for k in range(LEV):
                tile = vel[pl.ds(k * BN, BN), :]
                first = jnp.where(lane == 2 * LEV + k, pltpu.roll(tile, 2 * LEV + 1 + k, 1), first)
        if j == 1:
            copies[5].wait()
            own[pl.ds(NORTH_V, LEV), :] = vel[pl.ds(CELLS + BN - 1, LEV, stride=BN), :]
            rows_out = pltpu.make_async_copy(own.at[pl.ds(0, 328)], item.at[pl.ds(0, 328)], sems.at[7])
            rows_out.start()
        turn[...] = jnp.concatenate([first, second], axis=0).T
        own[pl.ds(EAST + j * LEV, LEV), :] = turn[pl.ds(0, LEV, stride=2), :]
        own[pl.ds(WEST + j * LEV, LEV), :] = turn[pl.ds(1, LEV, stride=2), :]
        if j == 0:
            own[pl.ds(EAST + 2 * LEV, LEV), :] = turn[pl.ds(2 * LEV, LEV), :]
    rest = pl.ds(328, ITEM - 328)
    rest_out = pltpu.make_async_copy(own.at[rest], item.at[rest], sems.at[8])
    rest_out.start()
    rows_out.wait()
    rest_out.wait()


def pack(tracers, velocity, depth):
    return pl.pallas_call(
        pack_kernel,
        out_shape=pltpu.HBM((ITEM, BE), F32),
        in_specs=[HBM, HBM, HBM],
        out_specs=HBM,
        scratch_shapes=[
            pltpu.VMEM((4 * CELLS, BE), F32),
            pltpu.VMEM((2 * CELLS, BE), F32),
            pltpu.VMEM((BE, BE), F32),
            pltpu.VMEM((ITEM, BE), F32),
            pltpu.VMEM((BN, BE), F32),
            pltpu.SemaphoreType.DMA((9,)),
        ],
        compiler_params=params(12),
        name="pack",
    )(tracers, velocity, depth)


def select_kernel(plan, got, out, chosen_parts, sems):
    def one(d, carry):
        chosen_parts[d] = got[plan[RELAY + d]]
        return carry

    copies = []
    for half in range(2):
        lax.fori_loop(64 * half, 64 * half + 64, one, 0, unroll=16)
        span = pl.ds(64 * half, 64)
        copies.append(pltpu.make_async_copy(chosen_parts.at[span], out.at[span], sems.at[half]))
        copies[-1].start()
    for copy in copies:
        copy.wait()


def select(plan, got):
    return pl.pallas_call(
        select_kernel,
        out_shape=pltpu.HBM((128, PART, BE), F32),
        in_specs=[SM, VM],
        out_specs=HBM,
        scratch_shapes=[pltpu.VMEM((128, PART, BE), F32), pltpu.SemaphoreType.DMA((2,))],
        compiler_params=params(2),
        name="select",
    )(plan, got)


def stencil_loads(fields, chunk, tracers, velocity, mixing, q, u, v, mix, sems):
    parts = LEV // chunk
    rows = chunk * BN
    copies = []
    for c in range(parts):
        row = []
        for i, f in enumerate(fields):
            row.append(pltpu.make_async_copy(
                tracers.at[pl.ds(f * CELLS + c * rows, rows)], q[i].at[pl.ds(8 + c * rows, rows)],
                sems.at[c, i]))
        row.append(pltpu.make_async_copy(
            velocity.at[pl.ds(CELLS + c * rows, rows)], v.at[pl.ds(8 + c * rows, rows)], sems.at[c, 2]))
        row.append(pltpu.make_async_copy(
            velocity.at[pl.ds(c * rows, rows)], u.at[pl.ds(c * rows, rows)], sems.at[c, 3]))
        if mixing is not None:
            size = rows if c + 1 < parts else rows - BN
            row.append(pltpu.make_async_copy(
                mixing.at[pl.ds(c * rows, size)], mix.at[pl.ds(c * rows, size)], sems.at[c, 4]))
        copies.append(row)
    pad = jnp.zeros((8, BE), F32)
    for ref in (*q, v):
        ref[pl.ds(0, 8), :] = pad
        ref[pl.ds(8 + CELLS, 8), :] = pad
    return copies


def stencil_level(k, q, u, v, s):
    lane = lax.broadcasted_iota(jnp.int32, (BN, BE), 1)
    row_id = lax.broadcasted_iota(jnp.int32, (BN, BE), 0)
    at = pl.multiple_of(k * BN, BN)
    here, north, south = pl.ds(at + 8, BN), pl.ds(at + 9, BN), pl.ds(at + 7, BN)
    half_u = 0.5 * u[pl.ds(at, BN), :]
    ua = jnp.where(lane == BE - 1, 0.0, half_u + diffusion)
    ub = jnp.where(lane == BE - 1, 0.0, half_u - diffusion)
    half_v, half_s = 0.5 * v[here, :], 0.5 * v[south, :]
    va = jnp.where(row_id == BN - 1, 0.0, half_v + diffusion)
    vb = jnp.where(row_id == BN - 1, 0.0, half_v - diffusion)
    vas = jnp.where(row_id == 0, 0.0, half_s + diffusion)
    vbs = jnp.where(row_id == 0, 0.0, half_s - diffusion)
    centre = 1.0 - (va - vbs)
    for f in range(2):
        tile = q[f][here, :]
        fe = ua * tile + ub * pltpu.roll(tile, BE - 1, 1)
        s[pl.ds(pl.multiple_of(f * CELLS + at, BN), BN), :] = (
            centre * tile - (fe - pltpu.roll(fe, 1, 1))
            - vb * q[f][north, :] + vas * q[f][south, :])


AHEAD = 6


def begin(copies, c):
    for copy in copies[c] if c < len(copies) else ():
        copy.start()


def arrived(copies, c, beyond=0):
    for d in range(1 + beyond) if c == 0 else (c + beyond,):
        for copy in copies[d] if d < len(copies) else ():
            copy.wait()
    begin(copies, c + AHEAD)


def stencil_kernel(group, chunk, *refs):
    parts = LEV // chunk
    rows = chunk * BN
    if group == 0:
        tracers, velocity, mixing, s, inv_out, q0, q1, u, v, inv, mix, sems, out_sems = refs
    else:
        tracers, velocity, _aliased, s, new, q0, q1, u, v, sems, out_sems = refs
        mixing = mix = None
        leave = pltpu.make_async_copy(s, new.at[pl.ds(0, 2 * CELLS)], out_sems.at[0, 0])
        leave.start()
    q = (q0, q1)
    copies = stencil_loads((2 * group, 2 * group + 1), chunk, tracers, velocity, mixing, q, u, v, mix, sems)
    for c in range(AHEAD):
        begin(copies, c)
    zero = jnp.zeros((BN, BE), F32)
    if group == 0:
        mix[pl.ds(CELLS - BN, BN), :] = zero
    else:
        leave.wait()

    def level(k, carry):
        stencil_level(k, q, u, v, s)
        if group == 1:
            return carry
        m_up, fac_up = carry
        span = pl.ds(pl.multiple_of(k * BN, BN), BN)
        m = mix[span, :]
        inverse = 1.0 / (1.0 + m_up + m - m_up * fac_up)
        inv[span, :] = inverse
        return m, m * inverse

    carry = (zero, zero) if group == 0 else 0
    outs = []
    for c in range(parts):
        arrived(copies, c, 1)
        carry = lax.fori_loop(c * chunk, (c + 1) * chunk, level, carry, unroll=2)
        if group == 0:
            span = pl.ds(c * rows, rows)
            outs.append(pltpu.make_async_copy(inv.at[span], inv_out.at[span], out_sems.at[c, 0]))
            outs[-1].start()
    for copy in outs:
        copy.wait()


def cells(extra=0, fields=1):
    return pltpu.VMEM((fields * CELLS + extra, BE), F32)


def stencil(group, args, chunk=6):
    parts = LEV // chunk
    if group == 0:
        outs, out_specs = (cells(0, 2), pltpu.HBM((CELLS, BE), F32)), (VM, HBM)
        more = [cells(), cells()]
    else:
        outs, out_specs = (cells(0, 2), pltpu.HBM((4 * CELLS, BE), F32)), (VM, HBM)
        more = []
    return pl.pallas_call(
        functools.partial(stencil_kernel, group, chunk),
        out_shape=outs,
        in_specs=[HBM] * 3 if group == 0 else [HBM, HBM, VM],
        out_specs=out_specs,
        input_output_aliases={} if group == 0 else {2: 0},
        scratch_shapes=[
            cells(16), cells(16), cells(), cells(16), *more,
            pltpu.SemaphoreType.DMA((parts, 5)),
            pltpu.SemaphoreType.DMA((parts, 2)),
        ],
        compiler_params=params(10),
        name=f"stencil{group}",
    )(*args)


EDGE_N, EDGE_S, EDGE = BN, BN + 40, BN + 80
BASE_D, BASE_S, BASE_N, BASE = BN, 2 * BN, 2 * BN + 8, 2 * BN + 16


def flux(speed, low, high):
    return speed * (0.5 * (low + high)) - diffusion * (high - low)


def edges(plan, own, halo, out, turn):
    lane = lax.broadcasted_iota(jnp.int32, (LEV, BE), 1)
    open_e, open_w, open_n, open_s = (plan[NBR + d] >= 0 for d in range(4))
    row = lambda ref, at: ref[pl.ds(at, LEV), :]
    v_own, v_south = row(own, NORTH_V), row(halo, NORTH_V)
    for f in range(4):
        fn = flux(v_own, row(own, NORTH_Q[f]), row(halo, SOUTH_Q[f]))
        fs = flux(v_south, row(halo, NORTH_Q[f]), row(own, SOUTH_Q[f]))
        out[pl.ds(f * EDGE + EDGE_N, LEV), :] = jnp.where(open_n, -fn, 0.0)
        out[pl.ds(f * EDGE + EDGE_S, LEV), :] = jnp.where(open_s, fs, 0.0)

    def both(speed):
        return jnp.where(lane < HALF, speed, pltpu.roll(speed, HALF, 1))

    u_own, u_west = both(row(own, EAST + 2 * LEV)), both(row(halo, EAST + 2 * LEV))
    for j in range(2):
        fe = flux(u_own, row(own, EAST + j * LEV), row(halo, WEST + j * LEV))
        fw = flux(u_west, row(halo, EAST + j * LEV), row(own, WEST + j * LEV))
        turn[...] = jnp.zeros((BE, BE), F32)
        turn[pl.ds(0, LEV, stride=2), :] = jnp.where(open_e, -fe, 0.0)
        turn[pl.ds(1, LEV, stride=2), :] = jnp.where(open_w, fw, 0.0)
        turned = turn[...].T
        out[pl.ds(j * EDGE, BN), :] = turned[:BN]
        out[pl.ds((2 + j) * EDGE, BN), :] = turned[BN:]


def solve_kernel(group, chunk, out_chunk, *refs):
    parts = LEV // chunk
    rows = chunk * BN
    outs = []
    if group == 0:
        (plan, _aliased, inv_in, mixing, own_in, halo, depth_in,
         s, edge_out, base, items, inv, mix, edge, turn, parts_out, own, depth,
         sems, side_sems) = refs
        sides = [pltpu.make_async_copy(a, b, side_sems.at[i]) for i, (a, b) in enumerate(
            ((own_in, own), (depth_in, depth)))]
    else:
        (_stirred, inv_in, mixing, edge_in, _new,
         s, new, inv, mix, edge, sems, out_sems, side_sems) = refs
        sides = [pltpu.make_async_copy(edge_in, edge, side_sems.at[0])]
    for copy in sides:
        copy.start()
    first = 2 * group
    copies = []
    for c in range(parts):
        row = []
        span = pl.ds(c * rows, rows)
        row.append(pltpu.make_async_copy(inv_in.at[span], inv.at[span], sems.at[c, 2]))
        span = pl.ds(c * rows, rows if c + 1 < parts else rows - BN)
        row.append(pltpu.make_async_copy(mixing.at[span], mix.at[span], sems.at[c, 3]))
        copies.append(row)
        begin(copies, c)
    for copy in sides:
        copy.wait()
    if group == 0:
        edges(plan, own, halo, edge, turn)
        base[pl.ds(BASE_D, BN), :] = depth[...]
        base[pl.ds(BASE_S, 8), :] = halo[pl.ds(NORTH_D - 4, 8), :]
        base[pl.ds(BASE_N, 8), :] = halo[pl.ds(SOUTH_D, 8), :]
        outs.append(pltpu.make_async_copy(edge, edge_out, side_sems.at[3]))
        outs[-1].start()
    lane = lax.broadcasted_iota(jnp.int32, (BN, BE), 1)
    rim = jnp.logical_or(lane == 0, lane == BE - 1)
    sub = lax.broadcasted_iota(jnp.int32, (8, BE), 0)
    tile = lambda f, k: pl.ds(f * CELLS + k * BN, BN)
    m_up, sol_up = None, [None, None]
    columns = [edge[pl.ds((first + f) * EDGE, BN), :] for f in range(2)]

    for c in range(parts):
        for copy in copies[c]:
            copy.wait()
        for k in range(c * chunk, (c + 1) * chunk):
            inverse = inv[tile(0, k), :]
            for f in range(2):
                value = s[tile(f, k), :] + jnp.where(
                    rim, pltpu.roll(columns[f], BE - 1 - 2 * k, 1), 0.0)
                row = (first + f) * EDGE + k
                value = jnp.concatenate([
                    value[:8] + jnp.where(sub == 0, edge[pl.ds(row + EDGE_S, 1), :], 0.0),
                    value[8:BN - 8],
                    value[BN - 8:] + jnp.where(sub == 7, edge[pl.ds(row + EDGE_N, 1), :], 0.0),
                ], axis=0)
                if k:
                    value = value + m_up * sol_up[f]
                sol_up[f] = value * inverse
                s[tile(f, k), :] = sol_up[f]
            m_up = mix[tile(0, k), :] if k + 1 < LEV else None
    heat, salt = sol_up
    total = None
    for k in range(LEV - 1, -1, -1):
        if k + 1 < LEV:
            factor = mix[tile(0, k), :] * inv[tile(0, k), :]
            heat = s[tile(0, k), :] + factor * heat
            salt = s[tile(1, k), :] + factor * salt
            s[tile(0, k), :] = heat
            s[tile(1, k), :] = salt
        if group == 0:
            weight = forcing * 2.0 * (k + 1) / (LEV * (LEV + 1))
            density = (haline * weight) * salt - heat * (thermal * weight + (cabbeling * weight) * heat)
            total = density if total is None else total + density
        if group == 1 and k % out_chunk == 0:
            for f in range(2):
                outs.append(pltpu.make_async_copy(
                    s.at[pl.ds(f * CELLS + k * BN, out_chunk * BN)],
                    new.at[pl.ds((first + f) * CELLS + k * BN, out_chunk * BN)],
                    out_sems.at[k // out_chunk, f]))
                outs[-1].start()
    if group == 0:
        field = total
        base[pl.ds(0, BN), :] = field
        turned = jnp.concatenate([field, depth[...]], axis=0).T
        east_item, west_item = turned[BE - 3:, :], turned[:3, :]
        sends = (east_item, west_item, field[BN - 3:, :], field[:3, :],
                 east_item, west_item, east_item, west_item)
        for d, item in enumerate(sends):
            to = plan[NBR + d]

            @pl.when(to >= 0)
            def _(to=to, item=item):
                parts_out[to, pl.ds(0, 3), :] = item

        outs.append(pltpu.make_async_copy(parts_out, items, side_sems.at[5]))
        outs[-1].start()
    for copy in outs:
        copy.wait()


def solve(group, args, chunk=12, out_chunk=6):
    edge_rows = 4 * EDGE
    block = lambda rows: pltpu.VMEM((rows, BE), F32)
    if group == 0:
        in_specs = [SM, VM, HBM, HBM, HBM, VM, HBM]
        outs = [cells(0, 2), pltpu.HBM((edge_rows, BE), F32), block(BASE),
                pltpu.HBM((128, PART, BE), F32)]
        out_specs = [VM, HBM, VM, HBM]
        scratch = [cells(), cells(), block(edge_rows), block(BE), pltpu.VMEM((128, PART, BE), F32),
                   block(ITEM), block(BN)]
    else:
        in_specs = [VM] + [HBM] * 4
        outs, out_specs = [cells(0, 2), pltpu.HBM((4 * CELLS, BE), F32)], [VM, HBM]
        scratch = [cells(), cells(), block(edge_rows)]
    scratch += [pltpu.SemaphoreType.DMA((LEV // chunk, 4))]
    if group == 1:
        scratch += [pltpu.SemaphoreType.DMA((LEV // out_chunk, 2))]
    scratch += [pltpu.SemaphoreType.DMA((6,))]
    return pl.pallas_call(
        functools.partial(solve_kernel, group, chunk, out_chunk),
        out_shape=tuple(outs),
        in_specs=in_specs,
        out_specs=tuple(out_specs),
        scratch_shapes=scratch,
        input_output_aliases={1: 0} if group == 0 else {0: 0, 4: 1},
        compiler_params=params(8),
        name=f"solve{group}",
    )(*args)


def chosen(shift, arrays, start, rows):
    value = arrays[-1][pl.ds(start, rows), :]
    for k in range(len(arrays) - 1):
        value = jnp.where(shift == k, arrays[k][pl.ds(start, rows), :], value)
    return value


TALL, WIDE = BN + 8, 2 * BE


def krylov_kernel(plan, base, got, vectors, sums, b_s, d_s):
    nothing = jnp.zeros((3, BE), F32)

    def item(d):
        to = plan[NBR + d]
        return jnp.where(to >= 0, got[jnp.maximum(to, 0), pl.ds(0, 3), :], nothing)

    for ref in (b_s, d_s):
        ref[pl.ds(BN, 8), :] = jnp.zeros((8, WIDE), F32)
    b_s[pl.ds(0, BN), pl.ds(0, BE)] = base[pl.ds(0, BN), :]
    d_s[pl.ds(0, BN), pl.ds(0, BE)] = base[pl.ds(BASE_D, BN), :]
    b_s[pl.ds(BN, 3), pl.ds(0, BE)] = item(2)
    b_s[pl.ds(TALL - 3, 3), pl.ds(0, BE)] = item(3)
    middle = jnp.zeros((BE - 6, BE), F32)
    sides = jnp.concatenate([item(0), middle, item(1)], axis=0).T
    b_s[pl.ds(0, BN), pl.ds(BE, BE)] = sides[:BN]
    d_s[pl.ds(0, BN), pl.ds(BE, BE)] = sides[BN:]
    place = lax.broadcasted_iota(jnp.int32, (3, BE), 1)
    place = jnp.where(place >= BN, place - BN, place)

    def corner(north, south):
        return jnp.where(place < 3, north, jnp.where(
            jnp.logical_and(place >= 5, place < 8), pltpu.roll(south, BE - BN + 8, 1), 0.0))

    corners = jnp.concatenate([corner(item(4), item(6)), middle, corner(item(5), item(7))], axis=0).T
    b_s[pl.ds(BN, 8), pl.ds(BE, BE)] = corners[:8]
    d_s[pl.ds(BN, 8), pl.ds(BE, BE)] = corners[BN:BN + 8]

    d_s[pl.ds(BN, 3), pl.ds(0, BE)] = jnp.where(
        plan[NBR + 2] >= 0, base[pl.ds(BASE_N, 3), :], 0.0)
    d_s[pl.ds(TALL - 3, 3), pl.ds(0, BE)] = jnp.where(
        plan[NBR + 3] >= 0, base[pl.ds(BASE_S + 4, 3), :], 0.0)
    d = d_s[...]
    east = lambda a: pltpu.roll(a, WIDE - 1, 1)
    west = lambda a: pltpu.roll(a, 1, 1)
    north = lambda a: pltpu.roll(a, TALL - 1, 0)
    south = lambda a: pltpu.roll(a, 1, 0)
    d_e, d_n = east(d), north(d)
    w_e = jnp.where(jnp.logical_and(d > 0, d_e > 0), 0.5 * (d + d_e), 0.0)
    w_n = jnp.where(jnp.logical_and(d > 0, d_n > 0), 0.5 * (d + d_n), 0.0)
    w_w, w_s = west(w_e), south(w_n)
    diagonal = area_term + w_e + w_w + w_n + w_s

    def operate(h):
        return diagonal * h - w_e * east(h) - w_w * west(h) - w_n * north(h) - w_s * south(h)

    v0 = b_s[...]
    v1 = operate(v0)
    v2 = operate(v1)
    v3 = operate(v2)
    v = [a[:BN, :BE] for a in (v0, v1, v2, v3)]
    for i in range(3):
        vectors[pl.ds(i * BN, BN), :] = v[i]
    pairs = ((0, 0), (0, 1), (1, 1), (1, 2), (2, 2), (2, 3))
    at = lax.broadcasted_iota(jnp.int32, (1, BE), 1)
    total = jnp.zeros((1, BE), F32)
    for i, (a, b) in enumerate(pairs):
        value = jnp.sum(jnp.sum(v[a] * v[b], axis=0, keepdims=True), axis=1, keepdims=True)
        total = jnp.where(at == i, value, total)
    for i in range(128):
        sums[i] = total


def krylov(plan, base, got):
    return pl.pallas_call(
        krylov_kernel,
        out_shape=(
            jax.ShapeDtypeStruct((3 * BN, BE), F32),
            jax.ShapeDtypeStruct((128, 1, BE), F32),
        ),
        in_specs=[SM, VM, VM],
        out_specs=(VM, VM),
        scratch_shapes=[pltpu.VMEM((TALL, WIDE), F32)] * 2,
        compiler_params=params(4),
        name="krylov",
    )(plan, base, got)


def combine_kernel(plan, sums, a0, a1, a2, a3, o0, o1, o2, o3):
    total = jnp.sum(sums[...], axis=0, keepdims=True)
    moment = [total[:, i:i + 1] for i in range(6)]

    def inner(a, b, lift):
        value = None
        for i in range(len(a)):
            for j in range(len(b)):
                term = a[i] * b[j] * moment[i + j + lift]
                value = term if value is None else value + term
        return value

    one = jnp.ones((1, 1), F32)
    zero = jnp.zeros((1, 1), F32)
    residual, direction = [one], [one]
    solution = [zero, zero, zero]
    rr = moment[0]
    for step in range(3):
        alpha = rr / inner(direction, direction, 1)
        for i, c in enumerate(direction):
            solution[i] = solution[i] + alpha * c
        if step < 2:
            image = [zero] + direction
            padded = residual + [zero]
            residual = [r - alpha * c for r, c in zip(padded, image)]
            following = inner(residual, residual, 0)
            beta = following / rr
            direction = [r + beta * c for r, c in zip(residual, direction + [zero])]
            rr = following
    solved = []
    for a in (a0, a1, a2, a3):
        v = [a[pl.ds(i * BN, BN), :] for i in range(3)]
        solved.append(solution[0] * v[0] + solution[1] * v[1] + solution[2] * v[2])
    for k, out in enumerate((o0, o1, o2, o3)):
        for b in range(2):
            shift = plan[TSEND + 2 * k + b]
            value = solved[3]
            for j in range(3):
                value = jnp.where(shift == j, solved[j], value)
            out[pl.ds(b * BN, BN), :] = value


def combine(plan, sums, arrays):
    return pl.pallas_call(
        combine_kernel,
        out_shape=(jax.ShapeDtypeStruct((2 * BN, BE), F32),) * 4,
        in_specs=[SM] + [VM] * 5,
        out_specs=(VM,) * 4,
        compiler_params=params(4),
        name="combine",
    )(plan, sums, *arrays)


def place_kernel(plan, a0, a1, a2, a3, out):
    for b in range(2):
        shift = plan[TFROM + b]
        value = chosen(shift, (a0, a1, a2, a3), b * BN, BN)
        out[b] = jnp.where(shift >= 0, value, 0.0)


def place(plan, arrays):
    return pl.pallas_call(
        place_kernel,
        out_shape=jax.ShapeDtypeStruct((2, BN, BE), F32),
        in_specs=[SM] + [VM] * 4,
        out_specs=VM,
        compiler_params=params(4),
        name="place",
    )(plan, *arrays)


def body(tracers, velocity, mixing_rate, column_depth, ocean_mask, clinic_list, tropic_list):
    side = SIDE
    depth = column_depth.reshape(BN, BE)
    every = lambda value: lax.all_to_all(value, EVERY, 0, 0)

    def along_y(value, k):
        return lax.ppermute(value, "y", [(y, (y + k) % side) for y in range(side)])

    def along_z(value, k):
        return lax.ppermute(value, "z", [(z, (z + k) % side) for z in range(side)])

    in_hbm = lambda value: pltpu.with_memory_space_constraint(value, pltpu.HBM)
    tracers = in_hbm(tracers.reshape(4 * CELLS, BE))
    velocity = in_hbm(velocity.reshape(2 * CELLS, BE))
    mixing = in_hbm(mixing_rate.reshape((LEV - 1) * BN, BE))
    depth = in_hbm(depth)
    own = pack(tracers, velocity, depth)
    in_vmem = lambda value: pltpu.with_memory_space_constraint(value, pltpu.VMEM)
    plan = pl.pallas_call(
        functools.partial(make_plan, SIDE, N_GY, N_GX),
        out_shape=jax.ShapeDtypeStruct((PLAN,), jnp.int32),
        in_specs=[SM, SM],
        out_specs=SM,
        scratch_shapes=[pltpu.SMEM(((N_GY + 2) * WRAP,), jnp.int32)],
        compiler_params=params(1),
        name="plan",
    )(clinic_list, tropic_list)
    first_two, inv = stencil(0, (tracers, velocity, mixing))
    first_two, inv = in_vmem(first_two), in_hbm(inv)
    scattered = every(own.reshape(128, PART, BE))
    halo = every(select(plan, scattered)).reshape(ITEM, BE)
    mixed, edge, base, items = solve(0, (plan, first_two, inv, mixing, in_hbm(own), halo, depth), chunk=36)
    got = every(items)
    edge = in_hbm(edge)
    last_two, new = stencil(1, (tracers, velocity, in_vmem(mixed)))
    got, last_two = lax.optimization_barrier((got, last_two))
    vectors, sums = krylov(plan, in_vmem(base), got)
    totals = every(sums)
    _, new = solve(1, (in_vmem(last_two), inv, mixing, edge, in_hbm(new)), chunk=18)
    totals, new = lax.optimization_barrier((totals, new))
    line = [vectors] + [along_y(vectors, k) for k in range(1, side)]
    sends = combine(plan, totals.reshape(128, BE), line)
    arrived = [sends[0]] + [along_z(sends[k], k) for k in range(1, side)]
    height = place(plan, arrived)
    return new.reshape(1, 1, 4, LEV, BN, BE), height[None]


def solution(mesh):
    mesh = Mesh(mesh.devices.reshape(*(SIZES[axis] for axis in "zyxc")), tuple("zyxc"))
    gx, gy = ("z", "y"), ("x", "c")
    return jax.shard_map(
        body,
        mesh=mesh,
        in_specs=(P(gy, gx), P(gy, gx), P(gy, gx), P(gy, gx), P(), P(), P()),
        out_specs=(P(gy, gx), P(gy, gx)),
        check_vma=False,
    )
```

```python
import functools
import jax
import jax.numpy as jnp
from jax import lax
from jax.experimental import pallas as pl
from jax.experimental.pallas import tpu as pltpu
from jax.sharding import Mesh, PartitionSpec as P

F32 = jnp.float32
LEV, BN, BE = 36, 64, 128
NBX = 28
N_GX, N_GY, SIDE = 16, 8, 4
SIZES = {"z": 4, "y": 4, "x": 4, "c": 2}
EVERY = ('c', 'z', 'x', 'y')
CELLS = LEV * BN
HALF = BE // 2

NORTH = 0
NORTH_Q = (0, LEV, 3 * LEV, 4 * LEV)
NORTH_V = 2 * LEV
NORTH_D = 5 * LEV
SOUTH = 184
SOUTH_Q = tuple(SOUTH + f * LEV for f in range(4))
SOUTH_D = SOUTH + 4 * LEV
EAST = 332
WEST = 440
ITEM = 512
PART = 4

diffusion = 0.12
area_term = 0.1
thermal = 0.2
haline = 0.25
cabbeling = 0.05
forcing = 4.0

NBR = 0
TFROM = 8
TSEND = 10
RELAY = 18
PLAN = RELAY + 128
WRAP = NBX + 4

DIRS = ((0, 1), (0, -1), (1, 0), (-1, 0), (1, 1), (1, -1), (-1, 1), (-1, -1))


def params(mib, **more):
    return pltpu.CompilerParams(vmem_limit_bytes=mib * 1024 * 1024, **more)


VM = pl.BlockSpec(memory_space=pltpu.VMEM)
SM = pl.BlockSpec(memory_space=pltpu.SMEM)
ANY = pl.BlockSpec(memory_space=pl.ANY)
HBM = pl.BlockSpec(memory_space=pltpu.HBM)


def shaped(*shape):
    return jax.ShapeDtypeStruct(shape, F32)


def place_of(axis, slot, row):
    return {"z": slot // SIDE, "y": slot % SIDE, "x": row // 2, "c": row % 2}[axis]


def device_of(slot, row):
    index = 0
    for axis in EVERY:
        index = index * SIZES[axis] + place_of(axis, slot, row)
    return index


def slot_of(device):
    stride, at = 1, {}
    for axis in reversed(EVERY):
        at[axis] = lax.rem(device // stride, SIZES[axis])
        stride *= SIZES[axis]
    return at["z"] * SIDE + at["y"]


def make_plan(side, n_gy, slots, clinic, tropic, out, pos):
    z, y = lax.axis_index("z"), lax.axis_index("y")
    gx = z * side + y
    gy = lax.axis_index("x") * 2 + lax.axis_index("c")

    def clear(i, carry):
        pos[i] = jnp.int32(-1)
        return carry

    lax.fori_loop(0, (n_gy + 2) * WRAP, clear, 0, unroll=16)
    for row in range(n_gy):
        for slot in range(slots):
            pos[(row + 1) * WRAP + 1 + clinic[row, slot]] = jnp.int32(device_of(slot, row))
    for row in range(1, n_gy + 1):
        pos[row * WRAP] = pos[row * WRAP + NBX]
        pos[row * WRAP + NBX + 1] = pos[row * WRAP + 1]
    centre = (gy + 1) * WRAP + 1 + clinic[gy, gx]
    for d, (dr, dc) in enumerate(DIRS):
        out[NBR + d] = pos[centre + (dr * WRAP + dc)]
    me = jnp.int32(0)
    for axis in EVERY:
        me = me * SIZES[axis] + lax.axis_index(axis)
    kind_s, kind_n, kind_w = me < SOUTH // PART, me < EAST // PART, me < WEST // PART
    move = jnp.where(kind_s, jnp.int32(-WRAP), jnp.where(kind_n, jnp.int32(WRAP), jnp.where(
        kind_w, jnp.int32(-1), jnp.int32(1))))
    for row in range(n_gy):
        for there in range(slots):
            source = pos[(row + 1) * WRAP + 1 + clinic[row, there] + move]
            out[RELAY + device_of(there, row)] = jnp.maximum(source, 0)

    def owner(there, b):
        column_b = tropic[gy, 2 * there + b]
        device = pos[(gy + 1) * WRAP + 1 + jnp.maximum(column_b, 0)]
        return jnp.where(column_b < 0, jnp.int32(-1), slot_of(device))

    for k in range(side):
        there = lax.rem(z + k, side) * side + y
        for b in range(2):
            slot = owner(there, b)
            shift = lax.rem(y - lax.rem(slot, side) + side, side)
            out[TSEND + 2 * k + b] = jnp.where(slot < 0, jnp.int32(0), shift)
    for b in range(2):
        slot = owner(gx, b)
        shift = lax.rem(z - slot // side + side, side)
        out[TFROM + b] = jnp.where(slot < 0, jnp.int32(-1), shift)


def pack_kernel(tracers, velocity, depth_in, item, q, vel, turn, own, depth, sems):
    order = (0, 2, 4, 1, 3, 5)
    copies = {}
    fetch_depth = pltpu.make_async_copy(depth_in, depth, sems.at[6])
    fetch_depth.start()
    for f in order:
        source, at = (tracers, f) if f < 4 else (velocity, f - 4)
        target = q if f < 4 else vel
        span = pl.ds(at * CELLS, CELLS)
        copies[f] = pltpu.make_async_copy(source.at[span], target.at[span], sems.at[f])
        copies[f].start()
    fetch_depth.wait()
    lane = lax.broadcasted_iota(jnp.int32, (BN, BE), 1)
    level = lane // 2
    own[pl.ds(NORTH_D, 3), :] = depth[pl.ds(BN - 3, 3), :]
    own[pl.ds(NORTH_D + 3, 1), :] = jnp.zeros((1, BE), F32)
    own[pl.ds(SOUTH_D, 3), :] = depth[pl.ds(0, 3), :]
    own[pl.ds(SOUTH_D + 3, 1), :] = jnp.zeros((1, BE), F32)

    def columns(f):
        copies[f].wait()
        sides = jnp.zeros((BN, BE), F32)
        for k in range(LEV):
            tile = q[pl.ds(f * CELLS + k * BN, BN), :]
            sides = jnp.where(level == k, pltpu.roll(tile, 2 * k + 1, 1), sides)
        own[pl.ds(NORTH_Q[f], LEV), :] = q[pl.ds(f * CELLS + BN - 1, LEV, stride=BN), :]
        own[pl.ds(SOUTH_Q[f], LEV), :] = q[pl.ds(f * CELLS, LEV, stride=BN), :]
        return sides

    for j in range(2):
        first, second = columns(j), columns(2 + j)
        if j == 0:
            copies[4].wait()
            for k in range(LEV):
                tile = vel[pl.ds(k * BN, BN), :]
                first = jnp.where(lane == 2 * LEV + k, pltpu.roll(tile, 2 * LEV + 1 + k, 1), first)
        if j == 1:
            copies[5].wait()
            own[pl.ds(NORTH_V, LEV), :] = vel[pl.ds(CELLS + BN - 1, LEV, stride=BN), :]
            rows_out = pltpu.make_async_copy(own.at[pl.ds(0, 328)], item.at[pl.ds(0, 328)], sems.at[7])
            rows_out.start()
        turn[...] = jnp.concatenate([first, second], axis=0).T
        own[pl.ds(EAST + j * LEV, LEV), :] = turn[pl.ds(0, LEV, stride=2), :]
        own[pl.ds(WEST + j * LEV, LEV), :] = turn[pl.ds(1, LEV, stride=2), :]
        if j == 0:
            own[pl.ds(EAST + 2 * LEV, LEV), :] = turn[pl.ds(2 * LEV, LEV), :]
    rest = pl.ds(328, ITEM - 328)
    rest_out = pltpu.make_async_copy(own.at[rest], item.at[rest], sems.at[8])
    rest_out.start()
    rows_out.wait()
    rest_out.wait()


def pack(tracers, velocity, depth):
    return pl.pallas_call(
        pack_kernel,
        out_shape=pltpu.HBM((ITEM, BE), F32),
        in_specs=[HBM, HBM, HBM],
        out_specs=HBM,
        scratch_shapes=[
            pltpu.VMEM((4 * CELLS, BE), F32),
            pltpu.VMEM((2 * CELLS, BE), F32),
            pltpu.VMEM((BE, BE), F32),
            pltpu.VMEM((ITEM, BE), F32),
            pltpu.VMEM((BN, BE), F32),
            pltpu.SemaphoreType.DMA((9,)),
        ],
        compiler_params=params(12),
        name="pack",
    )(tracers, velocity, depth)


def select_kernel(plan, got, out, chosen_parts, sems):
    def one(d, carry):
        chosen_parts[d] = got[plan[RELAY + d]]
        return carry

    copies = []
    for half in range(2):
        lax.fori_loop(64 * half, 64 * half + 64, one, 0, unroll=16)
        span = pl.ds(64 * half, 64)
        copies.append(pltpu.make_async_copy(chosen_parts.at[span], out.at[span], sems.at[half]))
        copies[-1].start()
    for copy in copies:
        copy.wait()


def select(plan, got):
    return pl.pallas_call(
        select_kernel,
        out_shape=pltpu.HBM((128, PART, BE), F32),
        in_specs=[SM, VM],
        out_specs=HBM,
        scratch_shapes=[pltpu.VMEM((128, PART, BE), F32), pltpu.SemaphoreType.DMA((2,))],
        compiler_params=params(2),
        name="select",
    )(plan, got)


def stencil_loads(fields, chunk, tracers, velocity, mixing, q, u, v, mix, sems):
    parts = LEV // chunk
    rows = chunk * BN
    copies = []
    for c in range(parts):
        row = []
        for i, f in enumerate(fields):
            row.append(pltpu.make_async_copy(
                tracers.at[pl.ds(f * CELLS + c * rows, rows)], q[i].at[pl.ds(8 + c * rows, rows)],
                sems.at[c, i]))
        row.append(pltpu.make_async_copy(
            velocity.at[pl.ds(CELLS + c * rows, rows)], v.at[pl.ds(8 + c * rows, rows)], sems.at[c, 2]))
        row.append(pltpu.make_async_copy(
            velocity.at[pl.ds(c * rows, rows)], u.at[pl.ds(c * rows, rows)], sems.at[c, 3]))
        if mixing is not None:
            size = rows if c + 1 < parts else rows - BN
            row.append(pltpu.make_async_copy(
                mixing.at[pl.ds(c * rows, size)], mix.at[pl.ds(c * rows, size)], sems.at[c, 4]))
        copies.append(row)
    pad = jnp.zeros((8, BE), F32)
    for ref in (*q, v):
        ref[pl.ds(0, 8), :] = pad
        ref[pl.ds(8 + CELLS, 8), :] = pad
    return copies


def stencil_level(k, q, u, v, s):
    lane = lax.broadcasted_iota(jnp.int32, (BN, BE), 1)
    row_id = lax.broadcasted_iota(jnp.int32, (BN, BE), 0)
    at = pl.multiple_of(k * BN, BN)
    here, north, south = pl.ds(at + 8, BN), pl.ds(at + 9, BN), pl.ds(at + 7, BN)
    half_u = 0.5 * u[pl.ds(at, BN), :]
    ua = jnp.where(lane == BE - 1, 0.0, half_u + diffusion)
    ub = jnp.where(lane == BE - 1, 0.0, half_u - diffusion)
    half_v, half_s = 0.5 * v[here, :], 0.5 * v[south, :]
    va = jnp.where(row_id == BN - 1, 0.0, half_v + diffusion)
    vb = jnp.where(row_id == BN - 1, 0.0, half_v - diffusion)
    vas = jnp.where(row_id == 0, 0.0, half_s + diffusion)
    vbs = jnp.where(row_id == 0, 0.0, half_s - diffusion)
    centre = 1.0 - (va - vbs)
    for f in range(2):
        tile = q[f][here, :]
        fe = ua * tile + ub * pltpu.roll(tile, BE - 1, 1)
        s[pl.ds(pl.multiple_of(f * CELLS + at, BN), BN), :] = (
            centre * tile - (fe - pltpu.roll(fe, 1, 1))
            - vb * q[f][north, :] + vas * q[f][south, :])


AHEAD = 6


def begin(copies, c):
    for copy in copies[c] if c < len(copies) else ():
        copy.start()


def arrived(copies, c, beyond=0):
    for d in range(1 + beyond) if c == 0 else (c + beyond,):
        for copy in copies[d] if d < len(copies) else ():
            copy.wait()
    begin(copies, c + AHEAD)


def stencil_kernel(group, chunk, *refs):
    parts = LEV // chunk
    rows = chunk * BN
    if group == 0:
        tracers, velocity, mixing, s, inv_out, q0, q1, u, v, inv, mix, sems, out_sems = refs
    else:
        tracers, velocity, _aliased, s, new, q0, q1, u, v, sems, out_sems = refs
        mixing = mix = None
        leave = pltpu.make_async_copy(s, new.at[pl.ds(0, 2 * CELLS)], out_sems.at[0, 0])
        leave.start()
    q = (q0, q1)
    copies = stencil_loads((2 * group, 2 * group + 1), chunk, tracers, velocity, mixing, q, u, v, mix, sems)
    for c in range(AHEAD):
        begin(copies, c)
    zero = jnp.zeros((BN, BE), F32)
    if group == 0:
        mix[pl.ds(CELLS - BN, BN), :] = zero
    else:
        leave.wait()

    def level(k, carry):
        stencil_level(k, q, u, v, s)
        if group == 1:
            return carry
        m_up, fac_up = carry
        span = pl.ds(pl.multiple_of(k * BN, BN), BN)
        m = mix[span, :]
        inverse = 1.0 / (1.0 + m_up + m - m_up * fac_up)
        inv[span, :] = inverse
        return m, m * inverse

    carry = (zero, zero) if group == 0 else 0
    outs = []
    for c in range(parts):
        arrived(copies, c, 1)
        carry = lax.fori_loop(c * chunk, (c + 1) * chunk, level, carry, unroll=2)
        if group == 0:
            span = pl.ds(c * rows, rows)
            outs.append(pltpu.make_async_copy(inv.at[span], inv_out.at[span], out_sems.at[c, 0]))
            outs[-1].start()
    for copy in outs:
        copy.wait()


def cells(extra=0, fields=1):
    return pltpu.VMEM((fields * CELLS + extra, BE), F32)


def stencil(group, args, chunk=6):
    parts = LEV // chunk
    if group == 0:
        outs, out_specs = (cells(0, 2), pltpu.HBM((CELLS, BE), F32)), (VM, HBM)
        more = [cells(), cells()]
    else:
        outs, out_specs = (cells(0, 2), pltpu.HBM((4 * CELLS, BE), F32)), (VM, HBM)
        more = []
    return pl.pallas_call(
        functools.partial(stencil_kernel, group, chunk),
        out_shape=outs,
        in_specs=[HBM] * 3 if group == 0 else [HBM, HBM, VM],
        out_specs=out_specs,
        input_output_aliases={} if group == 0 else {2: 0},
        scratch_shapes=[
            cells(16), cells(16), cells(), cells(16), *more,
            pltpu.SemaphoreType.DMA((parts, 5)),
            pltpu.SemaphoreType.DMA((parts, 2)),
        ],
        compiler_params=params(10),
        name=f"stencil{group}",
    )(*args)


EDGE_N, EDGE_S, EDGE = BN, BN + 40, BN + 80
BASE_D, BASE_S, BASE_N, BASE = BN, 2 * BN, 2 * BN + 8, 2 * BN + 16


def flux(speed, low, high):
    return speed * (0.5 * (low + high)) - diffusion * (high - low)


def edges(plan, own, halo, out, turn):
    lane = lax.broadcasted_iota(jnp.int32, (LEV, BE), 1)
    open_e, open_w, open_n, open_s = (plan[NBR + d] >= 0 for d in range(4))
    row = lambda ref, at: ref[pl.ds(at, LEV), :]
    v_own, v_south = row(own, NORTH_V), row(halo, NORTH_V)
    for f in range(4):
        fn = flux(v_own, row(own, NORTH_Q[f]), row(halo, SOUTH_Q[f]))
        fs = flux(v_south, row(halo, NORTH_Q[f]), row(own, SOUTH_Q[f]))
        out[pl.ds(f * EDGE + EDGE_N, LEV), :] = jnp.where(open_n, -fn, 0.0)
        out[pl.ds(f * EDGE + EDGE_S, LEV), :] = jnp.where(open_s, fs, 0.0)

    def both(speed):
        return jnp.where(lane < HALF, speed, pltpu.roll(speed, HALF, 1))

    u_own, u_west = both(row(own, EAST + 2 * LEV)), both(row(halo, EAST + 2 * LEV))
    for j in range(2):
        fe = flux(u_own, row(own, EAST + j * LEV), row(halo, WEST + j * LEV))
        fw = flux(u_west, row(halo, EAST + j * LEV), row(own, WEST + j * LEV))
        turn[...] = jnp.zeros((BE, BE), F32)
        turn[pl.ds(0, LEV, stride=2), :] = jnp.where(open_e, -fe, 0.0)
        turn[pl.ds(1, LEV, stride=2), :] = jnp.where(open_w, fw, 0.0)
        turned = turn[...].T
        out[pl.ds(j * EDGE, BN), :] = turned[:BN]
        out[pl.ds((2 + j) * EDGE, BN), :] = turned[BN:]


def solve_kernel(group, chunk, out_chunk, *refs):
    parts = LEV // chunk
    rows = chunk * BN
    outs = []
    if group == 0:
        (plan, _aliased, inv_in, mixing, own_in, halo, depth_in,
         s, edge_out, base, items, inv, mix, edge, turn, parts_out, own, depth,
         sems, side_sems) = refs
        sides = [pltpu.make_async_copy(a, b, side_sems.at[i]) for i, (a, b) in enumerate(
            ((own_in, own), (depth_in, depth)))]
    else:
        (_stirred, inv_in, mixing, edge_in, _new,
         s, new, inv, mix, edge, sems, out_sems, side_sems) = refs
        sides = [pltpu.make_async_copy(edge_in, edge, side_sems.at[0])]
    for copy in sides:
        copy.start()
    first = 2 * group
    copies = []
    for c in range(parts):
        row = []
        span = pl.ds(c * rows, rows)
        row.append(pltpu.make_async_copy(inv_in.at[span], inv.at[span], sems.at[c, 2]))
        span = pl.ds(c * rows, rows if c + 1 < parts else rows - BN)
        row.append(pltpu.make_async_copy(mixing.at[span], mix.at[span], sems.at[c, 3]))
        copies.append(row)
        begin(copies, c)
    for copy in sides:
        copy.wait()
    if group == 0:
        edges(plan, own, halo, edge, turn)
        base[pl.ds(BASE_D, BN), :] = depth[...]
        base[pl.ds(BASE_S, 8), :] = halo[pl.ds(NORTH_D - 4, 8), :]
        base[pl.ds(BASE_N, 8), :] = halo[pl.ds(SOUTH_D, 8), :]
        outs.append(pltpu.make_async_copy(edge, edge_out, side_sems.at[3]))
        outs[-1].start()
    lane = lax.broadcasted_iota(jnp.int32, (BN, BE), 1)
    rim = jnp.logical_or(lane == 0, lane == BE - 1)
    sub = lax.broadcasted_iota(jnp.int32, (8, BE), 0)
    tile = lambda f, k: pl.ds(f * CELLS + k * BN, BN)
    m_up, sol_up = None, [None, None]
    columns = [edge[pl.ds((first + f) * EDGE, BN), :] for f in range(2)]

    for c in range(parts):
        for copy in copies[c]:
            copy.wait()
        for k in range(c * chunk, (c + 1) * chunk):
            inverse = inv[tile(0, k), :]
            for f in range(2):
                value = s[tile(f, k), :] + jnp.where(
                    rim, pltpu.roll(columns[f], BE - 1 - 2 * k, 1), 0.0)
                row = (first + f) * EDGE + k
                value = jnp.concatenate([
                    value[:8] + jnp.where(sub == 0, edge[pl.ds(row + EDGE_S, 1), :], 0.0),
                    value[8:BN - 8],
                    value[BN - 8:] + jnp.where(sub == 7, edge[pl.ds(row + EDGE_N, 1), :], 0.0),
                ], axis=0)
                if k:
                    value = value + m_up * sol_up[f]
                sol_up[f] = value * inverse
                s[tile(f, k), :] = sol_up[f]
            m_up = mix[tile(0, k), :] if k + 1 < LEV else None
    heat, salt = sol_up
    total = None
    for k in range(LEV - 1, -1, -1):
        if k + 1 < LEV:
            factor = mix[tile(0, k), :] * inv[tile(0, k), :]
            heat = s[tile(0, k), :] + factor * heat
            salt = s[tile(1, k), :] + factor * salt
            s[tile(0, k), :] = heat
            s[tile(1, k), :] = salt
        if group == 0:
            weight = forcing * 2.0 * (k + 1) / (LEV * (LEV + 1))
            density = (haline * weight) * salt - heat * (thermal * weight + (cabbeling * weight) * heat)
            total = density if total is None else total + density
        if group == 1 and k % out_chunk == 0:
            for f in range(2):
                outs.append(pltpu.make_async_copy(
                    s.at[pl.ds(f * CELLS + k * BN, out_chunk * BN)],
                    new.at[pl.ds((first + f) * CELLS + k * BN, out_chunk * BN)],
                    out_sems.at[k // out_chunk, f]))
                outs[-1].start()
    if group == 0:
        field = total
        base[pl.ds(0, BN), :] = field
        turned = jnp.concatenate([field, depth[...]], axis=0).T
        east_item, west_item = turned[BE - 3:, :], turned[:3, :]
        sends = (east_item, west_item, field[BN - 3:, :], field[:3, :],
                 east_item, west_item, east_item, west_item)
        for d, item in enumerate(sends):
            to = plan[NBR + d]

            @pl.when(to >= 0)
            def _(to=to, item=item):
                parts_out[to, pl.ds(0, 3), :] = item

        outs.append(pltpu.make_async_copy(parts_out, items, side_sems.at[5]))
        outs[-1].start()
    for copy in outs:
        copy.wait()


def solve(group, args, chunk=12, out_chunk=6):
    edge_rows = 4 * EDGE
    block = lambda rows: pltpu.VMEM((rows, BE), F32)
    if group == 0:
        in_specs = [SM, VM, HBM, HBM, HBM, VM, HBM]
        outs = [cells(0, 2), pltpu.HBM((edge_rows, BE), F32), block(BASE),
                pltpu.HBM((128, PART, BE), F32)]
        out_specs = [VM, HBM, VM, HBM]
        scratch = [cells(), cells(), block(edge_rows), block(BE), pltpu.VMEM((128, PART, BE), F32),
                   block(ITEM), block(BN)]
    else:
        in_specs = [VM] + [HBM] * 4
        outs, out_specs = [cells(0, 2), pltpu.HBM((4 * CELLS, BE), F32)], [VM, HBM]
        scratch = [cells(), cells(), block(edge_rows)]
    scratch += [pltpu.SemaphoreType.DMA((LEV // chunk, 4))]
    if group == 1:
        scratch += [pltpu.SemaphoreType.DMA((LEV // out_chunk, 2))]
    scratch += [pltpu.SemaphoreType.DMA((6,))]
    return pl.pallas_call(
        functools.partial(solve_kernel, group, chunk, out_chunk),
        out_shape=tuple(outs),
        in_specs=in_specs,
        out_specs=tuple(out_specs),
        scratch_shapes=scratch,
        input_output_aliases={1: 0} if group == 0 else {0: 0, 4: 1},
        compiler_params=params(8),
        name=f"solve{group}",
    )(*args)


def chosen(shift, arrays, start, rows):
    value = arrays[-1][pl.ds(start, rows), :]
    for k in range(len(arrays) - 1):
        value = jnp.where(shift == k, arrays[k][pl.ds(start, rows), :], value)
    return value


TALL, WIDE = BN + 8, 2 * BE


def krylov_kernel(plan, base, got, vectors, sums, b_s, d_s):
    nothing = jnp.zeros((3, BE), F32)

    def item(d):
        to = plan[NBR + d]
        return jnp.where(to >= 0, got[jnp.maximum(to, 0), pl.ds(0, 3), :], nothing)

    for ref in (b_s, d_s):
        ref[pl.ds(BN, 8), :] = jnp.zeros((8, WIDE), F32)
    b_s[pl.ds(0, BN), pl.ds(0, BE)] = base[pl.ds(0, BN), :]
    d_s[pl.ds(0, BN), pl.ds(0, BE)] = base[pl.ds(BASE_D, BN), :]
    b_s[pl.ds(BN, 3), pl.ds(0, BE)] = item(2)
    b_s[pl.ds(TALL - 3, 3), pl.ds(0, BE)] = item(3)
    middle = jnp.zeros((BE - 6, BE), F32)
    sides = jnp.concatenate([item(0), middle, item(1)], axis=0).T
    b_s[pl.ds(0, BN), pl.ds(BE, BE)] = sides[:BN]
    d_s[pl.ds(0, BN), pl.ds(BE, BE)] = sides[BN:]
    place = lax.broadcasted_iota(jnp.int32, (3, BE), 1)
    place = jnp.where(place >= BN, place - BN, place)

    def corner(north, south):
        return jnp.where(place < 3, north, jnp.where(
            jnp.logical_and(place >= 5, place < 8), pltpu.roll(south, BE - BN + 8, 1), 0.0))

    corners = jnp.concatenate([corner(item(4), item(6)), middle, corner(item(5), item(7))], axis=0).T
    b_s[pl.ds(BN, 8), pl.ds(BE, BE)] = corners[:8]
    d_s[pl.ds(BN, 8), pl.ds(BE, BE)] = corners[BN:BN + 8]

    d_s[pl.ds(BN, 3), pl.ds(0, BE)] = jnp.where(
        plan[NBR + 2] >= 0, base[pl.ds(BASE_N, 3), :], 0.0)
    d_s[pl.ds(TALL - 3, 3), pl.ds(0, BE)] = jnp.where(
        plan[NBR + 3] >= 0, base[pl.ds(BASE_S + 4, 3), :], 0.0)
    d = d_s[...]
    east = lambda a: pltpu.roll(a, WIDE - 1, 1)
    west = lambda a: pltpu.roll(a, 1, 1)
    north = lambda a: pltpu.roll(a, TALL - 1, 0)
    south = lambda a: pltpu.roll(a, 1, 0)
    d_e, d_n = east(d), north(d)
    w_e = jnp.where(jnp.logical_and(d > 0, d_e > 0), 0.5 * (d + d_e), 0.0)
    w_n = jnp.where(jnp.logical_and(d > 0, d_n > 0), 0.5 * (d + d_n), 0.0)
    w_w, w_s = west(w_e), south(w_n)
    diagonal = area_term + w_e + w_w + w_n + w_s

    def operate(h):
        return diagonal * h - w_e * east(h) - w_w * west(h) - w_n * north(h) - w_s * south(h)

    v0 = b_s[...]
    v1 = operate(v0)
    v2 = operate(v1)
    v3 = operate(v2)
    v = [a[:BN, :BE] for a in (v0, v1, v2, v3)]
    for i in range(3):
        vectors[pl.ds(i * BN, BN), :] = v[i]
    pairs = ((0, 0), (0, 1), (1, 1), (1, 2), (2, 2), (2, 3))
    at = lax.broadcasted_iota(jnp.int32, (1, BE), 1)
    total = jnp.zeros((1, BE), F32)
    for i, (a, b) in enumerate(pairs):
        value = jnp.sum(jnp.sum(v[a] * v[b], axis=0, keepdims=True), axis=1, keepdims=True)
        total = jnp.where(at == i, value, total)
    for i in range(128):
        sums[i] = total


def krylov(plan, base, got):
    return pl.pallas_call(
        krylov_kernel,
        out_shape=(
            jax.ShapeDtypeStruct((3 * BN, BE), F32),
            jax.ShapeDtypeStruct((128, 1, BE), F32),
        ),
        in_specs=[SM, VM, VM],
        out_specs=(VM, VM),
        scratch_shapes=[pltpu.VMEM((TALL, WIDE), F32)] * 2,
        compiler_params=params(4),
        name="krylov",
    )(plan, base, got)


def combine_kernel(plan, sums, a0, a1, a2, a3, o0, o1, o2, o3):
    total = jnp.sum(sums[...], axis=0, keepdims=True)
    moment = [total[:, i:i + 1] for i in range(6)]

    def inner(a, b, lift):
        value = None
        for i in range(len(a)):
            for j in range(len(b)):
                term = a[i] * b[j] * moment[i + j + lift]
                value = term if value is None else value + term
        return value

    one = jnp.ones((1, 1), F32)
    zero = jnp.zeros((1, 1), F32)
    residual, direction = [one], [one]
    solution = [zero, zero, zero]
    rr = moment[0]
    for step in range(3):
        alpha = rr / inner(direction, direction, 1)
        for i, c in enumerate(direction):
            solution[i] = solution[i] + alpha * c
        if step < 2:
            image = [zero] + direction
            padded = residual + [zero]
            residual = [r - alpha * c for r, c in zip(padded, image)]
            following = inner(residual, residual, 0)
            beta = following / rr
            direction = [r + beta * c for r, c in zip(residual, direction + [zero])]
            rr = following
    solved = []
    for a in (a0, a1, a2, a3):
        v = [a[pl.ds(i * BN, BN), :] for i in range(3)]
        solved.append(solution[0] * v[0] + solution[1] * v[1] + solution[2] * v[2])
    for k, out in enumerate((o0, o1, o2, o3)):
        for b in range(2):
            shift = plan[TSEND + 2 * k + b]
            value = solved[3]
            for j in range(3):
                value = jnp.where(shift == j, solved[j], value)
            out[pl.ds(b * BN, BN), :] = value


def combine(plan, sums, arrays):
    return pl.pallas_call(
        combine_kernel,
        out_shape=(jax.ShapeDtypeStruct((2 * BN, BE), F32),) * 4,
        in_specs=[SM] + [VM] * 5,
        out_specs=(VM,) * 4,
        compiler_params=params(4),
        name="combine",
    )(plan, sums, *arrays)


def place_kernel(plan, a0, a1, a2, a3, out):
    for b in range(2):
        shift = plan[TFROM + b]
        value = chosen(shift, (a0, a1, a2, a3), b * BN, BN)
        out[b] = jnp.where(shift >= 0, value, 0.0)


def place(plan, arrays):
    return pl.pallas_call(
        place_kernel,
        out_shape=jax.ShapeDtypeStruct((2, BN, BE), F32),
        in_specs=[SM] + [VM] * 4,
        out_specs=VM,
        compiler_params=params(4),
        name="place",
    )(plan, *arrays)


def body(tracers, velocity, mixing_rate, column_depth, ocean_mask, clinic_list, tropic_list):
    side = SIDE
    depth = column_depth.reshape(BN, BE)
    every = lambda value: lax.all_to_all(value, EVERY, 0, 0)

    def along_y(value, k):
        return lax.ppermute(value, "y", [(y, (y + k) % side) for y in range(side)])

    def along_z(value, k):
        return lax.ppermute(value, "z", [(z, (z + k) % side) for z in range(side)])

    in_hbm = lambda value: pltpu.with_memory_space_constraint(value, pltpu.HBM)
    tracers = in_hbm(tracers.reshape(4 * CELLS, BE))
    velocity = in_hbm(velocity.reshape(2 * CELLS, BE))
    mixing = in_hbm(mixing_rate.reshape((LEV - 1) * BN, BE))
    depth = in_hbm(depth)
    own = pack(tracers, velocity, depth)
    in_vmem = lambda value: pltpu.with_memory_space_constraint(value, pltpu.VMEM)
    plan = pl.pallas_call(
        functools.partial(make_plan, SIDE, N_GY, N_GX),
        out_shape=jax.ShapeDtypeStruct((PLAN,), jnp.int32),
        in_specs=[SM, SM],
        out_specs=SM,
        scratch_shapes=[pltpu.SMEM(((N_GY + 2) * WRAP,), jnp.int32)],
        compiler_params=params(1),
        name="plan",
    )(clinic_list, tropic_list)
    first_two, inv = stencil(0, (tracers, velocity, mixing))
    first_two, inv = in_vmem(first_two), in_hbm(inv)
    scattered = every(own.reshape(128, PART, BE))
    halo = every(select(plan, scattered)).reshape(ITEM, BE)
    mixed, edge, base, items = solve(0, (plan, first_two, inv, mixing, in_hbm(own), halo, depth), chunk=36)
    got = every(items)
    edge = in_hbm(edge)
    last_two, new = stencil(1, (tracers, velocity, in_vmem(mixed)))
    got, last_two = lax.optimization_barrier((got, last_two))
    vectors, sums = krylov(plan, in_vmem(base), got)
    totals = lax.all_to_all(sums, ("c", "x", "y", "z"), 0, 0)
    _, new = solve(1, (in_vmem(last_two), inv, mixing, edge, in_hbm(new)), chunk=18)
    totals, new = lax.optimization_barrier((totals, new))
    line = [vectors] + [along_y(vectors, k) for k in range(1, side)]
    sends = combine(plan, totals.reshape(128, BE), line)
    arrived = [sends[0]] + [along_z(sends[k], k) for k in range(1, side)]
    height = place(plan, arrived)
    return new.reshape(1, 1, 4, LEV, BN, BE), height[None]


def solution(mesh):
    mesh = Mesh(mesh.devices.reshape(*(SIZES[axis] for axis in "zyxc")), tuple("zyxc"))
    gx, gy = ("z", "y"), ("x", "c")
    return jax.shard_map(
        body,
        mesh=mesh,
        in_specs=(P(gy, gx), P(gy, gx), P(gy, gx), P(gy, gx), P(), P(), P()),
        out_specs=(P(gy, gx), P(gy, gx)),
        check_vma=False,
    )
```

```python
import functools
import jax
import jax.numpy as jnp
from jax import lax
from jax.experimental import pallas as pl
from jax.experimental.pallas import tpu as pltpu
from jax.sharding import Mesh, PartitionSpec as P

F32 = jnp.float32
LEV, BN, BE = 36, 64, 128
NBX = 28
N_GX, N_GY, SIDE = 16, 8, 4
SIZES = {"z": 4, "y": 4, "x": 4, "c": 2}
EVERY = ('c', 'z', 'x', 'y')
CELLS = LEV * BN
HALF = BE // 2

NORTH = 0
NORTH_Q = (0, LEV, 3 * LEV, 4 * LEV)
NORTH_V = 2 * LEV
NORTH_D = 5 * LEV
SOUTH = 184
SOUTH_Q = tuple(SOUTH + f * LEV for f in range(4))
SOUTH_D = SOUTH + 4 * LEV
EAST = 332
WEST = 440
ITEM = 512
PART = 4

diffusion = 0.12
area_term = 0.1
thermal = 0.2
haline = 0.25
cabbeling = 0.05
forcing = 4.0

NBR = 0
TFROM = 8
TSEND = 10
RELAY = 18
PLAN = RELAY + 128
WRAP = NBX + 4

DIRS = ((0, 1), (0, -1), (1, 0), (-1, 0), (1, 1), (1, -1), (-1, 1), (-1, -1))


def params(mib, **more):
    return pltpu.CompilerParams(vmem_limit_bytes=mib * 1024 * 1024, **more)


VM = pl.BlockSpec(memory_space=pltpu.VMEM)
SM = pl.BlockSpec(memory_space=pltpu.SMEM)
ANY = pl.BlockSpec(memory_space=pl.ANY)
HBM = pl.BlockSpec(memory_space=pltpu.HBM)


def shaped(*shape):
    return jax.ShapeDtypeStruct(shape, F32)


def place_of(axis, slot, row):
    return {"z": slot // SIDE, "y": slot % SIDE, "x": row // 2, "c": row % 2}[axis]


def device_of(slot, row):
    index = 0
    for axis in EVERY:
        index = index * SIZES[axis] + place_of(axis, slot, row)
    return index


def slot_of(device):
    stride, at = 1, {}
    for axis in reversed(EVERY):
        at[axis] = lax.rem(device // stride, SIZES[axis])
        stride *= SIZES[axis]
    return at["z"] * SIDE + at["y"]


def make_plan(side, n_gy, slots, clinic, tropic, out, pos):
    z, y = lax.axis_index("z"), lax.axis_index("y")
    gx = z * side + y
    gy = lax.axis_index("x") * 2 + lax.axis_index("c")

    def clear(i, carry):
        pos[i] = jnp.int32(-1)
        return carry

    lax.fori_loop(0, (n_gy + 2) * WRAP, clear, 0, unroll=16)
    for row in range(n_gy):
        for slot in range(slots):
            pos[(row + 1) * WRAP + 1 + clinic[row, slot]] = jnp.int32(device_of(slot, row))
    for row in range(1, n_gy + 1):
        pos[row * WRAP] = pos[row * WRAP + NBX]
        pos[row * WRAP + NBX + 1] = pos[row * WRAP + 1]
    centre = (gy + 1) * WRAP + 1 + clinic[gy, gx]
    for d, (dr, dc) in enumerate(DIRS):
        out[NBR + d] = pos[centre + (dr * WRAP + dc)]
    me = jnp.int32(0)
    for axis in EVERY:
        me = me * SIZES[axis] + lax.axis_index(axis)
    kind_s, kind_n, kind_w = me < SOUTH // PART, me < EAST // PART, me < WEST // PART
    move = jnp.where(kind_s, jnp.int32(-WRAP), jnp.where(kind_n, jnp.int32(WRAP), jnp.where(
        kind_w, jnp.int32(-1), jnp.int32(1))))
    for row in range(n_gy):
        for there in range(slots):
            source = pos[(row + 1) * WRAP + 1 + clinic[row, there] + move]
            out[RELAY + device_of(there, row)] = jnp.maximum(source, 0)

    def owner(there, b):
        column_b = tropic[gy, 2 * there + b]
        device = pos[(gy + 1) * WRAP + 1 + jnp.maximum(column_b, 0)]
        return jnp.where(column_b < 0, jnp.int32(-1), slot_of(device))

    for k in range(side):
        there = lax.rem(z + k, side) * side + y
        for b in range(2):
            slot = owner(there, b)
            shift = lax.rem(y - lax.rem(slot, side) + side, side)
            out[TSEND + 2 * k + b] = jnp.where(slot < 0, jnp.int32(0), shift)
    for b in range(2):
        slot = owner(gx, b)
        shift = lax.rem(z - slot // side + side, side)
        out[TFROM + b] = jnp.where(slot < 0, jnp.int32(-1), shift)


def pack_kernel(tracers, velocity, depth_in, item, q, vel, turn, own, depth, sems):
    order = (0, 2, 4, 1, 3, 5)
    copies = {}
    fetch_depth = pltpu.make_async_copy(depth_in, depth, sems.at[6])
    fetch_depth.start()
    for f in order:
        source, at = (tracers, f) if f < 4 else (velocity, f - 4)
        target = q if f < 4 else vel
        size = CELLS // 2 if f == 0 else CELLS
        span = pl.ds(at * CELLS, size)
        copies[f] = pltpu.make_async_copy(source.at[span], target.at[span], sems.at[f])
        copies[f].start()
        if f == 0:
            span = pl.ds(size, size)
            second_half = pltpu.make_async_copy(source.at[span], target.at[span], sems.at[9])
            second_half.start()
    fetch_depth.wait()
    lane = lax.broadcasted_iota(jnp.int32, (BN, BE), 1)
    level = lane // 2
    own[pl.ds(NORTH_D, 3), :] = depth[pl.ds(BN - 3, 3), :]
    own[pl.ds(NORTH_D + 3, 1), :] = jnp.zeros((1, BE), F32)
    own[pl.ds(SOUTH_D, 3), :] = depth[pl.ds(0, 3), :]
    own[pl.ds(SOUTH_D + 3, 1), :] = jnp.zeros((1, BE), F32)

    def columns(f):
        copies[f].wait()
        sides = jnp.zeros((BN, BE), F32)
        for k in range(LEV):
            if f == 0 and k == LEV // 2:
                second_half.wait()
            tile = q[pl.ds(f * CELLS + k * BN, BN), :]
            sides = jnp.where(level == k, pltpu.roll(tile, 2 * k + 1, 1), sides)
        own[pl.ds(NORTH_Q[f], LEV), :] = q[pl.ds(f * CELLS + BN - 1, LEV, stride=BN), :]
        own[pl.ds(SOUTH_Q[f], LEV), :] = q[pl.ds(f * CELLS, LEV, stride=BN), :]
        return sides

    for j in range(2):
        first, second = columns(j), columns(2 + j)
        if j == 0:
            copies[4].wait()
            for k in range(LEV):
                tile = vel[pl.ds(k * BN, BN), :]
                first = jnp.where(lane == 2 * LEV + k, pltpu.roll(tile, 2 * LEV + 1 + k, 1), first)
        if j == 1:
            copies[5].wait()
            own[pl.ds(NORTH_V, LEV), :] = vel[pl.ds(CELLS + BN - 1, LEV, stride=BN), :]
            rows_out = pltpu.make_async_copy(own.at[pl.ds(0, 328)], item.at[pl.ds(0, 328)], sems.at[7])
            rows_out.start()
        turn[...] = jnp.concatenate([first, second], axis=0).T
        own[pl.ds(EAST + j * LEV, LEV), :] = turn[pl.ds(0, LEV, stride=2), :]
        own[pl.ds(WEST + j * LEV, LEV), :] = turn[pl.ds(1, LEV, stride=2), :]
        if j == 0:
            own[pl.ds(EAST + 2 * LEV, LEV), :] = turn[pl.ds(2 * LEV, LEV), :]
    rest = pl.ds(328, ITEM - 328)
    rest_out = pltpu.make_async_copy(own.at[rest], item.at[rest], sems.at[8])
    rest_out.start()
    rows_out.wait()
    rest_out.wait()


def pack(tracers, velocity, depth):
    return pl.pallas_call(
        pack_kernel,
        out_shape=pltpu.HBM((ITEM, BE), F32),
        in_specs=[HBM, HBM, HBM],
        out_specs=HBM,
        scratch_shapes=[
            pltpu.VMEM((4 * CELLS, BE), F32),
            pltpu.VMEM((2 * CELLS, BE), F32),
            pltpu.VMEM((BE, BE), F32),
            pltpu.VMEM((ITEM, BE), F32),
            pltpu.VMEM((BN, BE), F32),
            pltpu.SemaphoreType.DMA((10,)),
        ],
        compiler_params=params(12),
        name="pack",
    )(tracers, velocity, depth)


def select_kernel(plan, got, out, chosen_parts, sems):
    def one(d, carry):
        chosen_parts[d] = got[plan[RELAY + d]]
        return carry

    copies = []
    for half in range(2):
        lax.fori_loop(64 * half, 64 * half + 64, one, 0, unroll=16)
        span = pl.ds(64 * half, 64)
        copies.append(pltpu.make_async_copy(chosen_parts.at[span], out.at[span], sems.at[half]))
        copies[-1].start()
    for copy in copies:
        copy.wait()


def select(plan, got):
    return pl.pallas_call(
        select_kernel,
        out_shape=pltpu.HBM((128, PART, BE), F32),
        in_specs=[SM, VM],
        out_specs=HBM,
        scratch_shapes=[pltpu.VMEM((128, PART, BE), F32), pltpu.SemaphoreType.DMA((2,))],
        compiler_params=params(2),
        name="select",
    )(plan, got)


def stencil_loads(fields, chunk, tracers, velocity, mixing, q, u, v, mix, sems):
    parts = LEV // chunk
    rows = chunk * BN
    copies = []
    for c in range(parts):
        row = []
        for i, f in enumerate(fields):
            row.append(pltpu.make_async_copy(
                tracers.at[pl.ds(f * CELLS + c * rows, rows)], q[i].at[pl.ds(8 + c * rows, rows)],
                sems.at[c, i]))
        row.append(pltpu.make_async_copy(
            velocity.at[pl.ds(CELLS + c * rows, rows)], v.at[pl.ds(8 + c * rows, rows)], sems.at[c, 2]))
        row.append(pltpu.make_async_copy(
            velocity.at[pl.ds(c * rows, rows)], u.at[pl.ds(c * rows, rows)], sems.at[c, 3]))
        if mixing is not None:
            size = rows if c + 1 < parts else rows - BN
            row.append(pltpu.make_async_copy(
                mixing.at[pl.ds(c * rows, size)], mix.at[pl.ds(c * rows, size)], sems.at[c, 4]))
        copies.append(row)
    pad = jnp.zeros((8, BE), F32)
    for ref in (*q, v):
        ref[pl.ds(0, 8), :] = pad
        ref[pl.ds(8 + CELLS, 8), :] = pad
    return copies


def stencil_level(k, q, u, v, s):
    lane = lax.broadcasted_iota(jnp.int32, (BN, BE), 1)
    row_id = lax.broadcasted_iota(jnp.int32, (BN, BE), 0)
    at = pl.multiple_of(k * BN, BN)
    here, north, south = pl.ds(at + 8, BN), pl.ds(at + 9, BN), pl.ds(at + 7, BN)
    half_u = 0.5 * u[pl.ds(at, BN), :]
    ua = jnp.where(lane == BE - 1, 0.0, half_u + diffusion)
    ub = jnp.where(lane == BE - 1, 0.0, half_u - diffusion)
    half_v, half_s = 0.5 * v[here, :], 0.5 * v[south, :]
    va = jnp.where(row_id == BN - 1, 0.0, half_v + diffusion)
    vb = jnp.where(row_id == BN - 1, 0.0, half_v - diffusion)
    vas = jnp.where(row_id == 0, 0.0, half_s + diffusion)
    vbs = jnp.where(row_id == 0, 0.0, half_s - diffusion)
    centre = 1.0 - (va - vbs)
    for f in range(2):
        tile = q[f][here, :]
        fe = ua * tile + ub * pltpu.roll(tile, BE - 1, 1)
        s[pl.ds(pl.multiple_of(f * CELLS + at, BN), BN), :] = (
            centre * tile - (fe - pltpu.roll(fe, 1, 1))
            - vb * q[f][north, :] + vas * q[f][south, :])


AHEAD = 6


def begin(copies, c):
    for copy in copies[c] if c < len(copies) else ():
        copy.start()


def arrived(copies, c, beyond=0):
    for d in range(1 + beyond) if c == 0 else (c + beyond,):
        for copy in copies[d] if d < len(copies) else ():
            copy.wait()
    begin(copies, c + AHEAD)


def stencil_kernel(group, chunk, *refs):
    parts = LEV // chunk
    rows = chunk * BN
    if group == 0:
        tracers, velocity, mixing, s, inv_out, q0, q1, u, v, inv, mix, sems, out_sems = refs
    else:
        tracers, velocity, _aliased, s, new, q0, q1, u, v, sems, out_sems = refs
        mixing = mix = None
        leave = pltpu.make_async_copy(s, new.at[pl.ds(0, 2 * CELLS)], out_sems.at[0, 0])
        leave.start()
    q = (q0, q1)
    copies = stencil_loads((2 * group, 2 * group + 1), chunk, tracers, velocity, mixing, q, u, v, mix, sems)
    for c in range(AHEAD):
        begin(copies, c)
    zero = jnp.zeros((BN, BE), F32)
    if group == 0:
        mix[pl.ds(CELLS - BN, BN), :] = zero
    else:
        leave.wait()

    def level(k, carry):
        stencil_level(k, q, u, v, s)
        if group == 1:
            return carry
        m_up, fac_up = carry
        span = pl.ds(pl.multiple_of(k * BN, BN), BN)
        m = mix[span, :]
        inverse = 1.0 / (1.0 + m_up + m - m_up * fac_up)
        inv[span, :] = inverse
        return m, m * inverse

    carry = (zero, zero) if group == 0 else 0
    outs = []
    for c in range(parts):
        arrived(copies, c, 1)
        carry = lax.fori_loop(c * chunk, (c + 1) * chunk, level, carry, unroll=2)
        if group == 0:
            span = pl.ds(c * rows, rows)
            outs.append(pltpu.make_async_copy(inv.at[span], inv_out.at[span], out_sems.at[c, 0]))
            outs[-1].start()
    for copy in outs:
        copy.wait()


def cells(extra=0, fields=1):
    return pltpu.VMEM((fields * CELLS + extra, BE), F32)


def stencil(group, args, chunk=6):
    parts = LEV // chunk
    if group == 0:
        outs, out_specs = (cells(0, 2), pltpu.HBM((CELLS, BE), F32)), (VM, HBM)
        more = [cells(), cells()]
    else:
        outs, out_specs = (cells(0, 2), pltpu.HBM((4 * CELLS, BE), F32)), (VM, HBM)
        more = []
    return pl.pallas_call(
        functools.partial(stencil_kernel, group, chunk),
        out_shape=outs,
        in_specs=[HBM] * 3 if group == 0 else [HBM, HBM, VM],
        out_specs=out_specs,
        input_output_aliases={} if group == 0 else {2: 0},
        scratch_shapes=[
            cells(16), cells(16), cells(), cells(16), *more,
            pltpu.SemaphoreType.DMA((parts, 5)),
            pltpu.SemaphoreType.DMA((parts, 2)),
        ],
        compiler_params=params(10),
        name=f"stencil{group}",
    )(*args)


EDGE_N, EDGE_S, EDGE = BN, BN + 40, BN + 80
BASE_D, BASE_S, BASE_N, BASE = BN, 2 * BN, 2 * BN + 8, 2 * BN + 16


def flux(speed, low, high):
    return speed * (0.5 * (low + high)) - diffusion * (high - low)


def edges(plan, own, halo, out, turn):
    lane = lax.broadcasted_iota(jnp.int32, (LEV, BE), 1)
    open_e, open_w, open_n, open_s = (plan[NBR + d] >= 0 for d in range(4))
    row = lambda ref, at: ref[pl.ds(at, LEV), :]
    v_own, v_south = row(own, NORTH_V), row(halo, NORTH_V)
    for f in range(4):
        fn = flux(v_own, row(own, NORTH_Q[f]), row(halo, SOUTH_Q[f]))
        fs = flux(v_south, row(halo, NORTH_Q[f]), row(own, SOUTH_Q[f]))
        out[pl.ds(f * EDGE + EDGE_N, LEV), :] = jnp.where(open_n, -fn, 0.0)
        out[pl.ds(f * EDGE + EDGE_S, LEV), :] = jnp.where(open_s, fs, 0.0)

    def both(speed):
        return jnp.where(lane < HALF, speed, pltpu.roll(speed, HALF, 1))

    u_own, u_west = both(row(own, EAST + 2 * LEV)), both(row(halo, EAST + 2 * LEV))
    for j in range(2):
        fe = flux(u_own, row(own, EAST + j * LEV), row(halo, WEST + j * LEV))
        fw = flux(u_west, row(halo, EAST + j * LEV), row(own, WEST + j * LEV))
        turn[...] = jnp.zeros((BE, BE), F32)
        turn[pl.ds(0, LEV, stride=2), :] = jnp.where(open_e, -fe, 0.0)
        turn[pl.ds(1, LEV, stride=2), :] = jnp.where(open_w, fw, 0.0)
        turned = turn[...].T
        out[pl.ds(j * EDGE, BN), :] = turned[:BN]
        out[pl.ds((2 + j) * EDGE, BN), :] = turned[BN:]


def solve_kernel(group, chunk, out_chunk, *refs):
    parts = LEV // chunk
    rows = chunk * BN
    outs = []
    if group == 0:
        (plan, _aliased, inv_in, mixing, own_in, halo, depth_in,
         s, edge_out, base, items, inv, mix, edge, turn, parts_out, own, depth,
         sems, side_sems) = refs
        sides = [pltpu.make_async_copy(a, b, side_sems.at[i]) for i, (a, b) in enumerate(
            ((own_in, own), (depth_in, depth)))]
    else:
        (_stirred, inv_in, mixing, edge_in, _new,
         s, new, inv, mix, edge, sems, out_sems, side_sems) = refs
        sides = [pltpu.make_async_copy(edge_in, edge, side_sems.at[0])]
    for copy in sides:
        copy.start()
    first = 2 * group
    copies = []
    for c in range(parts):
        row = []
        span = pl.ds(c * rows, rows)
        row.append(pltpu.make_async_copy(inv_in.at[span], inv.at[span], sems.at[c, 2]))
        span = pl.ds(c * rows, rows if c + 1 < parts else rows - BN)
        row.append(pltpu.make_async_copy(mixing.at[span], mix.at[span], sems.at[c, 3]))
        copies.append(row)
        begin(copies, c)
    for copy in sides:
        copy.wait()
    if group == 0:
        edges(plan, own, halo, edge, turn)
        base[pl.ds(BASE_D, BN), :] = depth[...]
        base[pl.ds(BASE_S, 8), :] = halo[pl.ds(NORTH_D - 4, 8), :]
        base[pl.ds(BASE_N, 8), :] = halo[pl.ds(SOUTH_D, 8), :]
        outs.append(pltpu.make_async_copy(edge, edge_out, side_sems.at[3]))
        outs[-1].start()
    lane = lax.broadcasted_iota(jnp.int32, (BN, BE), 1)
    rim = jnp.logical_or(lane == 0, lane == BE - 1)
    sub = lax.broadcasted_iota(jnp.int32, (8, BE), 0)
    tile = lambda f, k: pl.ds(f * CELLS + k * BN, BN)
    m_up, sol_up = None, [None, None]
    columns = [edge[pl.ds((first + f) * EDGE, BN), :] for f in range(2)]

    for c in range(parts):
        for copy in copies[c]:
            copy.wait()
        for k in range(c * chunk, (c + 1) * chunk):
            inverse = inv[tile(0, k), :]
            for f in range(2):
                value = s[tile(f, k), :] + jnp.where(
                    rim, pltpu.roll(columns[f], BE - 1 - 2 * k, 1), 0.0)
                row = (first + f) * EDGE + k
                value = jnp.concatenate([
                    value[:8] + jnp.where(sub == 0, edge[pl.ds(row + EDGE_S, 1), :], 0.0),
                    value[8:BN - 8],
                    value[BN - 8:] + jnp.where(sub == 7, edge[pl.ds(row + EDGE_N, 1), :], 0.0),
                ], axis=0)
                if k:
                    value = value + m_up * sol_up[f]
                sol_up[f] = value * inverse
                s[tile(f, k), :] = sol_up[f]
            m_up = mix[tile(0, k), :] if k + 1 < LEV else None
    heat, salt = sol_up
    total = None
    for k in range(LEV - 1, -1, -1):
        if k + 1 < LEV:
            factor = mix[tile(0, k), :] * inv[tile(0, k), :]
            heat = s[tile(0, k), :] + factor * heat
            salt = s[tile(1, k), :] + factor * salt
            s[tile(0, k), :] = heat
            s[tile(1, k), :] = salt
        if group == 0:
            weight = forcing * 2.0 * (k + 1) / (LEV * (LEV + 1))
            density = (haline * weight) * salt - heat * (thermal * weight + (cabbeling * weight) * heat)
            total = density if total is None else total + density
        if group == 1 and k % out_chunk == 0:
            for f in range(2):
                outs.append(pltpu.make_async_copy(
                    s.at[pl.ds(f * CELLS + k * BN, out_chunk * BN)],
                    new.at[pl.ds((first + f) * CELLS + k * BN, out_chunk * BN)],
                    out_sems.at[k // out_chunk, f]))
                outs[-1].start()
    if group == 0:
        field = total
        base[pl.ds(0, BN), :] = field
        turned = jnp.concatenate([field, depth[...]], axis=0).T
        east_item, west_item = turned[BE - 3:, :], turned[:3, :]
        sends = (east_item, west_item, field[BN - 3:, :], field[:3, :],
                 east_item, west_item, east_item, west_item)
        for d, item in enumerate(sends):
            to = plan[NBR + d]

            @pl.when(to >= 0)
            def _(to=to, item=item):
                parts_out[to, pl.ds(0, 3), :] = item

        outs.append(pltpu.make_async_copy(parts_out, items, side_sems.at[5]))
        outs[-1].start()
    for copy in outs:
        copy.wait()


def solve(group, args, chunk=12, out_chunk=6):
    edge_rows = 4 * EDGE
    block = lambda rows: pltpu.VMEM((rows, BE), F32)
    if group == 0:
        in_specs = [SM, VM, HBM, HBM, HBM, VM, HBM]
        outs = [cells(0, 2), pltpu.HBM((edge_rows, BE), F32), block(BASE),
                pltpu.HBM((128, PART, BE), F32)]
        out_specs = [VM, HBM, VM, HBM]
        scratch = [cells(), cells(), block(edge_rows), block(BE), pltpu.VMEM((128, PART, BE), F32),
                   block(ITEM), block(BN)]
    else:
        in_specs = [VM] + [HBM] * 4
        outs, out_specs = [cells(0, 2), pltpu.HBM((4 * CELLS, BE), F32)], [VM, HBM]
        scratch = [cells(), cells(), block(edge_rows)]
    scratch += [pltpu.SemaphoreType.DMA((LEV // chunk, 4))]
    if group == 1:
        scratch += [pltpu.SemaphoreType.DMA((LEV // out_chunk, 2))]
    scratch += [pltpu.SemaphoreType.DMA((6,))]
    return pl.pallas_call(
        functools.partial(solve_kernel, group, chunk, out_chunk),
        out_shape=tuple(outs),
        in_specs=in_specs,
        out_specs=tuple(out_specs),
        scratch_shapes=scratch,
        input_output_aliases={1: 0} if group == 0 else {0: 0, 4: 1},
        compiler_params=params(8),
        name=f"solve{group}",
    )(*args)


def chosen(shift, arrays, start, rows):
    value = arrays[-1][pl.ds(start, rows), :]
    for k in range(len(arrays) - 1):
        value = jnp.where(shift == k, arrays[k][pl.ds(start, rows), :], value)
    return value


TALL, WIDE = BN + 8, 2 * BE


def krylov_kernel(plan, base, got, vectors, sums, b_s, d_s):
    nothing = jnp.zeros((3, BE), F32)

    def item(d):
        to = plan[NBR + d]
        return jnp.where(to >= 0, got[jnp.maximum(to, 0), pl.ds(0, 3), :], nothing)

    for ref in (b_s, d_s):
        ref[pl.ds(BN, 8), :] = jnp.zeros((8, WIDE), F32)
    b_s[pl.ds(0, BN), pl.ds(0, BE)] = base[pl.ds(0, BN), :]
    d_s[pl.ds(0, BN), pl.ds(0, BE)] = base[pl.ds(BASE_D, BN), :]
    b_s[pl.ds(BN, 3), pl.ds(0, BE)] = item(2)
    b_s[pl.ds(TALL - 3, 3), pl.ds(0, BE)] = item(3)
    middle = jnp.zeros((BE - 6, BE), F32)
    sides = jnp.concatenate([item(0), middle, item(1)], axis=0).T
    b_s[pl.ds(0, BN), pl.ds(BE, BE)] = sides[:BN]
    d_s[pl.ds(0, BN), pl.ds(BE, BE)] = sides[BN:]
    place = lax.broadcasted_iota(jnp.int32, (3, BE), 1)
    place = jnp.where(place >= BN, place - BN, place)

    def corner(north, south):
        return jnp.where(place < 3, north, jnp.where(
            jnp.logical_and(place >= 5, place < 8), pltpu.roll(south, BE - BN + 8, 1), 0.0))

    corners = jnp.concatenate([corner(item(4), item(6)), middle, corner(item(5), item(7))], axis=0).T
    b_s[pl.ds(BN, 8), pl.ds(BE, BE)] = corners[:8]
    d_s[pl.ds(BN, 8), pl.ds(BE, BE)] = corners[BN:BN + 8]

    d_s[pl.ds(BN, 3), pl.ds(0, BE)] = jnp.where(
        plan[NBR + 2] >= 0, base[pl.ds(BASE_N, 3), :], 0.0)
    d_s[pl.ds(TALL - 3, 3), pl.ds(0, BE)] = jnp.where(
        plan[NBR + 3] >= 0, base[pl.ds(BASE_S + 4, 3), :], 0.0)
    d = d_s[...]
    east = lambda a: pltpu.roll(a, WIDE - 1, 1)
    west = lambda a: pltpu.roll(a, 1, 1)
    north = lambda a: pltpu.roll(a, TALL - 1, 0)
    south = lambda a: pltpu.roll(a, 1, 0)
    d_e, d_n = east(d), north(d)
    w_e = jnp.where(jnp.logical_and(d > 0, d_e > 0), 0.5 * (d + d_e), 0.0)
    w_n = jnp.where(jnp.logical_and(d > 0, d_n > 0), 0.5 * (d + d_n), 0.0)
    w_w, w_s = west(w_e), south(w_n)
    diagonal = area_term + w_e + w_w + w_n + w_s

    def operate(h):
        return diagonal * h - w_e * east(h) - w_w * west(h) - w_n * north(h) - w_s * south(h)

    v0 = b_s[...]
    v1 = operate(v0)
    v2 = operate(v1)
    v3 = operate(v2)
    v = [a[:BN, :BE] for a in (v0, v1, v2, v3)]
    for i in range(3):
        vectors[pl.ds(i * BN, BN), :] = v[i]
    pairs = ((0, 0), (0, 1), (1, 1), (1, 2), (2, 2), (2, 3))
    at = lax.broadcasted_iota(jnp.int32, (1, BE), 1)
    total = jnp.zeros((1, BE), F32)
    for i, (a, b) in enumerate(pairs):
        value = jnp.sum(jnp.sum(v[a] * v[b], axis=0, keepdims=True), axis=1, keepdims=True)
        total = jnp.where(at == i, value, total)
    for i in range(128):
        sums[i] = total


def krylov(plan, base, got):
    return pl.pallas_call(
        krylov_kernel,
        out_shape=(
            jax.ShapeDtypeStruct((3 * BN, BE), F32),
            jax.ShapeDtypeStruct((128, 1, BE), F32),
        ),
        in_specs=[SM, VM, VM],
        out_specs=(VM, VM),
        scratch_shapes=[pltpu.VMEM((TALL, WIDE), F32)] * 2,
        compiler_params=params(4),
        name="krylov",
    )(plan, base, got)


def combine_kernel(plan, sums, a0, a1, a2, a3, o0, o1, o2, o3):
    total = jnp.sum(sums[...], axis=0, keepdims=True)
    moment = [total[:, i:i + 1] for i in range(6)]

    def inner(a, b, lift):
        value = None
        for i in range(len(a)):
            for j in range(len(b)):
                term = a[i] * b[j] * moment[i + j + lift]
                value = term if value is None else value + term
        return value

    one = jnp.ones((1, 1), F32)
    zero = jnp.zeros((1, 1), F32)
    residual, direction = [one], [one]
    solution = [zero, zero, zero]
    rr = moment[0]
    for step in range(3):
        alpha = rr / inner(direction, direction, 1)
        for i, c in enumerate(direction):
            solution[i] = solution[i] + alpha * c
        if step < 2:
            image = [zero] + direction
            padded = residual + [zero]
            residual = [r - alpha * c for r, c in zip(padded, image)]
            following = inner(residual, residual, 0)
            beta = following / rr
            direction = [r + beta * c for r, c in zip(residual, direction + [zero])]
            rr = following
    solved = []
    for a in (a0, a1, a2, a3):
        v = [a[pl.ds(i * BN, BN), :] for i in range(3)]
        solved.append(solution[0] * v[0] + solution[1] * v[1] + solution[2] * v[2])
    for k, out in enumerate((o0, o1, o2, o3)):
        for b in range(2):
            shift = plan[TSEND + 2 * k + b]
            value = solved[3]
            for j in range(3):
                value = jnp.where(shift == j, solved[j], value)
            out[pl.ds(b * BN, BN), :] = value


def combine(plan, sums, arrays):
    return pl.pallas_call(
        combine_kernel,
        out_shape=(jax.ShapeDtypeStruct((2 * BN, BE), F32),) * 4,
        in_specs=[SM] + [VM] * 5,
        out_specs=(VM,) * 4,
        compiler_params=params(4),
        name="combine",
    )(plan, sums, *arrays)


def place_kernel(plan, a0, a1, a2, a3, out):
    for b in range(2):
        shift = plan[TFROM + b]
        value = chosen(shift, (a0, a1, a2, a3), b * BN, BN)
        out[b] = jnp.where(shift >= 0, value, 0.0)


def place(plan, arrays):
    return pl.pallas_call(
        place_kernel,
        out_shape=jax.ShapeDtypeStruct((2, BN, BE), F32),
        in_specs=[SM] + [VM] * 4,
        out_specs=VM,
        compiler_params=params(4),
        name="place",
    )(plan, *arrays)


def body(tracers, velocity, mixing_rate, column_depth, ocean_mask, clinic_list, tropic_list):
    side = SIDE
    depth = column_depth.reshape(BN, BE)
    every = lambda value: lax.all_to_all(value, EVERY, 0, 0)

    def along_y(value, k):
        return lax.ppermute(value, "y", [(y, (y + k) % side) for y in range(side)])

    def along_z(value, k):
        return lax.ppermute(value, "z", [(z, (z + k) % side) for z in range(side)])

    in_hbm = lambda value: pltpu.with_memory_space_constraint(value, pltpu.HBM)
    tracers = in_hbm(tracers.reshape(4 * CELLS, BE))
    velocity = in_hbm(velocity.reshape(2 * CELLS, BE))
    mixing = in_hbm(mixing_rate.reshape((LEV - 1) * BN, BE))
    depth = in_hbm(depth)
    own = pack(tracers, velocity, depth)
    in_vmem = lambda value: pltpu.with_memory_space_constraint(value, pltpu.VMEM)
    plan = pl.pallas_call(
        functools.partial(make_plan, SIDE, N_GY, N_GX),
        out_shape=jax.ShapeDtypeStruct((PLAN,), jnp.int32),
        in_specs=[SM, SM],
        out_specs=SM,
        scratch_shapes=[pltpu.SMEM(((N_GY + 2) * WRAP,), jnp.int32)],
        compiler_params=params(1),
        name="plan",
    )(clinic_list, tropic_list)
    first_two, inv = stencil(0, (tracers, velocity, mixing))
    first_two, inv = in_vmem(first_two), in_hbm(inv)
    scattered = every(own.reshape(128, PART, BE))
    halo = every(select(plan, scattered)).reshape(ITEM, BE)
    mixed, edge, base, items = solve(0, (plan, first_two, inv, mixing, in_hbm(own), halo, depth), chunk=36)
    got = every(items)
    edge = in_hbm(edge)
    last_two, new = stencil(1, (tracers, velocity, in_vmem(mixed)))
    got, last_two = lax.optimization_barrier((got, last_two))
    vectors, sums = krylov(plan, in_vmem(base), got)
    totals = lax.all_to_all(sums, ("c", "x", "y", "z"), 0, 0)
    _, new = solve(1, (in_vmem(last_two), inv, mixing, edge, in_hbm(new)), chunk=18)
    totals, new = lax.optimization_barrier((totals, new))
    line = [vectors] + [along_y(vectors, k) for k in range(1, side)]
    sends = combine(plan, totals.reshape(128, BE), line)
    arrived = [sends[0]] + [along_z(sends[k], k) for k in range(1, side)]
    height = place(plan, arrived)
    return new.reshape(1, 1, 4, LEV, BN, BE), height[None]


def solution(mesh):
    mesh = Mesh(mesh.devices.reshape(*(SIZES[axis] for axis in "zyxc")), tuple("zyxc"))
    gx, gy = ("z", "y"), ("x", "c")
    return jax.shard_map(
        body,
        mesh=mesh,
        in_specs=(P(gy, gx), P(gy, gx), P(gy, gx), P(gy, gx), P(), P(), P()),
        out_specs=(P(gy, gx), P(gy, gx)),
        check_vma=False,
    )
```
